32 devices in a mesh: dp: 8 (over y, x, core), tensor: 4 (over z).
Axes of the slice: x: 2, y: 2, z: 4, core: 2. Of those that a mesh axis runs over, the one named last changes fastest.
Arguments:
- inputs: bfloat16 [16, 1024, 1024], P('dp', 'tensor'), may hold values from -6 to 6
- cotangent: bfloat16 [16, 1024, 1024], P('dp', 'tensor'), may hold values from -6 to 6
- lengths: int32 [16], P('dp'), may hold values from 1 to 1024, as said below
- block_ids: int32 [16, 1024], P('dp'), may hold values from 0 to 7, never falling along the last dimension, each value on 1 to 256 neighbouring positions
- ln1_gain: float32 [1024], replicated, may hold values from 0.5 to 1.5
- ln1_bias: float32 [1024], replicated, may hold values from -1 to 1
- ln2_gain: float32 [1024], replicated, may hold values from 0.5 to 1.5
- ln2_bias: float32 [1024], replicated, may hold values from -1 to 1
- w_qkv: bfloat16 [1024, 3072], P('dp', 'tensor'), may hold values from -0.1875 to 0.1875
- b_qkv: float32 [3072], P('tensor'), may hold values from -1 to 1
- w_out: bfloat16 [1024, 1024], P('dp', 'tensor'), may hold values from -1 to 1
- b_out: float32 [1024], replicated, may hold values from -1 to 1
- w_up: bfloat16 [1024, 4096], P('dp', 'tensor'), may hold values from -0.1875 to 0.1875
- b_up: float32 [4096], P('tensor'), may hold values from -1 to 1
- w_down: bfloat16 [1024, 4096], P('dp', 'tensor'), may hold values from -0.09375 to 0.09375
- b_down: float32 [1024], replicated, may hold values from -1 to 1
Outputs:
- layer_out: bfloat16 [16, 1024, 1024], P('dp', 'tensor')
- grad_inputs: float32 [16, 1024, 1024], P('dp', 'tensor')
- grad_w_qkv: float32 [1024, 3072], P('dp', 'tensor')
- grad_w_out: float32 [1024, 1024], P('dp', 'tensor')
- grad_w_up: float32 [1024, 4096], P('dp', 'tensor')
- grad_w_down: float32 [1024, 4096], P('dp', 'tensor')
- grad_b_qkv: float32 [3072], P('tensor')
- grad_b_up: float32 [4096], P('tensor')
- grad_ln1_gain: float32 [1024], replicated
- grad_ln1_bias: float32 [1024], replicated
- grad_ln2_gain: float32 [1024], replicated
- grad_ln2_bias: float32 [1024], replicated
- grad_b_out: float32 [1024], replicated
- grad_b_down: float32 [1024], replicated
The draws below stay inside these ranges and needn't reach their ends.
Inputs may be any that keep to these rules, and one draw needn't show every extreme that they name: `lengths`: live tokens of each sequence, at its start; keys from the length on are padding; some sequence has all 1024 live. `block_ids`: along each sequence the block number starts at 0 and never falls; each block spans 1 to 256 consecutive positions and some block spans exactly 256.
All inputs are finite; a program needn't handle non-finite values.
Results may differ from the reference program's by a relative error of at most 0.0098.
Values may be sent and summed in bfloat16 or wider, within the bound.
A program may use at most 256 MiB of HBM per device.

```python
import math
import jax
import jax.numpy as jnp
import numpy as np
from jax import lax

D = 1024
HEADS = 16
HEAD = 64
FF = 4096
ROT = 16
SEQ = 1024
BLOCK = 256
SEQS = 16


def draw_lengths(key, part):
    draw_key, pick_key = jax.random.split(key)
    drawn = jax.random.randint(draw_key, (SEQS,), 1, SEQ + 1)
    chosen = jax.random.randint(pick_key, (), 0, SEQS)
    return jnp.where(jnp.arange(SEQS) == chosen, SEQ, drawn).astype(jnp.int32)


def strengthened(result, own_key, source, target, blocks, factor):
    owner, partner = [(jnp.arange(result.shape[position]) // (result.shape[position] // blocks)).reshape([-1 if axis == position else 1 for axis in range(result.ndim)]) for position in (source, target)]
    chosen = jax.random.permutation(own_key, blocks)[partner]
    strong = (owner == chosen) | (owner == (partner + blocks // 2) % blocks)
    return jnp.where(strong, factor * result, result)


def block_scale(key, shape, shards, smallest, largest):
    def one(axis_at, parts):
        heights = jax.random.uniform(jax.random.fold_in(jax.random.fold_in(key, 6), axis_at), (parts,), jnp.float32, smallest / len(shards), largest / len(shards))
        return jnp.repeat(jnp.exp(heights), shape[axis_at] // parts).reshape((-1,) + (1,) * (len(shape) - axis_at - 1))

    loudness = one(*shards[0])
    for cut in shards[1:]:
        loudness = loudness * one(*cut)
    return loudness


def length_profile(count, total, reach, skew):
    weights = [(1 << 20) // math.isqrt(grade ** skew) + 1 for grade in range(2, count + 1)]
    surplus, given = total - reach - (count - 1), [1] * (count - 1)
    while surplus > 0:
        free = [i for i in range(count - 1) if given[i] < reach]
        mass, remaining = sum([weights[i] for i in free]), surplus
        for i in free:
            addition = min(reach - given[i], max(1, remaining * weights[i] // mass), surplus)
            given[i] = given[i] + addition
            surplus = surplus - addition
    return np.array([reach] + given)


def uneven_parts(key, count, total, most, slope):
    if count == 2:
        one = jax.random.randint(key, (), max(1, total - most), min(most, total - 1) + 1)
        return jnp.stack([one, total - one])
    sizes = jnp.asarray(length_profile(count, total, most, slope), jnp.int32)
    pairs = (count - 1) // 2
    giver, receiver = sizes[1:1 + 2 * pairs:2], sizes[2:2 + 2 * pairs:2]
    margin = jnp.minimum(giver - 1, most - receiver)
    passed = jax.random.randint(jax.random.fold_in(key, 1), (pairs,), 0, 1 << 20) % (margin + 1)
    sizes = sizes.at[1:1 + 2 * pairs:2].set(giver - passed).at[2:2 + 2 * pairs:2].set(receiver + passed)
    return sizes[jax.random.permutation(jax.random.fold_in(key, 2), count)]


def noise(stream_key, shape, deviation, reach, cuts=(), held_as=jnp.bfloat16):
    gain = block_scale(stream_key, shape, cuts, -0.22, 0.18) if cuts else 1.0
    result = jax.random.normal(stream_key, shape, jnp.float32) * deviation * gain
    return jnp.minimum(jnp.maximum(result, -reach), reach).astype(held_as)


def bell_draw_with(own_key, dims, scale, most, shards, heavy, kind=jnp.bfloat16):
    entries = scale * jax.random.normal(own_key, dims, jnp.float32)
    if shards:
        entries = entries * block_scale(own_key, dims, shards, -0.22, 0.18)
    return jnp.clip(strengthened(entries, jax.random.fold_in(own_key, 3), *heavy), -most, most).astype(kind)


def setup_inputs(seed: int = 0) -> dict:
    key_of = jax.random.split(jax.random.key(seed), 17)
    inputs = bell_draw_with(key_of[0], (SEQS, SEQ, D), 1.0, 6.0, ((0, 8), (1, 4)), (0, 2, 8, 2.0))
    cotangent = bell_draw_with(key_of[1], (SEQS, SEQ, D), 1.0, 6.0, ((0, 8), (1, 4)), (0, 2, 8, 2.0))
    lengths = draw_lengths(jax.random.fold_in(key_of[16], 71), 0)
    block_ids = jax.vmap(lambda own: jnp.searchsorted(jnp.cumsum(uneven_parts(own, 2 * SEQ // BLOCK, SEQ, BLOCK, 0)), jnp.arange(SEQ), side="right"))(jax.random.split(key_of[3], SEQS)).reshape((SEQS, SEQ)).astype(jnp.int32)
    ln1_gain = jnp.clip(1.0 + 0.1 * jax.random.normal(key_of[4], (D,), jnp.float32), 0.5, 1.5)
    ln1_bias = noise(key_of[5], (D,), 0.2, 1.0, (), jnp.float32)
    ln2_gain = jnp.clip(1.0 + 0.1 * jax.random.normal(key_of[6], (D,), jnp.float32), 0.5, 1.5)
    ln2_bias = noise(key_of[7], (D,), 0.2, 1.0, (), jnp.float32)
    w_qkv = noise(key_of[8], (D, 3 * D), D ** -0.5, 0.1875, ((0, 8), (1, 4)))
    b_qkv = noise(key_of[9], (3 * D,), 0.2, 1.0, ((0, 4),), jnp.float32)
    w_out = noise(key_of[10], (D, D), (D // 32) ** -0.5, 1.0, ((0, 8), (1, 4)))
    b_out = noise(key_of[11], (D,), 0.2, 1.0, (), jnp.float32)
    w_up = noise(key_of[12], (D, FF), D ** -0.5, 0.1875, ((0, 8), (1, 4)))
    b_up = noise(key_of[13], (FF,), 0.2, 1.0, ((0, 4),), jnp.float32)
    w_down = noise(key_of[14], (D, FF), FF ** -0.5, 0.09375, ((0, 8), (1, 4)))
    b_down = noise(key_of[15], (D,), 0.2, 1.0, (), jnp.float32)
    return {"inputs": inputs, "cotangent": cotangent, "lengths": lengths, "block_ids": block_ids, "ln1_gain": ln1_gain, "ln1_bias": ln1_bias, "ln2_gain": ln2_gain, "ln2_bias": ln2_bias, "w_qkv": w_qkv, "b_qkv": b_qkv, "w_out": w_out, "b_out": b_out, "w_up": w_up, "b_up": b_up, "w_down": w_down, "b_down": b_down}


@jax.custom_vjp
def low(v):
    return lax.optimization_barrier(v.astype(jnp.bfloat16)).astype(jnp.float32)

@jax.custom_vjp
def low_back(v):
    return v

def low_keep(v):
    return (low(v), None)

def low_pass(kept, grad):
    return (grad,)

def back_keep(v):
    return (v, None)

def back_low(kept, grad):
    return (low(grad),)
low.defvjp(low_keep, low_pass)
low_back.defvjp(back_keep, back_low)

def layer_norm(values, ln_gain, ln_bias):
    centre = lax.optimization_barrier(jnp.mean(values, axis=-1, keepdims=True))
    shifted = values - centre
    spread = lax.optimization_barrier(jnp.mean(shifted * shifted, axis=-1, keepdims=True))
    return shifted * lax.rsqrt(spread + 1e-05) * ln_gain + ln_bias

def rope_tables(length, rotary):
    halved = rotary // 2
    frequency = 1.0 / 10000.0 ** (jnp.arange(halved, dtype=jnp.float32) * (2.0 / rotary))
    angles = jnp.arange(length, dtype=jnp.float32)[:, None] * frequency[None, :]
    angles = jnp.concatenate([angles, angles], axis=1)[:, None, :]
    return (jnp.cos(angles), jnp.sin(angles))

def rotate(head_rows, cos_table, sin_table, rotary):
    halved = rotary // 2
    moving = head_rows[..., :rotary]
    turned = jnp.concatenate([-moving[..., halved:], moving[..., :halved]], axis=-1)
    moving = moving * cos_table + turned * sin_table
    return jnp.concatenate([moving, head_rows[..., rotary:]], axis=-1)

def precise(left_side, right_side):
    return jnp.dot(left_side, right_side, precision=lax.Precision.HIGHEST)

def sequence_forward(params, residual, limit, block_row):
    ln1_gain, ln1_bias, ln2_gain, ln2_bias, w_qkv, b_qkv, w_out, b_out, w_up, b_up, w_down, b_down = params
    length = residual.shape[0]
    normed_one = low(layer_norm(residual, ln1_gain, ln1_bias))
    normed_two = low(layer_norm(residual, ln2_gain, ln2_bias))
    projected = low_back(precise(normed_one, w_qkv) + b_qkv).reshape(length, HEADS, 3, HEAD)
    cos_table, sin_table = rope_tables(length, ROT)
    queries = low(rotate(projected[:, :, 0], cos_table, sin_table, ROT))
    key_rows = low(rotate(projected[:, :, 1], cos_table, sin_table, ROT))
    values = low(projected[:, :, 2])
    scores = jnp.einsum('qhe,khe->hqk', queries, key_rows, precision=lax.Precision.HIGHEST)
    scores = low_back(scores * HEAD ** (-0.5))
    positions = jnp.arange(length, dtype=jnp.int32)
    allowed = (block_row[None, :] <= block_row[:, None]) & (positions[None, :] < limit)
    scores = jnp.where(allowed[None], scores, -1e+30)
    soft_low = low(jax.nn.softmax(scores, axis=-1))
    attended = jnp.einsum('hqk,khe->qhe', soft_low, values, precision=lax.Precision.HIGHEST)
    attended = low_back(low(attended.reshape(length, HEADS * HEAD)))
    hidden_pre = low_back(precise(normed_two, w_up) + b_up)
    activated = low(jax.nn.gelu(hidden_pre, approximate=False))
    branches = precise(attended, w_out.T) + b_out + precise(activated, w_down.T) + b_down
    return residual + branches

def reference(inputs, cotangent, lengths, block_ids, ln1_gain, ln1_bias, ln2_gain, ln2_bias, w_qkv, b_qkv, w_out, b_out, w_up, b_up, w_down, b_down):
    params = tuple((element.astype(jnp.float32) for element in (ln1_gain, ln1_bias, ln2_gain, ln2_bias, w_qkv, b_qkv, w_out, b_out, w_up, b_up, w_down, b_down)))
    residual = inputs.astype(jnp.float32)
    checked = jax.checkpoint(sequence_forward)

    def forward(params_all, residual_all):

        def advance(carried, element):
            return (carried, checked(params_all, element[0], element[1], element[2]))
        carried_out, outputs = lax.scan(advance, None, (residual_all, lengths, block_ids))
        return outputs
    outputs, pullback = jax.vjp(forward, params, residual)
    grad_params, grad_inputs = pullback(cotangent.astype(jnp.float32))
    return (outputs.astype(jnp.bfloat16), grad_inputs, grad_params[4], grad_params[6], grad_params[8], grad_params[10], grad_params[5], grad_params[9], grad_params[0], grad_params[1], grad_params[2], grad_params[3], grad_params[7], grad_params[11])
```

```python
import jax
import jax.numpy as jnp
from jax import lax
from jax.sharding import PartitionSpec as P

HEAD = 64
ROT = 16
BLOCK = 256
F32 = jnp.float32
BF16 = jnp.bfloat16


def rope_tables(length):
    halved = ROT // 2
    frequency = 1.0 / 10000.0 ** (jnp.arange(halved, dtype=F32) * (2.0 / ROT))
    angles = jnp.arange(length, dtype=F32)[:, None] * frequency[None, :]
    angles = jnp.concatenate([angles, angles], axis=1)[:, None, :]
    return jnp.cos(angles), jnp.sin(angles)


def rotate(rows, cos_table, sin_table):
    halved = ROT // 2
    moving = rows[..., :ROT]
    turned = jnp.concatenate([-moving[..., halved:], moving[..., :halved]], axis=-1)
    moving = moving * cos_table + turned * sin_table
    return jnp.concatenate([moving, rows[..., ROT:]], axis=-1)


def visible(ids, limit, first, rows, key_end):
    own = ids[first : first + rows]
    pos = jnp.arange(key_end, dtype=jnp.int32)
    allowed = (ids[None, :key_end] <= own[:, None]) & (pos[None, :] < limit)
    return allowed[None]


def gelu_exact(v):
    return jax.nn.gelu(v, approximate=False)


def xor_pairs(n, mask):
    return [(i, i ^ mask) for i in range(n)]


def gather_line(block, axis, n):
    me = lax.axis_index(axis)
    right, left = block, block
    rights, lefts = [], []
    for s in range(1, n):
        right = lax.ppermute(right, axis, [(i, i + 1) for i in range(s - 1, n - 1)])
        left = lax.ppermute(left, axis, [(i, i - 1) for i in range(1, n - s + 1)])
        rights.append(right)
        lefts.append(left)
    line = jnp.concatenate(rights[::-1] + [block] + lefts, axis=0)
    rows = block.shape[0]
    return lax.dynamic_slice_in_dim(line, (n - 1 - me) * rows, n * rows, axis=0)


def scatter_line(partial, axis, n):
    me = lax.axis_index(axis)
    rows = partial.shape[0] // n

    def piece(index):
        index = jnp.clip(index, 0, n - 1)
        return lax.dynamic_slice_in_dim(partial, index * rows, rows, axis=0)

    from_left, from_right = None, None
    for s in range(1, n):
        to_right = piece(n - s + me)
        to_left = piece(s + me - n)
        if from_left is not None:
            to_right = to_right + from_left.astype(F32)
            to_left = to_left + from_right.astype(F32)
        from_left = lax.ppermute(to_right.astype(BF16), axis, [(i, i + 1) for i in range(0, s)])
        from_right = lax.ppermute(
            to_left.astype(BF16), axis, [(i, i - 1) for i in range(n - s, n)]
        )
    return piece(me) + from_left.astype(F32) + from_right.astype(F32)


def bits_of(n):
    return [1 << k for k in range(n.bit_length() - 1)]


def gather_cube(shard, axis, n, order):
    me = lax.axis_index(axis)
    pieces = {0: shard}
    for bit in order:
        new = {}
        held = sorted(pieces)
        moved = lax.ppermute(
            jnp.concatenate([pieces[m] for m in held], axis=0), axis, xor_pairs(n, bit)
        )
        rows = shard.shape[0]
        for k, m in enumerate(held):
            new[m] = pieces[m]
            new[m ^ bit] = moved[k * rows : (k + 1) * rows]
        pieces = new
    rows = shard.shape[0]
    full = jnp.zeros((n * rows,) + shard.shape[1:], shard.dtype)
    for m in range(n):
        full = lax.dynamic_update_slice_in_dim(full, pieces[m], (me ^ m) * rows, axis=0)
    return full


def scatter_cube(grad, axis, n, order):
    me = lax.axis_index(axis)
    nbits = n.bit_length() - 1
    rows = grad.shape[0] // n
    part = grad.reshape((2,) * nbits + (rows, grad.shape[1]))
    for bit in order:
        dim = nbits - bit.bit_length()
        mine = (me // bit) % 2
        keep = lax.dynamic_slice_in_dim(part, mine, 1, axis=dim)
        send = lax.dynamic_slice_in_dim(part, 1 - mine, 1, axis=dim)
        got = lax.ppermute(send.astype(BF16), axis, xor_pairs(n, bit))
        part = keep + got.astype(F32)
    return part.reshape(rows, grad.shape[1])


def all_sum(vec, axis, n):
    for bit in bits_of(n):
        vec = vec + lax.ppermute(vec, axis, xor_pairs(n, bit))
    return vec


def make(n_dp, n_tp):
    def on_device(
        inputs,
        cotangent,
        lengths,
        block_ids,
        ln1_gain,
        ln1_bias,
        ln2_gain,
        ln2_bias,
        w_qkv,
        b_qkv,
        w_out,
        b_out,
        w_up,
        b_up,
        w_down,
        b_down,
    ):
        seqs, own_rows, width = inputs.shape
        length = block_ids.shape[1]
        tile = min(512, length)
        heads = w_qkv.shape[1] // (3 * HEAD)
        scaling = HEAD ** (-0.5)
        cos_table, sin_table = rope_tables(length)
        starts = list(range(0, length, tile))
        ends = [min(length, first + tile + BLOCK) for first in starts]
        bits = bits_of(n_dp)
        asc = bits[1:] + bits[:1]
        desc = bits[1:][::-1] + bits[:1]

        x_all = [gather_line(inputs[i], "tensor", n_tp) for i in range(seqs)]
        qkv_w = gather_cube(w_qkv, "dp", n_dp, asc)
        up_w = gather_cube(w_up, "dp", n_dp, desc)
        down_w = gather_cube(w_down, "dp", n_dp, asc)
        out_w = gather_cube(w_out, "dp", n_dp, desc)
        c_all = [gather_line(cotangent[i], "tensor", n_tp) for i in range(seqs)]

        def dot(a, b, dims):
            return lax.dot_general(a, b, (dims, ((), ())), preferred_element_type=F32)

        def norm_stats(v):
            centre = jnp.mean(v, axis=-1, keepdims=True)
            shifted = v - centre
            spread = jnp.mean(shifted * shifted, axis=-1, keepdims=True)
            return centre, lax.rsqrt(spread + 1e-05)

        kept = []
        out_rows = []
        for i in range(seqs):
            res = x_all[i].astype(F32)
            centre, inv = norm_stats(res)
            xhat = (res - centre) * inv
            one = (xhat * ln1_gain + ln1_bias).astype(BF16)
            two = (xhat * ln2_gain + ln2_bias).astype(BF16)
            projected = (dot(one, qkv_w, ((1,), (0,))) + b_qkv).reshape(length, heads, 3, HEAD)
            queries = rotate(projected[:, :, 0], cos_table, sin_table).astype(BF16)
            keys = rotate(projected[:, :, 1], cos_table, sin_table).astype(BF16)
            values = projected[:, :, 2].astype(BF16)
            q_hd = (queries * BF16(scaling)).transpose(1, 0, 2)
            k_hd = keys.transpose(1, 0, 2)
            v_hd = values.transpose(1, 0, 2)
            logs, mixed = [], []
            for first, end in zip(starts, ends):
                allowed = visible(block_ids[i], lengths[i], first, tile, end)
                scores = jnp.einsum(
                    "hqe,hke->hqk",
                    q_hd[:, first : first + tile],
                    k_hd[:, :end],
                    preferred_element_type=F32,
                )
                scores = jnp.where(allowed, scores, -1e30)
                peak = jnp.max(scores, axis=-1)
                powered = jnp.exp(scores - peak[..., None])
                total = jnp.sum(powered, axis=-1)
                soft_low = (powered / total[..., None]).astype(BF16)
                logs.append(peak + jnp.log(total))
                mixed.append(
                    jnp.einsum("hqk,hke->hqe", soft_low, v_hd[:, :end], preferred_element_type=F32)
                )
            attended = (
                jnp.concatenate(mixed, axis=1)
                .transpose(1, 0, 2)
                .reshape(length, heads * HEAD)
                .astype(BF16)
            )
            hidden = dot(two, up_w, ((1,), (0,))) + b_up
            activated = gelu_exact(hidden).astype(BF16)
            partial = dot(attended, out_w, ((1,), (1,))) + dot(activated, down_w, ((1,), (1,)))
            reduced = scatter_line(partial, "tensor", n_tp)
            out_rows.append((inputs[i].astype(F32) + reduced + b_out + b_down).astype(BF16))
            kept.append((one, two, q_hd, k_hd, v_hd, logs, attended, hidden, activated))

        g_qkv = g_out = g_up = g_down = None
        s_qkv = s_up = s_g1 = s_b1 = s_g2 = s_b2 = s_slope = 0.0
        grad_rows = []

        def add(total, new):
            return new if total is None else total + new

        for i in range(seqs):
            one, two, q_hd, k_hd, v_hd, logs, attended, hidden, activated = kept[i]
            slope = c_all[i]
            g_out = add(g_out, dot(slope, attended, ((0,), (0,))))
            g_down = add(g_down, dot(slope, activated, ((0,), (0,))))
            grad_att = dot(slope, out_w, ((1,), (0,))).astype(BF16)
            grad_att = grad_att.reshape(length, heads, HEAD).transpose(1, 0, 2)
            grad_act = dot(slope, down_w, ((1,), (0,)))
            cdf = 0.5 * (1.0 + lax.erf(hidden * (0.5**0.5)))
            pdf = jnp.exp(-0.5 * hidden * hidden) * 0.3989422804014327
            grad_hidden = (grad_act * (cdf + hidden * pdf)).astype(BF16)
            g_up = add(g_up, dot(two, grad_hidden, ((0,), (0,))))
            s_up = s_up + jnp.sum(grad_hidden.astype(F32), axis=0)
            grad_two = dot(grad_hidden, up_w, ((1,), (1,)))
            gk = jnp.zeros((heads, length, HEAD), F32)
            gv = jnp.zeros((heads, length, HEAD), F32)
            gq = []
            for n, first in enumerate(starts):
                end = ends[n]
                q_t = q_hd[:, first : first + tile]
                g_t = grad_att[:, first : first + tile]
                k_t = k_hd[:, :end]
                allowed = visible(block_ids[i], lengths[i], first, tile, end)
                scores = jnp.einsum("hqe,hke->hqk", q_t, k_t, preferred_element_type=F32)
                scores = jnp.where(allowed, scores, -1e30)
                soft = jnp.exp(scores - logs[n][..., None])
                gv = gv.at[:, :end].add(
                    jnp.einsum("hqk,hqe->hke", soft.astype(BF16), g_t, preferred_element_type=F32)
                )
                grad_soft = jnp.einsum(
                    "hqe,hke->hqk", g_t, v_hd[:, :end], preferred_element_type=F32
                )
                centred = jnp.sum(soft * grad_soft, axis=-1)
                gs = (soft * (grad_soft - centred[..., None])).astype(BF16)
                gq.append(
                    jnp.einsum("hqk,hke->hqe", gs, k_t, preferred_element_type=F32) * scaling
                )
                gk = gk.at[:, :end].add(
                    jnp.einsum("hqk,hqe->hke", gs, q_t, preferred_element_type=F32)
                )
            gq = jnp.concatenate(gq, axis=1).transpose(1, 0, 2)
            gk = gk.transpose(1, 0, 2)
            gv = gv.transpose(1, 0, 2)
            gp = jnp.stack(
                [rotate(gq, cos_table, -sin_table), rotate(gk, cos_table, -sin_table), gv], axis=2
            )
            gp = gp.reshape(length, 3 * heads * HEAD).astype(BF16)
            g_qkv = add(g_qkv, dot(one, gp, ((0,), (0,))))
            s_qkv = s_qkv + jnp.sum(gp.astype(F32), axis=0)
            grad_one = dot(gp, qkv_w, ((1,), (1,)))
            res = x_all[i].astype(F32)
            centre, inv = norm_stats(res)
            xhat = (res - centre) * inv
            s_g1 = s_g1 + jnp.sum(grad_one * xhat, axis=0)
            s_b1 = s_b1 + jnp.sum(grad_one, axis=0)
            s_g2 = s_g2 + jnp.sum(grad_two * xhat, axis=0)
            s_b2 = s_b2 + jnp.sum(grad_two, axis=0)
            both = grad_one * ln1_gain + grad_two * ln2_gain
            e = scatter_line(both, "tensor", n_tp)
            mine = inputs[i].astype(F32)
            centre, inv = norm_stats(mine)
            xh = (mine - centre) * inv
            slope_own = cotangent[i].astype(F32)
            back = (
                e
                - jnp.mean(e, axis=-1, keepdims=True)
                - xh * jnp.mean(e * xh, axis=-1, keepdims=True)
            ) * inv
            grad_rows.append(slope_own + back)
            s_slope = s_slope + jnp.sum(slope_own, axis=0)
        r_asc = bits[:1] + bits[1:]
        r_desc = bits[:1] + bits[1:][::-1]
        o_down = scatter_cube(g_down, "dp", n_dp, r_asc)
        o_out = scatter_cube(g_out, "dp", n_dp, r_desc)
        o_up = scatter_cube(g_up, "dp", n_dp, r_desc)
        o_qkv = scatter_cube(g_qkv, "dp", n_dp, r_asc)
        vec = jnp.concatenate([s_g1, s_b1, s_g2, s_b2, s_slope, s_qkv, s_up])
        vec = all_sum(vec, "dp", n_dp)
        shared = all_sum(vec[: 5 * width], "tensor", n_tp).reshape(5, width)
        q_cols = w_qkv.shape[1]
        return (
            jnp.stack(out_rows),
            jnp.stack(grad_rows),
            o_qkv,
            o_out,
            o_up,
            o_down,
            vec[5 * width : 5 * width + q_cols],
            vec[5 * width + q_cols :],
            shared[0],
            shared[1],
            shared[2],
            shared[3],
            shared[4],
            shared[4],
        )

    return on_device


def solution(mesh):
    in_specs = (
        P("dp", "tensor", None),
        P("dp", "tensor", None),
        P("dp"),
        P("dp", None),
        P(),
        P(),
        P(),
        P(),
        P("dp", "tensor"),
        P("tensor"),
        P("dp", "tensor"),
        P(),
        P("dp", "tensor"),
        P("tensor"),
        P("dp", "tensor"),
        P(),
    )
    out_specs = (
        P("dp", "tensor", None),
        P("dp", "tensor", None),
        P("dp", "tensor"),
        P("dp", "tensor"),
        P("dp", "tensor"),
        P("dp", "tensor"),
        P("tensor"),
        P("tensor"),
        P(),
        P(),
        P(),
        P(),
        P(),
        P(),
    )
    return jax.shard_map(
        make(mesh.shape["dp"], mesh.shape["tensor"]),
        mesh=mesh,
        in_specs=in_specs,
        out_specs=out_specs,
        check_vma=False,
    )
```

```python
import jax
import jax.numpy as jnp
import numpy as np
from jax import lax
from jax.experimental import pallas as pl
from jax.experimental.pallas import tpu as pltpu
from jax.sharding import PartitionSpec as P

HEAD = 64
ROT = 16
BLOCK = 256
F32 = jnp.float32
BF16 = jnp.bfloat16
MIB = 1 << 20
CHUNK = 256


def mm(a, b, ca, cb):
    return lax.dot_general(a, b, (((ca,), (cb,)), ((), ())), preferred_element_type=F32)


def norm_parts(v):
    centre = jnp.mean(v, axis=-1, keepdims=True)
    shifted = v - centre
    spread = jnp.mean(shifted * shifted, axis=-1, keepdims=True)
    inv = lax.rsqrt(spread + 1e-05)
    return shifted * inv, inv


def turn_back_and_forth(rows, cos_t, up_t, dn_t):
    width = rows.shape[1]
    reps = width // cos_t.shape[1]
    tile = lambda t: jnp.concatenate([t] * reps, axis=1) if reps > 1 else t
    ahead = pltpu.roll(rows, width - ROT // 2, 1)
    behind = pltpu.roll(rows, ROT // 2, 1)
    return rows * tile(cos_t) + ahead * tile(up_t) + behind * tile(dn_t)


def rope_lanes(length):
    halved = ROT // 2
    frequency = 1.0 / 10000.0 ** (np.arange(halved, dtype=np.float32) * np.float32(2.0 / ROT))
    angles = np.arange(length, dtype=np.float32)[:, None] * frequency[None, :].astype(np.float32)
    cos_t, sin_t = np.cos(angles), np.sin(angles)
    flat = np.zeros((length, HEAD - ROT), np.float32)
    zero = np.zeros_like(sin_t)
    one_head = np.concatenate([cos_t, cos_t, flat + 1.0], axis=1)
    ahead = np.concatenate([-sin_t, zero, flat], axis=1)
    behind = np.concatenate([zero, sin_t, flat], axis=1)
    return np.stack([np.concatenate([t, t], axis=1) for t in (one_head, ahead, behind)]).astype(np.float32)


def tiles_of(length):
    out = []
    for first in range(0, length, CHUNK):
        out.append((first, min(length, first + CHUNK + BLOCK)))
    return out


def halves(pair_rows, which):
    blank = jnp.zeros_like(pair_rows)
    return jnp.concatenate([pair_rows, blank] if which == 0 else [blank, pair_rows], axis=0)


def lane_half(rows, which):
    lane = lax.broadcasted_iota(jnp.int32, rows.shape, 1)
    keep = lane < HEAD if which == 0 else lane >= HEAD
    return jnp.where(keep, rows, jnp.zeros_like(rows))


def sds(shape, dtype):
    return jax.ShapeDtypeStruct(shape, dtype)


VM = pltpu.VMEM
ANY = pl.ANY
MESH = pl.DeviceIdType.MESH
DMA = pltpu.SemaphoreType.DMA
TP, DP = "tensor", "dp"
LOAD, STORE = object(), object()


class Refs:
    def __init__(self, refs, loads, stores):
        self.refs, self.loads, self.stores = refs, loads, stores

    def __getattr__(self, name):
        refs = self.__dict__["refs"]
        return refs.get(name + "@", refs.get(name))

    def _copies(self, name, incoming, part=None):
        far, near, sem = self.refs[name], self.refs[name + "@"], self.refs[name + "#"]
        cuts = self.loads[name] if incoming else [...]
        for n, cut in enumerate(cuts):
            if part is not None and n != part:
                continue
            a, b = far.at[cut], near.at[cut]
            yield pltpu.make_async_copy(a if incoming else b, b if incoming else a, sem.at[n])

    def load(self, *names):
        for name in names:
            for copy in self._copies(name, True):
                copy.start()

    def ready(self, *names, part=None):
        for name in names:
            for copy in self._copies(name, True, part):
                copy.wait()

    def flush(self, *names):
        for name in names:
            for copy in self._copies(name, False):
                copy.start()

    def flush_rows(self, rows, *names):
        for name in names:
            far, near, sem = self.refs[name], self.refs[name + "@"], self.refs[name + "#"]
            pltpu.make_async_copy(near.at[rows, :], far.at[rows, :], sem.at[0]).start()

    def drain(self):
        for name in self.stores:
            for copy in self._copies(name, False):
                copy.wait()


def call(name, body, ins, outs, scratch, cid, limit=58):
    arrays, in_specs, in_names, out_shapes, out_specs = [], [], [], [], []
    loads, stores, extra = {}, [], {}
    for key, item in ins.items():
        array, kind = item[0], item[1]
        arrays.append(array)
        in_names.append(key)
        if kind is LOAD:
            loads[key] = item[2] if len(item) > 2 else [...]
            extra[key + "@"] = VM(array.shape, array.dtype)
            extra[key + "#"] = DMA((len(loads[key]),))
            kind = ANY
        in_specs.append(pl.BlockSpec(memory_space=kind))
    for key, (shape, kind) in outs.items():
        out_shapes.append(shape)
        if kind is STORE:
            stores.append(key)
            extra[key + "@"] = VM(shape.shape, shape.dtype)
            extra[key + "#"] = DMA((1,))
            kind = ANY
        out_specs.append(pl.BlockSpec(memory_space=kind))
    scratch = {**extra, **scratch}
    names = in_names + list(outs) + list(scratch)

    def kernel(*refs):
        body(Refs(dict(zip(names, refs, strict=True)), loads, stores))

    res = pl.pallas_call(
        kernel,
        name=name,
        out_shape=out_shapes,
        in_specs=in_specs,
        out_specs=out_specs,
        scratch_shapes=list(scratch.values()),
        compiler_params=pltpu.CompilerParams(
            vmem_limit_bytes=limit * MIB, collective_id=cid, has_side_effects=True
        ),
    )(*arrays)
    return dict(zip(outs, res))


def greet(n, others=()):
    barrier = pltpu.get_barrier_semaphore()
    me = lax.axis_index(TP)

    def signal(peer):
        pl.semaphore_signal(barrier, inc=1, device_id=peer, device_id_type=MESH)

    @pl.when(me > 0)
    def _():
        signal({TP: lax.rem(me + n - 1, n)})

    @pl.when(me < n - 1)
    def _():
        signal({TP: lax.rem(me + 1, n)})

    for peer in others:
        signal(peer)
    inside = (me > 0) & (me < n - 1)

    @pl.when(inside)
    def _():
        pl.semaphore_wait(barrier, len(others) + 2)

    @pl.when(jnp.logical_not(inside))
    def _():
        pl.semaphore_wait(barrier, len(others) + 1)


def remote(src, dst, send, recv, peer):
    return pltpu.make_async_remote_copy(
        src_ref=src, dst_ref=dst, send_sem=send, recv_sem=recv, device_id=peer, device_id_type=MESH
    )


class Gather:
    def __init__(self, own, full, sems, local, n):
        self.own, self.full, self.sems, self.local, self.n = own, full, sems, local, n
        self.me = lax.axis_index(TP)
        self.rows = own.shape[0]

    @staticmethod
    def scratch(tag, n):
        return {
            tag + "_sems": DMA((4, n - 1)),
            tag + "_local": DMA,
        }

    def block(self, index):
        return self.full.at[pl.ds(pl.multiple_of(index * self.rows, self.rows), self.rows), :]

    def copy(self, side, s):
        index = self.me - s + 1 if side == 0 else self.me + s - 1
        peer = lax.rem(self.me + (1 if side == 0 else self.n - 1), self.n)
        place = self.block(index)
        return remote(
            self.own if s == 1 else place,
            place,
            self.sems.at[2 * side, s - 1],
            self.sems.at[2 * side + 1, s - 1],
            {TP: peer},
        )

    def sends(self, side, s):
        if side == 0:
            return (self.me >= s - 1) & (self.me < self.n - 1)
        return (self.me <= self.n - s) & (self.me > 0)

    def receives(self, side, s):
        return self.me >= s if side == 0 else self.me <= self.n - 1 - s

    def step(self, s):
        if s == 1:
            pltpu.make_async_copy(self.own, self.block(self.me), self.local).start()
        for side in range(2):
            if s > 1:

                @pl.when(self.receives(side, s - 1))
                def _():
                    self.copy(side, s - 1).wait_recv()

            if s < self.n:

                @pl.when(self.sends(side, s))
                def _():
                    self.copy(side, s).start()

        if s == self.n:
            pltpu.make_async_copy(self.own, self.block(self.me), self.local).wait()
            for side in range(2):
                for k in range(1, self.n):

                    @pl.when(self.sends(side, k))
                    def _():
                        self.copy(side, k).wait_send()


class Scatter:
    def __init__(self, far, part, inbox, sems, n):
        self.far, self.part, self.inbox, self.sems, self.n = far, part, inbox, sems, n
        self.me = lax.axis_index(TP)
        self.rows = part.shape[0] // n

    @staticmethod
    def scratch(tag, n, rows, width):
        return {
            tag + "_inbox": VM((2, n - 1, rows, width), BF16),
            tag + "_sems": DMA((4, n - 1)),
        }

    def mine(self, index):
        return self.far.at[pl.ds(pl.multiple_of(index * self.rows, self.rows), self.rows), :]

    def target(self, side, s):
        return self.n - s + self.me if side == 0 else s + self.me - self.n

    def first(self, side):
        return self.me == 0 if side == 0 else self.me == self.n - 1

    def sends(self, side, s):
        if side == 0:
            return (self.me <= s - 1) & (self.me < self.n - 1)
        return (self.me >= self.n - s) & (self.me > 0)

    def copy(self, side, s, start):
        peer = lax.rem(self.me + (1 if side == 0 else self.n - 1), self.n)
        src = self.mine(self.target(side, s)) if start else self.inbox.at[side, max(s - 2, 0)]
        return remote(
            src,
            self.inbox.at[side, s - 1],
            self.sems.at[2 * side, s - 1],
            self.sems.at[2 * side + 1, s - 1],
            {TP: peer},
        )

    def step(self, s):
        for side in range(2):

            @pl.when(self.first(side))
            def _():
                self.copy(side, s, True).start()

            if s > 1:

                @pl.when(self.sends(side, s) & jnp.logical_not(self.first(side)))
                def _():
                    self.copy(side, s - 1, False).wait_recv()
                    index = self.target(side, s)
                    rows = pl.ds(pl.multiple_of(index * self.rows, self.rows), self.rows)
                    self.inbox[side, s - 2] = (
                        self.inbox[side, s - 2].astype(F32) + self.part[rows, :].astype(F32)
                    ).astype(BF16)
                    self.copy(side, s, False).start()

    def finish(self, total):
        n = self.n
        rows = pl.ds(pl.multiple_of(self.me * self.rows, self.rows), self.rows)
        total[...] = self.part[rows, :].astype(F32)
        for side in range(2):

            @pl.when(jnp.logical_not(self.first(side)))
            def _():
                self.copy(side, n - 1, False).wait_recv()
                total[...] += self.inbox[side, n - 2].astype(F32)

            for s in range(1, n):

                @pl.when(self.sends(side, s) & self.first(side))
                def _():
                    self.copy(side, s, True).wait_send()

                if s > 1:

                    @pl.when(self.sends(side, s) & jnp.logical_not(self.first(side)))
                    def _():
                        self.copy(side, s, False).wait_send()


def bits_of(n):
    return [1 << k for k in range(n.bit_length() - 1)]


def span(bits):
    masks = [0]
    for bit in bits:
        masks = masks + [m ^ bit for m in masks]
    return masks


def cube_peers(n):
    me = lax.axis_index(DP)
    return [{DP: me ^ bit} for bit in bits_of(n)]


class CubeGather:
    def __init__(self, own, full, sems, local, n):
        self.own, self.full, self.sems, self.local, self.n = own, full, sems, local, n
        self.me = lax.axis_index(DP)
        high = bits_of(n)[1:]
        self.orders = [high, high[::-1]]
        cols = own.shape[1]
        self.cols = [slice(0, cols // 2), slice(cols // 2, cols)]

    @staticmethod
    def scratch(tag, n):
        return {
            tag + "_sems": DMA((2, 2, n)),
            tag + "_local": DMA,
        }

    def copy(self, half, mask, bit):
        cols = self.cols[half]
        place = self.full.at[self.me ^ mask, :, cols]
        src = self.own.at[:, cols] if mask == 0 else place
        slot = mask ^ bit
        return remote(
            src, place, self.sems.at[half, 0, slot], self.sems.at[half, 1, slot], {DP: self.me ^ bit}
        )

    def send(self, half, stage):
        bit = self.orders[half][stage]
        for mask in span(self.orders[half][:stage]):
            self.copy(half, mask, bit).start()

    def arrive(self, half, stage):
        bit = self.orders[half][stage]
        for mask in span(self.orders[half][:stage]):
            self.copy(half, mask, bit).wait_recv()

    def to_sibling(self, half, masks):
        for mask in masks:
            self.copy(half, mask, 1).start()

    def start(self):
        pltpu.make_async_copy(self.own, self.full.at[self.me], self.local).start()
        for half in range(2):
            if self.orders[half]:
                self.send(half, 0)
        for half in range(2):
            self.to_sibling(half, [0])

    def step(self, stage):
        for half in range(2):
            order = self.orders[half]
            self.arrive(half, stage)
            if stage + 1 < len(order):
                self.send(half, stage + 1)
            self.to_sibling(half, [m ^ order[stage] for m in span(order[:stage])])

    def stages(self):
        return len(self.orders[0])

    def finish(self):
        pltpu.make_async_copy(self.own, self.full.at[self.me], self.local).wait()
        for half in range(2):
            order = self.orders[half]
            for stage, bit in enumerate(order):
                for mask in span(order[:stage]):
                    self.copy(half, mask, bit).wait_send()
            for mask in span(order):
                c = self.copy(half, mask, 1)
                c.wait_send()
                c.wait_recv()


class CubeScatter:
    def __init__(self, part, acc, inbox, sibling, sems, sib_sems, n):
        self.part, self.acc, self.inbox, self.sibling = part, acc, inbox, sibling
        self.sems, self.sib_sems, self.n = sems, sib_sems, n
        self.me = lax.axis_index(DP)
        self.q = self.me // 2
        self.core = self.me % 2
        high = [b // 2 for b in bits_of(n)[1:]]
        self.orders = [high, high[::-1]]
        cols = part.shape[2]
        self.cols = [slice(0, cols // 2), slice(cols // 2, cols)]

    @staticmethod
    def scratch(tag, n, rows, cols):
        return {
            tag + "_acc": VM((n // 2, rows, cols), BF16),
            tag + "_inbox": VM((max(n // 2, 1), rows, cols), BF16),
            tag + "_sibling": VM((n // 2, rows, cols), BF16),
            tag + "_sems": DMA((2, 2, n)),
            tag + "_sib_sems": DMA((3, n)),
        }

    def sib_copy(self, mask):
        q = self.q ^ mask
        return remote(
            self.part.at[2 * q + 1 - self.core],
            self.sibling.at[q],
            self.sib_sems.at[0, mask],
            self.sib_sems.at[1, mask],
            {DP: self.me ^ 1},
        )

    def order_of_masks(self):
        masks = span(self.orders[0])
        return sorted(masks, key=lambda m: -bin(m).count("1"))

    def own_copy(self, mask):
        q = self.q ^ mask
        return pltpu.make_async_copy(
            self.part.at[2 * q + self.core], self.acc.at[q], self.sib_sems.at[2, mask]
        )

    def start(self):
        for mask in self.order_of_masks():
            self.sib_copy(mask).start()
            self.own_copy(mask).start()

    def join_sibling(self, mask):
        self.own_copy(mask).wait()
        self.sib_copy(mask).wait_recv()
        q = self.q ^ mask
        self.acc[q] = (self.acc[q].astype(F32) + self.sibling[q].astype(F32)).astype(BF16)

    def copy(self, half, stage, mask):
        bit = self.orders[half][stage]
        cols = self.cols[half]
        return remote(
            self.acc.at[self.q ^ mask, :, cols],
            self.inbox.at[mask, :, cols],
            self.sems.at[half, 0, mask],
            self.sems.at[half, 1, mask],
            {DP: self.me ^ (2 * bit)},
        )

    def moved(self, half, stage):
        order = self.orders[half]
        return [m ^ order[stage] for m in span(order[stage + 1 :])]

    def send(self, half, stage, mask):
        self.copy(half, stage, mask).start()

    def first_sends(self):
        for mask in self.order_of_masks():
            self.join_sibling(mask)
            for half in range(2):
                if self.orders[half] and mask in self.moved(half, 0):
                    self.send(half, 0, mask)

    def add(self, half, stage):
        order = self.orders[half]
        bit = order[stage]
        cols = self.cols[half]
        for mask in self.moved(half, stage):
            self.copy(half, stage, mask).wait_recv()
            q = self.q ^ mask ^ bit
            self.acc[q, :, cols] = (
                self.acc[q, :, cols].astype(F32) + self.inbox[mask, :, cols].astype(F32)
            ).astype(BF16)

    def step(self, stage):
        for half in range(2):
            self.add(half, stage)
            if stage + 1 < len(self.orders[half]):
                for mask in self.moved(half, stage + 1):
                    self.send(half, stage + 1, mask)

    def stages(self):
        return len(self.orders[0])

    def finish(self):
        for mask in self.order_of_masks():
            self.sib_copy(mask).wait_send()
        for half in range(2):
            for stage in range(len(self.orders[half])):
                for mask in self.moved(half, stage):
                    self.copy(half, stage, mask).wait_send()


class AllSum:
    def __init__(self, value, inbox, sems, hops):
        self.value, self.inbox, self.sems, self.hops = value, inbox, sems, hops

    @staticmethod
    def hops_of(n_dp, n_tp):
        return [(DP, b) for b in bits_of(n_dp)] + [(TP, b) for b in bits_of(n_tp)]

    @staticmethod
    def scratch(tag, hops, shape):
        return {
            tag + "_value": VM((hops + 1,) + shape, F32),
            tag + "_inbox": VM((hops,) + shape, F32),
            tag + "_sems": DMA((2, hops)),
        }

    def copy(self, k):
        axis, bit = self.hops[k]
        return remote(
            self.value.at[k],
            self.inbox.at[k],
            self.sems.at[0, k],
            self.sems.at[1, k],
            {axis: lax.axis_index(axis) ^ bit},
        )

    def start(self, k):
        self.copy(k).start()

    def step(self, k):
        self.copy(k).wait_recv()
        self.value[k + 1] = self.value[k] + self.inbox[k]
        if k + 1 < len(self.hops):
            self.start(k + 1)

    def finish(self):
        for k in range(len(self.hops)):
            self.copy(k).wait_send()


def spread_ids(m, length):
    for first in range(0, length, 128):
        row = jnp.broadcast_to(m.key_row[0:1, first : first + 128], (128, 128))
        m.key_ids[first : first + 128, :] = row.T


def seen_by(m, end, cols):
    keys = jnp.concatenate([m.key_ids[0:end, :]] * (CHUNK // 128), axis=1)
    return keys <= m.query_row[0:1, cols]


def forward_body(m, tick):
    length, width = m.x.shape
    wide = m.att.shape[1]
    hidden = m.act.shape[1]
    qkv = 3 * wide
    pairs = wide // (2 * HEAD)
    chunks = length // CHUNK
    scaling = HEAD ** (-0.5)
    half = hidden // 2
    tick(0)
    m.load("x", "w", "tabs")
    spread_ids(m, length)
    m.ready("x", "tabs")
    m.ready("w", part=0)

    @pl.loop(0, chunks)
    def _(r):
        rows = pl.ds(pl.multiple_of(r * CHUNK, CHUNK), CHUNK)
        xhat, _ = norm_parts(m.x[rows, :].astype(F32))
        one = (xhat * m.vec[0:1, :] + m.vec[1:2, :]).astype(BF16)
        m.one[rows, :] = one
        m.two[rows, :] = (xhat * m.vec[2:3, :] + m.vec[3:4, :]).astype(BF16)
        proj = mm(one, m.w[:, 0:qkv], 1, 0) + m.bias[0:1, 0:qkv]
        tabs = (m.tabs[0, rows, :], m.tabs[1, rows, :], m.tabs[2, rows, :])
        q = turn_back_and_forth(proj[:, 0:wide], *tabs).astype(BF16) * BF16(scaling)
        k = turn_back_and_forth(proj[:, wide : 2 * wide], *tabs).astype(BF16)
        v = proj[:, 2 * wide : qkv].astype(BF16)
        m.q[rows, :] = q
        m.k[rows, :] = k
        m.v[rows, :] = v
        m.qt[:, rows] = q.T
        m.kt[:, rows] = k.T
        m.vt[:, rows] = v.T

    m.flush("one", "two", "q", "k", "v", "qt", "kt")

    @pl.loop(0, pairs)
    def _(p):
        lanes = pl.ds(pl.multiple_of(p * 2 * HEAD, 2 * HEAD), 2 * HEAD)
        for first, end in tiles_of(length):
            cols = slice(first, first + CHUNK)
            outs = []
            for h in range(2):
                head = pl.ds(pl.multiple_of(p * 2 * HEAD + h * HEAD, HEAD), HEAD)
                s = mm(m.k[0:end, lanes], halves(m.qt[head, cols], h), 1, 0)
                s = jnp.where(seen_by(m, end, cols), s, -1e30)
                peak = jnp.max(s, axis=0, keepdims=True)
                pw = jnp.exp(s - peak)
                total = jnp.sum(pw, axis=0, keepdims=True)
                o = mm(m.vt[head, 0:end], pw.astype(BF16), 1, 0) / total
                m.attt[head, cols] = o
                outs.append(o)
                m.lse[pl.ds(p * 2 + h, 1), cols] = peak + jnp.log(total)
            m.att[cols, lanes] = jnp.concatenate(outs, axis=0).T.astype(BF16)

        @pl.when(p == 0)
        def _():
            tick(1)

    m.flush("att", "attt", "lse")
    m.ready("w", part=1)

    @pl.loop(0, chunks)
    def _(r):
        rows = pl.ds(pl.multiple_of(r * CHUNK, CHUNK), CHUNK)
        acc = mm(m.att[rows, :], m.w[:, qkv : qkv + wide], 1, 1)
        for c in range(2):
            cols = slice(c * half, (c + 1) * half)
            up = slice(qkv + wide + c * half, qkv + wide + (c + 1) * half)
            down = slice(qkv + wide + hidden + c * half, qkv + wide + hidden + (c + 1) * half)
            h = mm(m.two[rows, :], m.w[:, up], 1, 0)
            h = h + m.bias[0:1, qkv + c * half : qkv + (c + 1) * half]
            cdf = 0.5 * (1.0 + lax.erf(h * (0.5**0.5)))
            pdf = jnp.exp(-0.5 * h * h) * 0.3989422804014327
            act = (h * cdf).astype(BF16)
            m.act[rows, cols] = act
            m.dg[rows, cols] = (cdf + h * pdf).astype(BF16)
            acc = acc + mm(act, m.w[:, down], 1, 1)
        m.part[rows, :] = acc.astype(BF16)
        m.flush_rows(rows, "act", "dg", "part")

        @pl.when(r == 1)
        def _():
            tick(2)

    tick(3)
    m.drain()


def backward_body(m, tick, me):
    length, width = m.x.shape
    wide = m.att.shape[1]
    hidden = m.act.shape[1]
    qkv = 3 * wide
    pairs = wide // (2 * HEAD)
    chunks = length // CHUNK
    half = hidden // 2
    scaling = HEAD ** (-0.5)
    tick(0)
    m.load("slope", "w", "dg", "attt", "lse", "k", "qt", "v", "kt", "q", "tabs", "x", "one", "att", "two", "act")
    first_call = m.prev is None
    if not first_call:
        m.load("prev")
    spread_ids(m, length)
    m.gk[...] = jnp.zeros_like(m.gk)
    m.gv[...] = jnp.zeros_like(m.gv)
    if first_call:
        m.tok[...] = jnp.zeros_like(m.tok)
        m.sums[...] = jnp.zeros_like(m.sums)
    else:
        m.tok[...] = m.tok_in[...]
        m.sums[...] = m.sums_in[...]
    m.ready("slope", "w", "dg")
    own = m.own_rows
    mine = pl.ds(pl.multiple_of(me * own, own), own)
    m.sums[4:5, :] += jnp.sum(m.slope[mine, :].astype(F32), axis=0, keepdims=True)

    @pl.loop(0, chunks)
    def _(r):
        rows = pl.ds(pl.multiple_of(r * CHUNK, CHUNK), CHUNK)
        s = m.slope[rows, :]
        g = mm(s, m.w[:, qkv : qkv + wide], 1, 0).astype(BF16)
        m.gat[rows, :] = g
        m.gatt[:, rows] = g.T
        for c in range(2):
            cols = slice(c * half, (c + 1) * half)
            down = slice(qkv + wide + hidden + c * half, qkv + wide + hidden + (c + 1) * half)
            t = (mm(s, m.w[:, down], 1, 0) * m.dg[rows, cols].astype(F32)).astype(BF16)
            m.gh[rows, cols] = t
            m.tok[0:1, qkv + c * half : qkv + (c + 1) * half] += jnp.sum(
                t.astype(F32), axis=0, keepdims=True
            )

    m.ready("attt", "lse", "k", "qt", "v", "kt", "q", "tabs")
    for h in range(2 * pairs):
        head = slice(h * HEAD, (h + 1) * HEAD)
        m.delta[h : h + 1, :] = jnp.sum(
            m.gatt[head, :].astype(F32) * m.attt[head, :], axis=0, keepdims=True
        )

    @pl.loop(0, pairs)
    def _(p):
        lanes = pl.ds(pl.multiple_of(p * 2 * HEAD, 2 * HEAD), 2 * HEAD)
        for first, end in tiles_of(length):
            cols = slice(first, first + CHUNK)
            dqs, dss, pws = [], [], []
            for h in range(2):
                head = pl.ds(pl.multiple_of(p * 2 * HEAD + h * HEAD, HEAD), HEAD)
                s = mm(m.k[0:end, lanes], halves(m.qt[head, cols], h), 1, 0)
                row = pl.ds(p * 2 + h, 1)
                pw = jnp.where(seen_by(m, end, cols), jnp.exp(s - m.lse[row, cols]), 0.0)
                dp = mm(m.v[0:end, lanes], halves(m.gatt[head, cols], h), 1, 0)
                ds = (pw * (dp - m.delta[row, cols])).astype(BF16)
                dss.append(ds)
                pws.append(pw.astype(BF16))
                dqs.append(mm(m.kt[head, 0:end], ds, 1, 0))
            qs = jnp.concatenate([lane_half(m.q[cols, lanes], h) for h in range(2)], axis=0)
            gs = jnp.concatenate([lane_half(m.gat[cols, lanes], h) for h in range(2)], axis=0)
            m.gk[0:end, lanes] += mm(jnp.concatenate(dss, axis=1), qs, 1, 0)
            m.gv[0:end, lanes] += mm(jnp.concatenate(pws, axis=1), gs, 1, 0)
            dq = jnp.concatenate(dqs, axis=0).T * scaling
            tabs = (m.tabs[0, cols, :], -m.tabs[1, cols, :], -m.tabs[2, cols, :])
            m.gp[cols, lanes] = turn_back_and_forth(dq, *tabs).astype(BF16)

        @pl.when(p == 0)
        def _():
            tick(1)

    m.ready("x", "one", "att", "two", "act")

    @pl.loop(0, chunks)
    def _(r):
        rows = pl.ds(pl.multiple_of(r * CHUNK, CHUNK), CHUNK)
        tabs = (m.tabs[0, rows, :], -m.tabs[1, rows, :], -m.tabs[2, rows, :])
        m.gp[rows, wide : 2 * wide] = turn_back_and_forth(m.gk[rows, :], *tabs).astype(BF16)
        m.gp[rows, 2 * wide : qkv] = m.gv[rows, :].astype(BF16)
        g = m.gp[rows, :]
        m.tok[0:1, 0:qkv] += jnp.sum(g.astype(F32), axis=0, keepdims=True)
        xhat, _ = norm_parts(m.x[rows, :].astype(F32))
        d1 = mm(g, m.w[:, 0:qkv], 1, 1)
        d2 = mm(m.gh[rows, :], m.w[:, qkv + wide : qkv + wide + hidden], 1, 1)
        m.sums[0:1, :] += jnp.sum(d1 * xhat, axis=0, keepdims=True)
        m.sums[1:2, :] += jnp.sum(d1, axis=0, keepdims=True)
        m.sums[2:3, :] += jnp.sum(d2 * xhat, axis=0, keepdims=True)
        m.sums[3:4, :] += jnp.sum(d2, axis=0, keepdims=True)
        m.e[rows, :] = (d1 * m.vec[0:1, :] + d2 * m.vec[2:3, :]).astype(BF16)
        m.flush_rows(rows, "e")

        @pl.when(r == 1)
        def _():
            tick(2)

    if not first_call:
        m.ready("prev")

    @pl.loop(0, width // CHUNK)
    def _(r):
        rows = pl.ds(pl.multiple_of(r * CHUNK, CHUNK), CHUNK)

        def put(start, left, right):
            cols = slice(start, start + right.shape[1])
            new = mm(left[:, rows], right[...], 0, 0)
            if not first_call:
                new = new + m.prev[rows, cols].astype(F32)
            m.grad[rows, cols] = new.astype(BF16)

        put(0, m.one, m.gp)
        put(qkv, m.slope, m.att)
        put(qkv + wide, m.two, m.gh)
        put(qkv + wide + hidden, m.slope, m.act)
        m.flush_rows(rows, "grad")

    tick(3)
    m.drain()


def start_kernel(inputs, cotangent, shards, heads, n_dp, n_tp, cid):
    _, own_rows, width = inputs.shape
    rows = shards["w_qkv"].shape[0]
    qkv = shards["w_qkv"].shape[1]
    cols = sum(s.shape[1] for s in shards.values())

    def body(m):
        greet(n_tp, cube_peers(n_dp))
        line = Gather(m.inputs.at[0], m.x, m.line_sems, m.line_local, n_tp)
        cube = CubeGather(m.mine, m.w, m.cube_sems, m.cube_local, n_dp)
        line.step(1)
        at = qkv
        copies = []
        for n, key in enumerate(("w_out", "w_up", "w_down")):
            src = m.refs[key]
            copies.append(
                pltpu.make_async_copy(src, m.mine.at[:, at : at + src.shape[1]], m.piece_sems.at[n])
            )
            copies[-1].start()
            at += src.shape[1]
        for h in range(heads):
            for j in range(3):
                m.mine[:, j * heads * HEAD + h * HEAD : j * heads * HEAD + (h + 1) * HEAD] = m.w_qkv[
                    :, (3 * h + j) * HEAD : (3 * h + j + 1) * HEAD
                ]
        for copy in copies:
            copy.wait()
        cube.start()
        for stage in range(cube.stages()):
            cube.step(stage)
            if stage + 2 < n_tp:
                line.step(stage + 2)
        for s in range(cube.stages() + 2, n_tp + 1):
            line.step(s)
        cube.finish()

    ins = dict(inputs=(inputs, ANY), w_qkv=(shards["w_qkv"], VM))
    ins.update({k: (shards[k], ANY) for k in ("w_out", "w_up", "w_down")})
    outs = dict(
        x=(sds((n_tp * own_rows, width), BF16), ANY),
        w=(sds((n_dp, rows, cols), BF16), ANY),
    )
    scratch = dict(mine=VM((rows, cols), BF16), piece_sems=DMA((3,)))
    scratch.update(Gather.scratch("line", n_tp))
    scratch.update(CubeGather.scratch("cube", n_dp))
    return call("gather_start", body, ins, outs, scratch, cid)


def out_epilogue(m, own):
    m.done[...] = (own.astype(F32) + m.total[...] + m.b_sum[0:1, :]).astype(BF16)


def grad_epilogue(m, own, slope):
    xh, inv = norm_parts(own.astype(F32))
    e = m.total[...]
    back = (
        e - jnp.mean(e, axis=-1, keepdims=True) - xh * jnp.mean(e * xh, axis=-1, keepdims=True)
    ) * inv
    m.done[...] = slope.astype(F32) + back


def with_transfers(m, n_tp, gathers, scatters):
    line = Gather(m.g_own, m.g_full, m.line_sems, m.line_local, n_tp) if gathers else None
    sums = Scatter(m.refs["s_part"], m.s_part, m.sum_inbox, m.sum_sems, n_tp) if scatters else None

    def tick(k):
        last = k == 3
        for s in range(k + 1, n_tp + 1) if last else [k + 1]:
            if line is not None:
                line.step(s)
            if sums is not None and s < n_tp:
                if s == 1:
                    m.load("s_part")
                if s == 2:
                    m.ready("s_part")
                sums.step(s)
        if last and sums is not None:
            sums.finish(m.total)

    return tick


def transfer_specs(ins, outs, scratch, n_tp, gather, scatter, done):
    if gather is not None:
        rows, width = gather.shape
        ins["g_own"] = (gather, ANY)
        outs["g_full"] = (sds((n_tp * rows, width), BF16), ANY)
        scratch.update(Gather.scratch("line", n_tp))
    if scatter is not None:
        length, width = scatter.shape
        ins["s_part"] = (scatter, LOAD)
        outs["done"] = (sds((length // n_tp, width), done), VM)
        scratch["total"] = VM((length // n_tp, width), F32)
        scratch.update(Scatter.scratch("sum", n_tp, length // n_tp, width))


def run_forward(x, w, shared, key_row, query_row, wide, hidden, n_tp, gather, scatter, own, cid):
    length, width = x.shape
    qkv = 3 * wide
    ins = dict(
        x=(x, LOAD),
        w=(w, LOAD, [(slice(None), slice(0, qkv)), (slice(None), slice(qkv, w.shape[1]))]),
        tabs=(shared["tabs"], LOAD),
        vec=(shared["vec"], VM),
        bias=(shared["bias"], VM),
        key_row=(key_row, VM),
        query_row=(query_row, VM),
    )
    outs = dict(
        one=(sds((length, width), BF16), STORE),
        two=(sds((length, width), BF16), STORE),
        q=(sds((length, wide), BF16), STORE),
        k=(sds((length, wide), BF16), STORE),
        v=(sds((length, wide), BF16), STORE),
        qt=(sds((wide, length), BF16), STORE),
        kt=(sds((wide, length), BF16), STORE),
        att=(sds((length, wide), BF16), STORE),
        attt=(sds((wide, length), F32), STORE),
        lse=(sds((wide // HEAD, length), F32), STORE),
        act=(sds((length, hidden), BF16), STORE),
        dg=(sds((length, hidden), BF16), STORE),
        part=(sds((length, width), BF16), STORE),
    )
    scratch = dict(vt=VM((wide, length), BF16), key_ids=VM((length, 128), jnp.int32))
    transfer_specs(ins, outs, scratch, n_tp, gather, scatter, BF16)
    if scatter is not None:
        ins["own"] = (own, VM)
        ins["b_sum"] = (shared["b_sum"], VM)

    def body(m):
        greet(n_tp)
        forward_body(m, with_transfers(m, n_tp, gather is not None, scatter is not None))
        if scatter is not None:
            out_epilogue(m, m.own[...])

    return call("forward_" + str(cid), body, ins, outs, scratch, cid)


KEPT = ("one", "two", "q", "k", "v", "qt", "kt", "att", "attt", "lse", "act", "dg")


def run_backward(
    slope, x, w, shared, key_row, query_row, kept, prev, n_tp, gather, scatter, own, own_slope, cid
):
    length, width = x.shape
    wide = kept["att"].shape[1]
    hidden = kept["act"].shape[1]
    qkv = 3 * wide
    ins = dict(
        slope=(slope, LOAD),
        x=(x, LOAD),
        w=(w, LOAD),
        tabs=(shared["tabs"], LOAD),
        vec=(shared["vec"], VM),
        key_row=(key_row, VM),
        query_row=(query_row, VM),
    )
    for key in KEPT:
        ins[key] = (kept[key], LOAD)
    if prev is not None:
        ins["prev"] = (prev["grad"], LOAD)
        ins["sums_in"] = (prev["sums"], VM)
        ins["tok_in"] = (prev["tok"], VM)
    outs = dict(
        grad=(sds(w.shape, BF16), STORE),
        e=(sds((length, width), BF16), STORE),
        sums=(sds((8, width), F32), VM),
        tok=(sds((8, qkv + hidden), F32), VM),
    )
    scratch = dict(
        key_ids=VM((length, 128), jnp.int32),
        gh=VM((length, hidden), BF16),
        gat=VM((length, wide), BF16),
        gatt=VM((wide, length), BF16),
        delta=VM((wide // HEAD, length), F32),
        gk=VM((length, wide), F32),
        gv=VM((length, wide), F32),
        gp=VM((length, qkv), BF16),
    )
    transfer_specs(ins, outs, scratch, n_tp, gather, scatter, BF16 if own_slope is None else F32)
    ins["own"] = (own, VM)
    if own_slope is None:
        ins["b_sum"] = (shared["b_sum"], VM)
    else:
        ins["own_slope"] = (own_slope, VM)

    def body(m):
        greet(n_tp)
        m.own_rows = length // n_tp
        tick = with_transfers(m, n_tp, gather is not None, scatter is not None)
        backward_body(m, tick, lax.axis_index(TP))
        if own_slope is None:
            out_epilogue(m, m.own[...])
        else:
            grad_epilogue(m, m.own[...], m.own_slope[...])

    return call("backward_" + str(cid), body, ins, outs, scratch, cid, limit=60)


def end_kernel(e, grad, sums, tok, own, own_slope, heads, wide, hidden, n_dp, n_tp, cid):
    length, width = e.shape
    qkv = 3 * wide
    rows = width // n_dp
    cols = grad.shape[1]
    hops = AllSum.hops_of(n_dp, n_tp)
    dp_hops = len(bits_of(n_dp))
    ins = dict(
        grad=(grad.reshape(n_dp, rows, cols), ANY),
        sums=(sums, VM),
        tok=(tok, VM),
        own=(own, VM),
        own_slope=(own_slope, VM),
    )
    outs = dict(
        o_qkv=(sds((rows, qkv), F32), VM),
        o_out=(sds((rows, wide), F32), VM),
        o_up=(sds((rows, hidden), F32), VM),
        o_down=(sds((rows, hidden), F32), VM),
        o_sums=(sds((8, width), F32), VM),
        o_tok=(sds((8, qkv + hidden), F32), VM),
    )
    scratch = dict()
    transfer_specs(ins, outs, scratch, n_tp, None, e, F32)
    scratch.update(CubeScatter.scratch("cube", n_dp, rows, cols))
    scratch.update(AllSum.scratch("all", len(hops), (8, width)))
    scratch.update(AllSum.scratch("tok_all", dp_hops, (8, qkv + hidden)))

    def body(m):
        tensor = lax.axis_index(TP)
        peers = [{TP: tensor ^ b} for b in bits_of(n_tp)]
        greet(n_tp, cube_peers(n_dp) + peers)
        line = Scatter(m.refs["s_part"], m.s_part, m.sum_inbox, m.sum_sems, n_tp)
        cube = CubeScatter(
            m.grad, m.cube_acc, m.cube_inbox, m.cube_sibling, m.cube_sems, m.cube_sib_sems, n_dp
        )
        small = AllSum(m.all_value, m.all_inbox, m.all_sems, hops)
        toks = AllSum(m.tok_all_value, m.tok_all_inbox, m.tok_all_sems, hops[:dp_hops])
        line.step(1)
        cube.start()
        m.load("s_part")
        m.all_value[0] = m.sums[...]
        m.tok_all_value[0] = m.tok[...]
        small.start(0)
        toks.start(0)
        cube.first_sends()
        m.ready("s_part")
        small.step(0)
        toks.step(0)
        line.step(2)
        small.step(1)
        toks.step(1)
        for s in range(2, len(hops)):
            if s - 2 < cube.stages():
                cube.step(s - 2)
            if s + 1 < n_tp:
                line.step(s + 1)
            small.step(s)
            if s < dp_hops:
                toks.step(s)
        line.finish(m.total)
        grad_epilogue(m, m.own[...], m.own_slope[...])
        cube.finish()
        small.finish()
        toks.finish()
        me = lax.axis_index(DP) // 2
        for h in range(heads):
            for j in range(3):
                m.o_qkv[:, (3 * h + j) * HEAD : (3 * h + j + 1) * HEAD] = m.cube_acc[
                    me, :, j * wide + h * HEAD : j * wide + (h + 1) * HEAD
                ].astype(F32)
        m.o_out[...] = m.cube_acc[me, :, qkv : qkv + wide].astype(F32)
        m.o_up[...] = m.cube_acc[me, :, qkv + wide : qkv + wide + hidden].astype(F32)
        m.o_down[...] = m.cube_acc[me, :, qkv + wide + hidden :].astype(F32)
        m.o_sums[...] = m.all_value[len(hops)]
        m.o_tok[...] = m.tok_all_value[dp_hops]

    return call("scatter_end", body, ins, outs, scratch, cid)


def make(n_dp, n_tp):
    def on_device(
        inputs, cotangent, lengths, block_ids, ln1_gain, ln1_bias, ln2_gain, ln2_bias,
        w_qkv, b_qkv, w_out, b_out, w_up, b_up, w_down, b_down,
    ):
        seqs, own_rows, width = inputs.shape
        length = block_ids.shape[1]
        heads = w_qkv.shape[1] // (3 * HEAD)
        wide = heads * HEAD
        qkv = 3 * wide
        hidden = w_up.shape[1]
        shards = dict(w_qkv=w_qkv, w_out=w_out, w_up=w_up, w_down=w_down)
        first = start_kernel(inputs, cotangent, shards, heads, n_dp, n_tp, 1)
        w = first["w"].reshape(width, qkv + wide + 2 * hidden)
        bias = jnp.concatenate(
            [b_qkv.reshape(heads, 3, HEAD).transpose(1, 0, 2).reshape(qkv), b_up]
        ).reshape(1, qkv + hidden)
        place = jnp.arange(length, dtype=jnp.int32)
        limited = jnp.where(place[None, :] < lengths[:, None], block_ids, jnp.int32(1 << 30))
        shared = dict(
            vec=jnp.stack([ln1_gain, ln1_bias, ln2_gain, ln2_bias]),
            bias=bias,
            b_sum=(b_out + b_down)[None, :],
            tabs=jnp.asarray(rope_lanes(length)),
        )
        key = lambda i: (limited[i : i + 1], block_ids[i : i + 1])
        fa = run_forward(
            first["x"], w, shared, *key(0), wide, hidden, n_tp, inputs[1], None, None, 2
        )
        fb = run_forward(
            fa["g_full"], w, shared, *key(1), wide, hidden, n_tp, cotangent[0], fa["part"], inputs[0], 3
        )
        ba = run_backward(
            fb["g_full"], first["x"], w, shared, *key(0), fa, None, n_tp,
            cotangent[1], fb["part"], inputs[1], None, 4,
        )
        bb = run_backward(
            ba["g_full"], fa["g_full"], w, shared, *key(1), fb, ba, n_tp,
            None, ba["e"], inputs[0], cotangent[0], 5,
        )
        end = end_kernel(
            bb["e"], bb["grad"], bb["sums"], bb["tok"], inputs[1], cotangent[1],
            heads, wide, hidden, n_dp, n_tp, 6,
        )
        sums, tok = end["o_sums"], end["o_tok"][0]
        return (
            jnp.stack([fb["done"], ba["done"]]),
            jnp.stack([bb["done"], end["done"]]),
            end["o_qkv"],
            end["o_out"],
            end["o_up"],
            end["o_down"],
            tok[:qkv].reshape(3, heads, HEAD).transpose(1, 0, 2).reshape(qkv),
            tok[qkv:],
            sums[0],
            sums[1],
            sums[2],
            sums[3],
            sums[4],
            sums[4],
        )

    return on_device


def solution(mesh):
    in_specs = (
        P(DP, TP, None),
        P(DP, TP, None),
        P(DP),
        P(DP, None),
        P(),
        P(),
        P(),
        P(),
        P(DP, TP),
        P(TP),
        P(DP, TP),
        P(),
        P(DP, TP),
        P(TP),
        P(DP, TP),
        P(),
    )
    out_specs = (
        P(DP, TP, None),
        P(DP, TP, None),
        P(DP, TP),
        P(DP, TP),
        P(DP, TP),
        P(DP, TP),
        P(TP),
        P(TP),
        P(),
        P(),
        P(),
        P(),
        P(),
        P(),
    )
    return jax.shard_map(
        make(mesh.shape[DP], mesh.shape[TP]),
        mesh=mesh,
        in_specs=in_specs,
        out_specs=out_specs,
        check_vma=False,
    )
```

```python
import jax
import jax.numpy as jnp
import numpy as np
from jax import lax
from jax.experimental import pallas as pl
from jax.experimental.pallas import tpu as pltpu
from jax.sharding import PartitionSpec as P

HEAD = 64
ROT = 16
BLOCK = 256
F32 = jnp.float32
BF16 = jnp.bfloat16
MIB = 1 << 20
CHUNK = 256


def mm(a, b, ca, cb):
    return lax.dot_general(a, b, (((ca,), (cb,)), ((), ())), preferred_element_type=F32)


def norm_parts(v):
    centre = jnp.mean(v, axis=-1, keepdims=True)
    shifted = v - centre
    spread = jnp.mean(shifted * shifted, axis=-1, keepdims=True)
    inv = lax.rsqrt(spread + 1e-05)
    return shifted * inv, inv


def turn_back_and_forth(rows, cos_t, sin_t):
    reps = rows.shape[1] // cos_t.shape[1]
    if reps > 1:
        cos_t = jnp.concatenate([cos_t] * reps, axis=1)
        sin_t = jnp.concatenate([sin_t] * reps, axis=1)
    ahead = pltpu.roll(rows, rows.shape[1] - ROT // 2, 1)
    behind = pltpu.roll(rows, ROT // 2, 1)
    lane = lax.broadcasted_iota(jnp.int32, rows.shape, 1)
    return rows * cos_t + jnp.where(lane % HEAD < ROT // 2, ahead, behind) * sin_t


def rope_lanes(length):
    halved = ROT // 2
    frequency = 1.0 / 10000.0 ** (np.arange(halved, dtype=np.float32) * np.float32(2.0 / ROT))
    angles = np.arange(length, dtype=np.float32)[:, None] * frequency[None, :].astype(np.float32)
    cos_t, sin_t = np.cos(angles), np.sin(angles)
    flat = np.zeros((length, HEAD - ROT), np.float32)
    one_head = np.concatenate([cos_t, cos_t, flat + 1.0], axis=1)
    turned = np.concatenate([-sin_t, sin_t, flat], axis=1)
    return np.stack([np.concatenate([t, t], axis=1) for t in (one_head, turned)]).astype(np.float32)


def tiles_of(length):
    out = []
    for first in range(0, length, CHUNK):
        out.append((first, min(length, first + CHUNK + BLOCK)))
    return out


def halves(pair_rows, which):
    blank = jnp.zeros_like(pair_rows)
    return jnp.concatenate([pair_rows, blank] if which == 0 else [blank, pair_rows], axis=0)


def lane_half(rows, which):
    lane = lax.broadcasted_iota(jnp.int32, rows.shape, 1)
    keep = lane < HEAD if which == 0 else lane >= HEAD
    return jnp.where(keep, rows, jnp.zeros_like(rows))


def sds(shape, dtype):
    return jax.ShapeDtypeStruct(shape, dtype)


VM = pltpu.VMEM
ANY = pl.ANY
MESH = pl.DeviceIdType.MESH
DMA = pltpu.SemaphoreType.DMA
TP, DP = "tensor", "dp"
LOAD, STORE = object(), object()
LINE = 4


class Refs:
    def __init__(self, refs, stores):
        self.refs, self.stores = refs, stores

    def __getattr__(self, name):
        refs = self.__dict__["refs"]
        return refs.get(name + "@", refs.get(name))

    def copy_of(self, name, cut, incoming, n):
        far, near = self.refs[name].at[cut], self.refs[name + "@"].at[cut]
        src, dst = (far, near) if incoming else (near, far)
        return pltpu.make_async_copy(src, dst, self.refs[name + "#"].at[n])

    def load(self, *names, cut=..., n=0):
        for name in names:
            self.copy_of(name, cut, True, n).start()

    def ready(self, *names, cut=..., n=0):
        for name in names:
            self.copy_of(name, cut, True, n).wait()

    def flush(self, *names, cut=...):
        for name in names:
            self.copy_of(name, cut, False, 0).start()

    def drain(self):
        for name in self.stores:
            self.copy_of(name, ..., False, 0).wait()


def call(name, body, ins, outs, scratch, cid, limit):
    arrays, in_specs, in_names, out_shapes, out_specs = [], [], [], [], []
    stores, extra = [], {}
    for key, (array, kind) in ins.items():
        arrays.append(array)
        in_names.append(key)
        if kind is LOAD:
            extra[key + "@"] = VM(array.shape, array.dtype)
            extra[key + "#"] = DMA((2,))
            kind = ANY
        in_specs.append(pl.BlockSpec(memory_space=kind))
    for key, (shape, kind) in outs.items():
        out_shapes.append(shape)
        if kind is STORE:
            stores.append(key)
            extra[key + "@"] = VM(shape.shape, shape.dtype)
            extra[key + "#"] = DMA((1,))
            kind = ANY
        out_specs.append(pl.BlockSpec(memory_space=kind))
    scratch = {**extra, **scratch}
    names = in_names + list(outs) + list(scratch)

    def kernel(*refs):
        body(Refs(dict(zip(names, refs, strict=True)), stores))

    res = pl.pallas_call(
        kernel,
        name=name,
        out_shape=out_shapes,
        in_specs=in_specs,
        out_specs=out_specs,
        scratch_shapes=list(scratch.values()),
        compiler_params=pltpu.CompilerParams(
            vmem_limit_bytes=limit * MIB, collective_id=cid, has_side_effects=cid is not None
        ),
    )(*arrays)
    return dict(zip(outs, res))


def remote(src, dst, send, recv, peer):
    return pltpu.make_async_remote_copy(
        src_ref=src, dst_ref=dst, send_sem=send, recv_sem=recv, device_id=peer, device_id_type=MESH
    )


def bits_of(n):
    return [1 << k for k in range(n.bit_length() - 1)]


def span(bits):
    masks = [0]
    for bit in bits:
        masks = masks + [m ^ bit for m in masks]
    return masks


def greet(n_dp):
    barrier = pltpu.get_barrier_semaphore()
    me, dp = lax.axis_index(TP), lax.axis_index(DP)
    others = [{DP: dp ^ bit} for bit in bits_of(n_dp)]
    others += [{TP: me ^ 2}, {DP: dp ^ 1, TP: me ^ 2}]

    def signal(peer):
        pl.semaphore_signal(barrier, inc=1, device_id=peer, device_id_type=MESH)

    for peer in others:
        signal(peer)
    for t in range(LINE):

        @pl.when(me == t)
        def _():
            near = [s for s in (t - 1, t + 1) if 0 <= s < LINE]
            for s in near:
                signal({TP: s})
            pl.semaphore_wait(barrier, len(others) + len(near))


def at_each(run):
    me = lax.axis_index(TP)
    for t in range(LINE):

        @pl.when(me == t)
        def _():
            run(t)


def way(src, dst):
    return 0 if dst > src else 1


class LineGather:
    MOVES = {
        1: ((0, 1, 1, 0), (1, 2, 1, 1), (2, 3, 1, 2), (1, 0, 0, 1), (2, 1, 0, 2), (3, 2, 0, 3)),
        2: ((0, 1, 0, 0), (1, 2, 1, 0), (2, 3, 1, 1), (3, 2, 1, 3), (2, 1, 0, 3), (1, 0, 0, 2)),
        3: ((2, 3, 1, 0), (1, 0, 0, 3)),
    }

    def __init__(self, own, full, relay, sems, shares, local, parts):
        self.own, self.full, self.relay = own, full, relay
        self.sems, self.shares, self.local, self.parts = sems, shares, local, parts
        self.size = own.shape[1]

    @staticmethod
    def scratch(parts):
        return [DMA((4, 3, parts)), DMA((2, LINE)), DMA]

    def rows(self, part, base=0):
        size = self.size // self.parts
        return slice(base + part * size, base + (part + 1) * size)

    def place(self, which, block):
        return self.full.at[which, block * self.size : (block + 1) * self.size, :]

    def spot(self, device, seq, block, part):
        if device // 2 == seq:
            return self.full.at[0, self.rows(part, block * self.size), :]
        return self.relay.at[self.rows(part), :]

    def copy(self, step, move, part):
        src, dst, seq, block = move
        if block == src:
            a = self.own.at[seq, self.rows(part), :]
        else:
            a = self.spot(src, seq, block, part)
        k = 2 * way(src, dst)
        return remote(
            a,
            self.spot(dst, seq, block, part),
            self.sems.at[k, step - 1, part],
            self.sems.at[k + 1, step - 1, part],
            {TP: dst},
        )

    def share(self, block, own=None):
        src = self.place(0, block) if own is None else self.own.at[own]
        dp = lax.axis_index(DP)
        return remote(
            src, self.place(1, block), self.shares.at[0, block], self.shares.at[1, block], {DP: dp ^ 1}
        )

    def keep(self, t):
        return pltpu.make_async_copy(self.own.at[t // 2], self.place(0, t), self.local)

    def sends(self, t, step, own):
        return [mv for mv in self.MOVES.get(step, ()) if mv[0] == t and (mv[3] == t) == own]

    def begin(self, steps):
        def run(t):
            for step in steps:
                for mv in self.sends(t, step, True):
                    for part in range(self.parts):
                        self.copy(step, mv, part).start()
            if 1 in steps:
                self.keep(t).start()
                self.share(t, t // 2).start()

        at_each(run)

    def advance(self, step, part):
        def run(t):
            got = [mv for mv in self.MOVES[step] if mv[1] == t]
            for mv in got:
                self.copy(step, mv, part).wait_recv()
                for go in self.sends(t, step + 1, False):
                    if go[2:] == mv[2:]:
                        self.copy(step + 1, go, part).start()
            if part == self.parts - 1:
                for mv in got:
                    if t // 2 == mv[2]:
                        self.share(mv[3]).start()

        at_each(run)

    def settle(self):
        at_each(lambda t: self.keep(t).wait())
        for block in range(LINE):
            self.share(block).wait_recv()

    def finish(self):
        def run(t):
            for step in self.MOVES:
                for mv in self.sends(t, step, True) + self.sends(t, step, False):
                    for part in range(self.parts):
                        self.copy(step, mv, part).wait_send()

        at_each(run)
        for block in range(LINE):
            self.share(block).wait_send()


RAW, SUM, PASS = 0, 1, 2


class LineScatter:
    MOVES = {
        1: ((0, 1, 3, RAW), (2, 3, 3, RAW), (3, 2, 0, RAW), (1, 0, 0, RAW)),
        2: ((0, 1, 2, RAW), (1, 2, 3, SUM), (3, 2, 1, RAW), (2, 1, 0, SUM)),
        3: ((0, 1, 1, RAW), (1, 2, 2, SUM), (2, 3, 3, PASS), (3, 2, 2, RAW), (2, 1, 1, SUM), (1, 0, 0, PASS)),
    }
    LAST = (
        ((True, 1, 1), (False, 1, 3)),
        ((True, 0, 3), (False, 1, 3)),
        ((False, 0, 3), (True, 1, 3)),
        ((False, 0, 3), (True, 0, 1)),
    )

    def __init__(self, far, near, inbox, sems, parts):
        self.far, self.near, self.inbox, self.sems, self.parts = far, near, inbox, sems, parts
        self.size = inbox.shape[2]

    @staticmethod
    def scratch(rows, width, parts):
        return [VM((2, 3, rows, width), BF16), DMA((4, 3, parts))]

    def rows(self, part, base=0):
        size = self.size // self.parts
        return slice(base + part * size, base + (part + 1) * size)

    def copy(self, step, move, part):
        src, dst, block, kind = move
        d = way(src, dst)
        rows = self.rows(part)
        if kind == RAW:
            a = self.far.at[self.rows(part, block * self.size), :]
        else:
            a = self.inbox.at[d, step - 2, rows, :]
        b = self.inbox.at[d, step - 1, rows, :]
        return remote(a, b, self.sems.at[2 * d, step - 1, part], self.sems.at[2 * d + 1, step - 1, part], {TP: dst})

    def begin(self, steps):
        def run(t):
            for step in steps:
                for mv in self.MOVES[step]:
                    if mv[0] == t and mv[3] == RAW:
                        for part in range(self.parts):
                            self.copy(step, mv, part).start()

        at_each(run)

    def advance(self, step, part):
        def run(t):
            for mv in self.MOVES[step]:
                if mv[1] == t:
                    self.copy(step, mv, part).wait_recv()
            for mv in self.MOVES.get(step + 1, ()):
                if mv[0] != t or mv[3] == RAW:
                    continue
                if mv[3] == SUM:
                    d = way(mv[0], mv[1])
                    rows = self.rows(part)
                    term = self.near(self.rows(part, mv[2] * self.size))
                    self.inbox[d, step - 1, rows, :] = (
                        self.inbox[d, step - 1, rows, :].astype(F32) + term.astype(F32)
                    ).astype(BF16)
                self.copy(step + 1, mv, part).start()

        at_each(run)

    def totals(self, use):
        def run(t):
            for seq, (mine, d, step) in enumerate(self.LAST[t]):
                for part in range(self.parts):
                    rows = self.rows(part)
                    total = self.inbox[d, step - 1, rows, :].astype(F32)
                    if mine:
                        total = total + self.near(self.rows(part, t * self.size)).astype(F32)
                    use(seq, rows, total)

        at_each(run)

    def finish(self):
        def run(t):
            for step, moves in self.MOVES.items():
                for mv in moves:
                    if mv[0] == t:
                        for part in range(self.parts):
                            self.copy(step, mv, part).wait_send()

        at_each(run)


def halves_of(cols):
    middle = (cols.start + cols.stop) // 2
    return [slice(cols.start, middle), slice(middle, cols.stop)]


class WeightGather:
    def __init__(self, own, full, near_sems, z_sems, xy_sems, cuts, n_dp):
        self.own, self.full, self.cuts = own, full, cuts
        self.near_sems, self.z_sems, self.xy_sems = near_sems, z_sems, xy_sems
        self.dp, self.tp = lax.axis_index(DP), lax.axis_index(TP)
        self.q, self.core = self.dp // 2, self.dp % 2
        self.home = self.tp // 2
        self.fast = self.core == self.home
        high = [b // 2 for b in bits_of(n_dp)[1:]]
        self.orders = [high, high[::-1]]
        self.stages = len(high)

    @staticmethod
    def scratch(cuts, n_dp):
        return [DMA((cuts, 3)), DMA((cuts, 3)), DMA((cuts, 2, 2, max(n_dp // 2, 1)))]

    def kept(self, k):
        cols = self.cuts[k]
        return pltpu.make_async_copy(
            self.own.at[:, cols], self.full.at[self.dp, :, cols], self.near_sems.at[k, 2]
        )

    def beside(self, k):
        cols = self.cuts[k]
        return remote(
            self.own.at[:, cols],
            self.full.at[self.dp, :, cols],
            self.near_sems.at[k, 0],
            self.near_sems.at[k, 1],
            {DP: self.dp ^ 1},
        )

    def across(self, k, core):
        cols = self.cuts[k]
        return remote(
            self.own.at[:, cols],
            self.full.at[self.dp, :, cols],
            self.z_sems.at[k, 2],
            self.z_sems.at[k, core],
            {DP: 2 * self.q + self.home, TP: self.tp ^ 2},
        )

    def begin_plane(self, k):
        @pl.when(self.fast)
        def _():
            self.kept(k).start()

        @pl.when(jnp.logical_not(self.fast))
        def _():
            self.beside(k).start()

    def begin_z(self, k):
        self.across(k, self.core).start()

    def pair(self, k, half, stage, mask):
        bit = self.orders[half][stage]
        place = self.full.at[pl.ds(2 * (self.q ^ mask), 2), :, halves_of(self.cuts[k])[half]]
        slot = mask ^ bit
        return remote(
            place,
            place,
            self.xy_sems.at[k, half, 0, slot],
            self.xy_sems.at[k, half, 1, slot],
            {DP: self.dp ^ (2 * bit)},
        )

    def send(self, k, stage):
        if stage < self.stages:
            for half in range(2):
                for mask in span(self.orders[half][:stage]):
                    self.pair(k, half, stage, mask).start()

    def from_plane(self, k):
        self.kept(k).wait()
        self.beside(k).wait_recv()
        self.send(k, 0)

    def from_z(self, k):
        for core in range(2):
            self.across(k, core).wait_recv()
        self.send(k, 0)

    def advance(self, k, stage):
        for half in range(2):
            for mask in span(self.orders[half][:stage]):
                self.pair(k, half, stage, mask).wait_recv()
        self.send(k, stage + 1)

    def finish(self):
        for k in range(len(self.cuts)):
            self.across(k, self.core).wait_send()

            @pl.when(jnp.logical_not(self.fast))
            def _():
                self.beside(k).wait_send()

            for half in range(2):
                for stage in range(self.stages):
                    for mask in span(self.orders[half][:stage]):
                        self.pair(k, half, stage, mask).wait_send()


class GradScatter:
    def __init__(self, part, inbox, zbox, sbox, xy_sems, end_sems, cuts, n_dp):
        self.part, self.inbox, self.zbox, self.sbox = part, inbox, zbox, sbox
        self.xy_sems, self.end_sems, self.cuts = xy_sems, end_sems, cuts
        self.dp, self.tp = lax.axis_index(DP), lax.axis_index(TP)
        self.q, self.core = self.dp // 2, self.dp % 2
        self.home = self.tp // 2
        self.fast = self.core == self.home
        high = [b // 2 for b in bits_of(n_dp)[1:]]
        self.orders = [high, high[::-1]]
        self.stages = len(high)

    @staticmethod
    def scratch(cuts, n_dp, rows, cols):
        pairs = max(n_dp // 2, 2)
        return [
            VM((pairs - 1, 2, rows, cols), BF16),
            VM((rows, cols), BF16),
            VM((rows, cols), BF16),
            DMA((cuts, 2, 2, pairs)),
            DMA((cuts, 5)),
        ]

    def pair(self, k, half, stage, mask):
        bit = self.orders[half][stage]
        cols = halves_of(self.cuts[k])[half]
        return remote(
            self.part.at[pl.ds(2 * (self.q ^ mask), 2), :, cols],
            self.inbox.at[mask - 1, :, :, cols],
            self.xy_sems.at[k, half, 0, mask],
            self.xy_sems.at[k, half, 1, mask],
            {DP: self.dp ^ (2 * bit)},
        )

    def moved(self, half, stage):
        order = self.orders[half]
        return [m ^ order[stage] for m in span(order[stage + 1 :])]

    def to_owner(self, k, which):
        cols = self.cuts[k]
        return remote(
            self.part.at[2 * self.q + which, :, cols],
            self.zbox.at[:, cols],
            self.end_sems.at[k, which],
            self.end_sems.at[k, 2],
            {DP: 2 * self.q + which, TP: self.tp ^ 2},
        )

    def to_sibling(self, k):
        cols = self.cuts[k]
        return remote(
            self.part.at[self.dp ^ 1, :, cols],
            self.sbox.at[:, cols],
            self.end_sems.at[k, 3],
            self.end_sems.at[k, 4],
            {DP: self.dp ^ 1},
        )

    def send(self, k, stage):
        if stage < self.stages:
            for half in range(2):
                for mask in self.moved(half, stage):
                    self.pair(k, half, stage, mask).start()
            return

        @pl.when(self.fast)
        def _():
            self.to_sibling(k).start()

        @pl.when(jnp.logical_not(self.fast))
        def _():
            self.to_owner(k, 0).start()
            self.to_owner(k, 1).start()

    def advance(self, k, stage):
        for half in range(2):
            bit = self.orders[half][stage]
            cols = halves_of(self.cuts[k])[half]
            for mask in self.moved(half, stage):
                self.pair(k, half, stage, mask).wait_recv()
                rows = pl.ds(2 * (self.q ^ mask ^ bit), 2)
                self.part[rows, :, cols] = (
                    self.part[rows, :, cols].astype(F32) + self.inbox[mask - 1, :, :, cols].astype(F32)
                ).astype(BF16)
        self.send(k, stage + 1)

    def result(self, k, use):
        cols = self.cuts[k]
        self.to_owner(k, 0).wait_recv()

        @pl.when(self.fast)
        def _():
            use(self.part[self.dp, :, cols].astype(F32) + self.zbox[:, cols].astype(F32))

        @pl.when(jnp.logical_not(self.fast))
        def _():
            self.to_sibling(k).wait_recv()
            use(self.sbox[:, cols].astype(F32) + self.zbox[:, cols].astype(F32))

    def finish(self):
        for k in range(len(self.cuts)):
            for half in range(2):
                for stage in range(self.stages):
                    for mask in self.moved(half, stage):
                        self.pair(k, half, stage, mask).wait_send()

            @pl.when(self.fast)
            def _():
                self.to_sibling(k).wait_send()

            @pl.when(jnp.logical_not(self.fast))
            def _():
                self.to_owner(k, 0).wait_send()
                self.to_owner(k, 1).wait_send()


class AllSum:
    def __init__(self, value, inbox, sems, hops):
        self.value, self.inbox, self.sems, self.hops = value, inbox, sems, hops

    @staticmethod
    def scratch(hops, shape):
        return [VM((hops + 1,) + shape, F32), VM((hops,) + shape, F32), DMA((2, hops))]

    def copy(self, k):
        axis, bit = self.hops[k]
        peer = {axis: lax.axis_index(axis) ^ bit}
        return remote(self.value.at[k], self.inbox.at[k], self.sems.at[0, k], self.sems.at[1, k], peer)

    def start(self, k):
        if k < len(self.hops):
            self.copy(k).start()

    def step(self, k):
        if k < len(self.hops):
            self.copy(k).wait_recv()
            self.value[k + 1] = self.value[k] + self.inbox[k]
            self.start(k + 1)

    def finish(self):
        for k in range(len(self.hops)):
            self.copy(k).wait_send()


def spread_ids(m, s, length):
    for first in range(0, length, 128):
        lanes = jnp.broadcast_to(m.ids[s : s + 1, first : first + 128], (128, 128))
        m.key_ids[first : first + 128, :] = lanes.T


def seen_by(m, s, end, cols):
    keys = jnp.concatenate([m.key_ids[0:end, :]] * (CHUNK // 128), axis=1)
    return keys <= m.ids[2 + s : 3 + s, cols]


def chunk_rows(r):
    return pl.ds(pl.multiple_of(r * CHUNK, CHUNK), CHUNK)


def flat(w, cols):
    part = w[:, :, cols]
    return part.reshape(part.shape[0] * part.shape[1], part.shape[2])


def tables(m, rows, sign=1):
    return m.tabs[0, rows, :], m.tabs[1, rows, :] * sign


def regroup(out, row, heads):
    wide = heads * HEAD
    for h in range(heads):
        for j in range(3):
            out[:, (3 * h + j) * HEAD : (3 * h + j + 1) * HEAD] = row[
                :, j * wide + h * HEAD : j * wide + (h + 1) * HEAD
            ]


def degroup(out, row, heads):
    wide = heads * HEAD
    for h in range(heads):
        for j in range(3):
            out[:, j * wide + h * HEAD : j * wide + (h + 1) * HEAD] = row[
                :, (3 * h + j) * HEAD : (3 * h + j + 1) * HEAD
            ]


def project(m, s, qkv, wide):
    scaling = HEAD ** (-0.5)

    @pl.loop(0, m.x.shape[1] // CHUNK)
    def _(r):
        rows = chunk_rows(r)
        xhat, _ = norm_parts(m.x[s, rows, :].astype(F32))
        one = (xhat * m.vec[0:1, :] + m.vec[1:2, :]).astype(BF16)
        m.two[s, rows, :] = (xhat * m.vec[2:3, :] + m.vec[3:4, :]).astype(BF16)
        proj = mm(one, flat(m.w, slice(0, qkv)), 1, 0) + m.bias_now[0:1, 0:qkv]
        tabs = tables(m, rows)
        q = turn_back_and_forth(proj[:, 0:wide], *tabs).astype(BF16) * BF16(scaling)
        k = turn_back_and_forth(proj[:, wide : 2 * wide], *tabs).astype(BF16)
        v = proj[:, 2 * wide : qkv].astype(BF16)
        m.pk[s, rows, 0:wide] = q
        m.pk[s, rows, wide : 2 * wide] = k
        m.pk[s, rows, 2 * wide : qkv] = v
        m.qt[s, :, rows] = q.T
        m.kt[s, :, rows] = k.T
        m.vt[:, rows] = v.T


def attend(m, s, length, wide, midway):
    spread_ids(m, s, length)

    @pl.loop(0, wide // (2 * HEAD))
    def _(p):
        lanes = pl.ds(pl.multiple_of(p * 2 * HEAD, 2 * HEAD), 2 * HEAD)
        key_lanes = pl.ds(pl.multiple_of(wide + p * 2 * HEAD, 2 * HEAD), 2 * HEAD)
        for first, end in tiles_of(length):
            cols = slice(first, first + CHUNK)
            outs = []
            for h in range(2):
                head = pl.ds(pl.multiple_of(p * 2 * HEAD + h * HEAD, HEAD), HEAD)
                sc = mm(m.pk[s, 0:end, key_lanes], halves(m.qt[s, head, cols], h), 1, 0)
                sc = jnp.where(seen_by(m, s, end, cols), sc, -1e30)
                peak = jnp.max(sc, axis=0, keepdims=True)
                pw = jnp.exp(sc - peak)
                total = jnp.sum(pw, axis=0, keepdims=True)
                o = mm(m.vt[head, 0:end], pw.astype(BF16), 1, 0) / total
                outs.append(o)
                m.lse[s, pl.ds(p * 2 + h, 1), cols] = peak + jnp.log(total)
            m.att[s, cols, lanes] = jnp.concatenate(outs, axis=0).T.astype(BF16)

        @pl.when(p == 0)
        def _():
            midway()


def feed_up(m, s, wide, hidden):
    qkv = 3 * wide
    half = hidden // 2

    @pl.loop(0, m.x.shape[1] // CHUNK)
    def _(r):
        rows = chunk_rows(r)
        for c in range(2):
            cols = slice(c * half, (c + 1) * half)
            up = slice(qkv + c * half, qkv + (c + 1) * half)
            h = mm(m.two[s, rows, :], flat(m.w, up), 1, 0) + m.bias_now[0:1, up]
            cdf = 0.5 * (1.0 + lax.erf(h * (0.5**0.5)))
            pdf = jnp.exp(-0.5 * h * h) * 0.3989422804014327
            m.act[s, rows, cols] = (h * cdf).astype(BF16)
            m.dg[s, rows, cols] = (cdf + h * pdf).astype(BF16)
        m.flush("act", "dg", cut=(s, rows))


def feed_down(m, s, wide, hidden, use):
    at = 3 * wide + hidden

    @pl.loop(0, m.x.shape[1] // CHUNK)
    def _(r):
        rows = chunk_rows(r)
        acc = mm(m.att[s, rows, :], flat(m.w, slice(at, at + wide)), 1, 1)
        acc = acc + mm(m.act[s, rows, :], flat(m.w, slice(at + wide, at + wide + hidden)), 1, 1)
        use(r, rows, acc)


def run_forward(inputs, cotangent, shards, bias, vec, tabs, lengths, query_row, n_dp):
    _, own_rows, width = inputs.shape
    length = query_row.shape[1]
    shard_rows, qkv = shards["w_qkv"].shape
    wide = shards["w_out"].shape[1]
    hidden = shards["w_up"].shape[1]
    heads = wide // HEAD
    cols = qkv + wide + 2 * hidden
    cuts = [slice(0, qkv), slice(qkv, qkv + hidden), slice(qkv + hidden, cols)]
    ins = dict(
        inputs=(inputs, ANY), cotangent=(cotangent, ANY), tabs=(tabs, LOAD), b_qkv=(bias[0], VM), b_up=(bias[1], VM),
        g1=(vec[0], VM), b1=(vec[1], VM), g2=(vec[2], VM), b2=(vec[3], VM),
        lengths=(lengths, pltpu.SMEM), query_row=(query_row, VM),
        w_qkv=(shards["w_qkv"], VM), w_out=(shards["w_out"], ANY), w_up=(shards["w_up"], ANY),
        w_down=(shards["w_down"], ANY),
    )
    outs = dict(
        x=(sds((2, length, width), BF16), STORE),
        c=(sds((2, length, width), BF16), ANY),
        w=(sds((n_dp, shard_rows, cols), BF16), STORE),
        two=(sds((2, length, width), BF16), STORE),
        pk=(sds((2, length, qkv), BF16), STORE),
        qt=(sds((2, wide, length), BF16), STORE),
        kt=(sds((2, wide, length), BF16), STORE),
        att=(sds((2, length, wide), BF16), STORE),
        lse=(sds((2, heads, length), F32), STORE),
        act=(sds((2, length, hidden), BF16), STORE),
        dg=(sds((2, length, hidden), BF16), STORE),
        s_out=(sds((length, width), BF16), STORE),
        ids=(sds((4, length), jnp.int32), VM),
        vec=(sds((4, width), F32), VM),
    )
    small = (1, qkv + hidden)
    scratch = dict(
        vt=VM((wide, length), BF16),
        key_ids=VM((length, 128), jnp.int32),
        mine=VM((shard_rows, cols), BF16),
        relay=VM((own_rows, width), BF16),
        relay_c=VM((own_rows, width), BF16),
        term=VM((length, width), BF16),
        term_in=VM((length, width), BF16),
        bias=VM(small, F32),
        bias_in=VM(small, F32),
        bias_now=VM(small, F32),
        key_row=VM(query_row.shape, jnp.int32),
        key_in=VM(query_row.shape, jnp.int32),
        query_in=VM(query_row.shape, jnp.int32),
        piece_sems=DMA((3,)),
        small_sems=DMA((2, 3)),
        term_sems=DMA((2, length // CHUNK)),
    )
    for tag, group in (
        ("xg", LineGather.scratch(2)), ("cg", LineGather.scratch(1)), ("wg", WeightGather.scratch(3, n_dp)),
    ):
        for n, item in enumerate(group):
            scratch[tag + str(n)] = item

    def body(m):
        tp, dp = lax.axis_index(TP), lax.axis_index(DP)
        fast = dp % 2 == tp // 2
        slow = jnp.logical_not(fast)
        sibling = {DP: dp ^ 1}
        greet(n_dp)
        xg = LineGather(m.inputs, m.x, m.relay, m.xg0, m.xg1, m.xg2, 2)
        cg = LineGather(m.cotangent, m.c, m.relay_c, m.cg0, m.cg1, m.cg2, 1)
        wg = WeightGather(m.mine, m.w, m.wg0, m.wg1, m.wg2, cuts, n_dp)
        xg.begin((1,))
        at, copies = qkv, []
        for n, src in enumerate((m.w_up, m.w_out, m.w_down)):
            copies.append(
                pltpu.make_async_copy(src, m.mine.at[:, at : at + src.shape[1]], m.piece_sems.at[n])
            )
            copies[-1].start()
            at += src.shape[1]
        degroup(m.mine, m.w_qkv, heads)
        wg.begin_z(0)
        wg.begin_plane(0)
        for copy in copies:
            copy.wait()
        wg.begin_plane(1)
        wg.begin_plane(2)
        xg.begin((2,))
        edge = (tp == 0) | (tp == LINE - 1)

        @pl.when(edge)
        def _():
            wg.begin_z(1)
            wg.begin_z(2)

        degroup(m.bias, m.b_qkv, heads)
        m.bias[:, qkv:] = m.b_up[...]
        place = lax.broadcasted_iota(jnp.int32, (1, length), 1)
        for s in range(2):
            m.key_row[s : s + 1, :] = jnp.where(place < m.lengths[s], m.query_row[s : s + 1, :], 1 << 30)
        swaps = [
            remote(a, b, m.small_sems.at[0, n], m.small_sems.at[1, n], peer)
            for n, (a, b, peer) in enumerate(
                (
                    (m.key_row, m.key_in, sibling),
                    (m.query_row, m.query_in, sibling),
                    (m.bias, m.bias_in, {TP: tp ^ 2}),
                )
            )
        ]
        for swap in swaps:
            swap.start()
        m.load("tabs")
        for n, ref in enumerate((m.g1, m.b1, m.g2, m.b2)):
            m.vec[n : n + 1, :] = ref[...]

        stages = range(wg.stages)

        def quick(k, stage):
            if stage < wg.stages:

                @pl.when(fast)
                def _():
                    wg.advance(k, stage)

        def slowly(k, stage):
            @pl.when(slow)
            def _():
                if stage < 0:
                    wg.from_z(k)
                elif stage < wg.stages:
                    wg.advance(k, stage)

        @pl.when(fast)
        def _():
            for k in range(3):
                wg.from_plane(k)

        xg.advance(1, 0)
        quick(0, 0)
        xg.advance(1, 1)
        xg.advance(2, 0)
        slowly(0, -1)
        quick(0, 1)
        xg.advance(2, 1)

        @pl.when(jnp.logical_not(edge))
        def _():
            wg.begin_z(1)
            wg.begin_z(2)

        cg.begin((1, 2))
        quick(1, 0)
        quick(2, 0)
        slowly(0, 0)
        for swap in swaps:
            swap.wait()
        group = pl.ds(tp // 2, 1)
        m.ids[0:1, :] = m.key_row[group, :]
        m.ids[1:2, :] = m.key_in[group, :]
        m.ids[2:3, :] = m.query_row[group, :]
        m.ids[3:4, :] = m.query_in[group, :]
        m.bias_now[...] = jnp.where(fast, m.bias[...], m.bias_in[...])
        slowly(0, 1)
        for stage in stages[2:]:
            quick(0, stage)
            slowly(0, stage)
        xg.advance(3, 0)
        xg.advance(3, 1)
        xg.settle()
        m.flush("x")
        m.ready("tabs")

        project(m, 0, qkv, wide)
        slowly(1, -1)
        attend(m, 0, length, wide, lambda: slowly(1, 0))
        slowly(2, -1)
        slowly(1, 1)
        for stage in stages[1:]:
            quick(1, stage)
            quick(2, stage)
        project(m, 1, qkv, wide)
        m.flush("two", "pk", "qt", "kt")
        slowly(2, 0)
        attend(m, 1, length, wide, lambda: cg.advance(1, 0))
        m.flush("att", "lse")
        for stage in stages[2:]:
            slowly(1, stage)

        def term(r, rows):
            return remote(
                m.term.at[rows, :], m.term_in.at[rows, :], m.term_sems.at[0, r], m.term_sems.at[1, r], sibling
            )

        def give(r, rows, acc):
            m.term[rows, :] = acc.astype(BF16)
            term(r, rows).start()

        def take(r, rows, acc):
            term(r, rows).wait_recv()
            m.s_out[rows, :] = (acc + m.term_in[rows, :].astype(F32)).astype(BF16)
            m.flush("s_out", cut=(rows,))

        slowly(2, 1)
        for stage in stages[2:]:
            slowly(2, stage)
        feed_up(m, 1, wide, hidden)
        cg.advance(2, 0)
        feed_up(m, 0, wide, hidden)
        m.flush("w")
        feed_down(m, 1, wide, hidden, give)
        feed_down(m, 0, wide, hidden, take)
        cg.advance(3, 0)
        cg.settle()
        for r in range(length // CHUNK):
            term(r, slice(r * CHUNK, (r + 1) * CHUNK)).wait_send()
        xg.finish()
        cg.finish()
        wg.finish()
        m.drain()

    return call("forward_all", body, ins, outs, scratch, 1, 60)


def hidden_back(m, s, wide, hidden):
    qkv = 3 * wide
    half = hidden // 2

    @pl.loop(0, m.slope.shape[1] // CHUNK)
    def _(r):
        rows = chunk_rows(r)
        slope = m.slope[s, rows, :]
        at = qkv + hidden
        g = mm(slope, flat(m.w, slice(at, at + wide)), 1, 0).astype(BF16)
        m.gat[s, rows, :] = g
        for c in range(2):
            cols = slice(c * half, (c + 1) * half)
            down = slice(at + wide + c * half, at + wide + (c + 1) * half)
            t = (mm(slope, flat(m.w, down), 1, 0) * m.dg[s, rows, cols].astype(F32)).astype(BF16)
            m.dg[s, rows, cols] = t
            m.tok[0:1, qkv + c * half : qkv + (c + 1) * half] += jnp.sum(
                t.astype(F32), axis=0, keepdims=True
            )


def attend_back(m, s, length, wide, midway):
    scaling = HEAD ** (-0.5)
    spread_ids(m, s, length)
    m.gk[...] = jnp.zeros_like(m.gk)
    m.gv[...] = jnp.zeros_like(m.gv)
    for first in range(0, length, CHUNK):
        rows = slice(first, first + CHUNK)
        both = (m.gat[s, rows, :].astype(F32) * m.att[s, rows, :].astype(F32)).T
        for h in range(wide // HEAD):
            m.delta[h : h + 1, rows] = jnp.sum(both[h * HEAD : (h + 1) * HEAD, :], axis=0, keepdims=True)

    @pl.loop(0, wide // (2 * HEAD))
    def _(p):
        def lanes_at(start):
            return pl.ds(pl.multiple_of(start + p * 2 * HEAD, 2 * HEAD), 2 * HEAD)

        lanes, k_lanes, v_lanes = lanes_at(0), lanes_at(wide), lanes_at(2 * wide)
        for first, end in tiles_of(length):
            cols = slice(first, first + CHUNK)
            dqs, dss, pws = [], [], []
            turned = m.gat[s, cols, lanes].T
            for h in range(2):
                head = pl.ds(pl.multiple_of(p * 2 * HEAD + h * HEAD, HEAD), HEAD)
                row = pl.ds(p * 2 + h, 1)
                sc = mm(m.act[s, 0:end, k_lanes], halves(m.qt[s, head, cols], h), 1, 0)
                pw = jnp.where(seen_by(m, s, end, cols), jnp.exp(sc - m.lse[s, row, cols]), 0.0)
                dp = mm(m.act[s, 0:end, v_lanes], halves(turned[h * HEAD : (h + 1) * HEAD, :], h), 1, 0)
                ds = (pw * (dp - m.delta[row, cols])).astype(BF16)
                dss.append(ds)
                pws.append(pw.astype(BF16))
                dqs.append(mm(m.kt[s, head, 0:end], ds, 1, 0))
            qs = jnp.concatenate([lane_half(m.act[s, cols, lanes], h) for h in range(2)], axis=0)
            gs = jnp.concatenate([lane_half(m.gat[s, cols, lanes], h) for h in range(2)], axis=0)
            m.gk[0:end, lanes] += mm(jnp.concatenate(dss, axis=1), qs, 1, 0)
            m.gv[0:end, lanes] += mm(jnp.concatenate(pws, axis=1), gs, 1, 0)
            dq = jnp.concatenate(dqs, axis=0).T * scaling
            m.gp[cols, lanes] = turn_back_and_forth(dq, *tables(m, cols, -1)).astype(BF16)

        @pl.when(p == 0)
        def _():
            midway()


def input_back(m, s, wide, hidden, use):
    qkv = 3 * wide
    chunks = m.gp.shape[0] // CHUNK

    @pl.loop(0, chunks)
    def _(n):
        r = lax.rem(n + chunks - 1, chunks)
        rows = chunk_rows(r)
        m.gp[rows, wide : 2 * wide] = turn_back_and_forth(m.gk[rows, :], *tables(m, rows, -1)).astype(BF16)
        m.gp[rows, 2 * wide : qkv] = m.gv[rows, :].astype(BF16)
        g = m.gp[rows, :]
        m.tok[0:1, 0:qkv] += jnp.sum(g.astype(F32), axis=0, keepdims=True)
        xhat, _ = norm_parts(m.bx[s, rows, :].astype(F32))
        m.bx[s, rows, :] = (xhat * m.vec[0:1, :] + m.vec[1:2, :]).astype(BF16)
        d1 = mm(g, flat(m.w, slice(0, qkv)), 1, 1)
        d2 = mm(m.dg[s, rows, :], flat(m.w, slice(qkv, qkv + hidden)), 1, 1)
        m.sums[0:1, :] += jnp.sum(d1 * xhat, axis=0, keepdims=True)
        m.sums[1:2, :] += jnp.sum(d1, axis=0, keepdims=True)
        m.sums[2:3, :] += jnp.sum(d2 * xhat, axis=0, keepdims=True)
        m.sums[3:4, :] += jnp.sum(d2, axis=0, keepdims=True)
        use(n, r, rows, d1 * m.vec[0:1, :] + d2 * m.vec[2:3, :])


def weight_back(m, cols, pairs, again=False):
    n_dp, shard_rows, _ = m.grad.shape
    per = CHUNK // shard_rows

    @pl.loop(0, n_dp // per)
    def _(r):
        rows = chunk_rows(r)
        new = None
        for left, right in pairs:
            term = mm(left[:, rows], right[...], 0, 0)
            new = term if new is None else new + term
        new = new.reshape(per, shard_rows, new.shape[1])
        blocks = pl.ds(r * per, per)
        if again:
            new = new + m.grad[blocks, :, cols].astype(F32)
        m.grad[blocks, :, cols] = new.astype(BF16)


def run_backward(f, inputs, cotangent, tabs, b_out, b_down, n_dp):
    _, own_rows, width = inputs.shape
    _, length, _ = f["x"].shape
    _, shard_rows, cols = f["w"].shape
    wide = f["att"].shape[2]
    hidden = f["act"].shape[2]
    qkv = 3 * wide
    heads = wide // HEAD
    out_at, down_at = qkv + hidden, qkv + hidden + wide
    cuts = [slice(out_at, cols), slice(qkv, out_at), slice(0, qkv)]
    hops = [(DP, b) for b in bits_of(n_dp)] + [(TP, 1), (TP, 2)]
    tok_hops = [(DP, b) for b in bits_of(n_dp)[1:]] + [(TP, 2)]
    ins = dict(
        s_out=(f["s_out"], ANY), slope=(f["c"], LOAD), w=(f["w"], LOAD), dg=(f["dg"], LOAD),
        act=(f["act"], LOAD), att=(f["att"], LOAD), lse=(f["lse"], LOAD),
        qt=(f["qt"], LOAD), kt=(f["kt"], LOAD), tabs=(tabs, LOAD), ids=(f["ids"], VM),
        two=(f["two"], ANY), x=(f["x"], ANY), pk=(f["pk"], ANY),
        vec=(f["vec"], VM), b_out=(b_out, VM), b_down=(b_down, VM), inputs=(inputs, ANY), cotangent=(cotangent, ANY),
    )
    line = lambda n: sds((1, n), F32)
    outs = dict(
        done=(sds((2, own_rows, width), BF16), ANY),
        final=(sds((2, own_rows, width), F32), ANY),
        o_qkv=(sds((shard_rows, qkv), F32), VM),
        o_out=(sds((shard_rows, wide), F32), VM),
        o_up=(sds((shard_rows, hidden), F32), VM),
        o_down=(sds((shard_rows, hidden), F32), VM),
        o_bqkv=(line(qkv), VM),
        o_bup=(line(hidden), VM),
        o_g1=(line(width), VM),
        o_b1=(line(width), VM),
        o_g2=(line(width), VM),
        o_b2=(line(width), VM),
        o_s=(line(width), VM),
    )
    scratch = dict(
        key_ids=VM((length, 128), jnp.int32),
        bx=VM((2, length, width), BF16),
        gat=VM((2, length, wide), BF16),
        delta=VM((heads, length), F32),
        gk=VM((length, wide), F32),
        gv=VM((length, wide), F32),
        gp=VM((length, qkv), BF16),
        grad=VM((n_dp, shard_rows, cols), BF16),
        term_in=VM((length, width), BF16),
        sums=VM((8, width), F32),
        tok=VM((1, qkv + hidden), F32),
        tok_in=VM((1, qkv + hidden), F32),
        term_sems=DMA((2, length // CHUNK)),
        piece=VM((own_rows, width), BF16),
        more_sems=DMA((16,)),
        final_sems=DMA((2, width // wide)),
    )
    for tag, group in (
        ("zo", LineScatter.scratch(own_rows, width, 1)), ("ze", LineScatter.scratch(own_rows, width, 2)),
        ("gs", GradScatter.scratch(3, n_dp, shard_rows, cols)),
        ("sm", AllSum.scratch(len(hops), (8, width))), ("tk", AllSum.scratch(len(tok_hops), (1, qkv + hidden))),
    ):
        for n, item in enumerate(group):
            scratch[tag + str(n)] = item

    def body(m):
        tp, dp = lax.axis_index(TP), lax.axis_index(DP)
        fast = dp % 2 == tp // 2
        sibling = {DP: dp ^ 1}
        greet(n_dp)

        def fetched(rows):
            copy = pltpu.make_async_copy(m.s_out.at[rows, :], m.piece, m.more_sems.at[7])
            copy.start()
            copy.wait()
            return m.piece[...]

        zo = LineScatter(m.s_out, fetched, m.zo0, m.zo1, 1)
        ze = LineScatter(m.slope.at[0], lambda rows: m.slope[0, rows, :], m.ze0, m.ze1, 2)
        gs = GradScatter(m.grad, m.gs0, m.gs1, m.gs2, m.gs3, m.gs4, cuts, n_dp)
        small = AllSum(m.sm0, m.sm1, m.sm2, hops)
        toks = AllSum(m.tk0, m.tk1, m.tk2, tok_hops)
        zo.begin((1, 2, 3))
        tail = (slice(None), slice(None), slice(out_at, cols))
        front = (slice(None), slice(None), slice(0, out_at))
        m.load("slope", "dg", cut=(1,))
        m.load("w", cut=tail)
        m.load("slope", "dg", cut=(0,), n=1)

        def more(far, near, n):
            return pltpu.make_async_copy(far, near, m.more_sems.at[n])

        m.tok[...] = jnp.zeros_like(m.tok)
        m.sums[...] = jnp.zeros_like(m.sums)
        m.ready("slope", "dg", cut=(1,))
        m.ready("w", cut=tail)
        m.load("act", "att", "qt", "kt", "lse", "tabs")
        m.load("w", cut=front, n=1)
        xs = more(m.x, m.bx, 0)
        xs.start()
        hidden_back(m, 1, wide, hidden)
        m.ready("slope", "dg", cut=(0,), n=1)
        hidden_back(m, 0, wide, hidden)
        m.ready("w", cut=front, n=1)
        m.ready("act", "att", "qt", "kt", "lse", "tabs")
        zo.advance(1, 0)
        weight_back(m, slice(down_at, cols), [(m.slope.at[s], m.act.at[s]) for s in range(2)])
        pks = [more(m.pk.at[s], m.act.at[s, :, 0:qkv], 1 + s) for s in range(2)]
        for s in (1, 0):
            pks[s].start()
        weight_back(m, slice(out_at, down_at), [(m.slope.at[s], m.att.at[s]) for s in range(2)])
        gs.send(0, 0)
        pks[1].wait()

        attend_back(m, 1, length, wide, lambda: zo.advance(2, 0))
        spare = m.act.at[1]
        own_x = [pl.ds(s * own_rows, own_rows) for s in range(2)]
        own_c = [pl.ds((2 + s) * own_rows, own_rows) for s in range(2)]
        x_in = [more(m.inputs.at[s], spare.at[own_x[s], :], 8 + s) for s in range(2)]
        c_in = [more(m.cotangent.at[s], spare.at[own_c[s], :], 10 + s) for s in range(2)]
        out = [more(spare.at[own_c[s], :], m.done.at[s], 12 + s) for s in range(2)]
        for copy in x_in:
            copy.start()
        xs.wait()

        def term(r, rows):
            return remote(
                m.slope.at[1, rows, :], m.term_in.at[rows, :], m.term_sems.at[0, r], m.term_sems.at[1, r], sibling
            )

        def give(n, r, rows, e):
            m.slope[1, rows, :] = e.astype(BF16)
            term(r, rows).start()

        input_back(m, 1, wide, hidden, give)
        gs.advance(0, 0)
        weight_back(m, cuts[2], [(m.bx.at[1], m.gp)])
        twos = [more(m.two.at[0], m.act.at[0], 3), more(m.two.at[1], m.bx.at[1], 4)]
        twos[1].start()
        zo.advance(3, 0)
        for copy in x_in:
            copy.wait()
        bias = m.b_out[...] + m.b_down[...]

        def put_out(seq, rows, total):
            here = pl.ds(seq * own_rows + rows.start, rows.stop - rows.start)
            there = pl.ds((2 + seq) * own_rows + rows.start, rows.stop - rows.start)
            m.act[1, there, :] = (m.act[1, here, :].astype(F32) + total + bias).astype(BF16)

        zo.totals(put_out)
        for copy in out:
            copy.start()
        pks[0].wait()
        attend_back(m, 0, length, wide, lambda: gs.advance(0, 1))
        twos[0].start()
        for copy in out:
            copy.wait()
        for copy in c_in:
            copy.start()

        def take(n, r, rows, e):
            term(r, rows).wait_recv()
            m.slope[0, rows, :] = (e + m.term_in[rows, :].astype(F32)).astype(BF16)

            @pl.when(n == 1)
            def _():
                ze.begin((1,))

        input_back(m, 0, wide, hidden, take)
        ze.begin((2, 3))
        for s in range(2):
            c_in[s].wait()
            m.sums[4:5, :] += jnp.sum(m.act[1, own_c[s], :].astype(F32), axis=0, keepdims=True)
        m.sm0[0] = m.sums[...]
        m.tk0[0] = m.tok[...]
        small.start(0)
        toks.start(0)
        for copy in twos:
            copy.wait()
        weight_back(m, cuts[1], [(m.act.at[0], m.dg.at[0]), (m.bx.at[1], m.dg.at[1])])
        gs.send(1, 0)
        weight_back(m, cuts[2], [(m.bx.at[0], m.gp)], again=True)
        gs.send(2, 0)
        def save(k):
            def use(value):
                if k == 0:
                    m.o_out[...] = value[:, 0:wide]
                    m.o_down[...] = value[:, wide:]
                elif k == 1:
                    m.o_up[...] = value
                else:
                    regroup(m.o_qkv, value, heads)

            return use

        def sums(k):
            small.step(k)
            toks.step(k)

        ze.advance(1, 0)
        sums(0)
        ze.advance(1, 1)
        sums(1)
        for stage in range(2, gs.stages):
            gs.advance(0, stage)
        ze.advance(2, 0)
        gs.advance(1, 0)
        sums(2)
        ze.advance(2, 1)
        gs.result(0, save(0))
        gs.advance(2, 0)
        sums(3)
        ze.advance(3, 0)
        for stage in range(1, gs.stages):
            gs.advance(1, stage)
            gs.advance(2, stage)
        for k in range(4, len(hops)):
            sums(k)
        last_tok = remote(
            m.tk0.at[len(tok_hops)], m.tok_in, m.more_sems.at[5], m.more_sems.at[6], sibling
        )
        last_tok.start()
        ze.advance(3, 1)

        parts = width // wide
        boxes = (m.gk, m.gv)

        def put_total(seq, rows, total):
            for k in range(parts):
                here = pl.ds(k * own_rows + rows.start, rows.stop - rows.start)
                boxes[seq][here, :] = total[:, k * wide : (k + 1) * wide]

        def box(seq, k):
            return boxes[seq].at[k * own_rows : (k + 1) * own_rows, :]

        def finals(seq):
            return [
                pltpu.make_async_copy(
                    box(seq, k), m.final.at[seq, :, k * wide : (k + 1) * wide], m.final_sems.at[seq, k]
                )
                for k in range(parts)
            ]

        ze.totals(put_total)
        for seq in range(2):
            e = jnp.concatenate([box(seq, k)[...] for k in range(parts)], axis=1)
            xh, inv = norm_parts(m.act[1, own_x[seq], :].astype(F32))
            back = e - jnp.mean(e, axis=-1, keepdims=True) - xh * jnp.mean(e * xh, axis=-1, keepdims=True)
            back = m.act[1, own_c[seq], :].astype(F32) + back * inv
            for k in range(parts):
                box(seq, k)[...] = back[:, k * wide : (k + 1) * wide]
            for copy in finals(seq):
                copy.start()
        last_tok.wait_recv()
        tok = jnp.where(fast, m.tk0[len(tok_hops)], m.tok_in[...])
        regroup(m.o_bqkv, tok[:, 0:qkv], heads)
        m.o_bup[...] = tok[:, qkv:]
        for n, ref in enumerate((m.o_g1, m.o_b1, m.o_g2, m.o_b2, m.o_s)):
            ref[...] = m.sm0[len(hops), n : n + 1, :]
        gs.result(1, save(1))
        gs.result(2, save(2))
        for r in range(length // CHUNK):
            term(r, slice(r * CHUNK, (r + 1) * CHUNK)).wait_send()
        last_tok.wait_send()
        for seq in range(2):
            for copy in finals(seq):
                copy.wait()
        zo.finish()
        ze.finish()
        gs.finish()
        small.finish()
        toks.finish()

    return call("backward_all", body, ins, outs, scratch, 2, 63)


def settle_outputs(arrays):
    keys = list(arrays)

    def body(m):
        m.load(*keys)
        for n, key in enumerate(keys):
            m.ready(key)
            pltpu.make_async_copy(m.refs[key + "@"], m.refs[key + key], m.sems.at[n]).start()
        for n, key in enumerate(keys):
            pltpu.make_async_copy(m.refs[key + "@"], m.refs[key + key], m.sems.at[n]).wait()

    ins = {key: (a, LOAD) for key, a in arrays.items()}
    outs = {key + key: (sds(a.shape, a.dtype), ANY) for key, a in arrays.items()}
    res = call("settle", body, ins, outs, dict(sems=DMA((len(keys),))), None, 62)
    return {key: res[key + key] for key in keys}


def make(n_dp, n_tp):
    assert n_tp == LINE

    def on_device(
        inputs, cotangent, lengths, block_ids, ln1_gain, ln1_bias, ln2_gain, ln2_bias,
        w_qkv, b_qkv, w_out, b_out, w_up, b_up, w_down, b_down,
    ):
        shards = dict(w_qkv=w_qkv, w_out=w_out, w_up=w_up, w_down=w_down)
        line = lambda v: v.reshape(1, -1)
        tabs = jnp.asarray(rope_lanes(block_ids.shape[1]))
        vec = [line(v) for v in (ln1_gain, ln1_bias, ln2_gain, ln2_bias)]
        f = run_forward(
            inputs, cotangent, shards, (line(b_qkv), line(b_up)), vec, tabs, lengths, block_ids, n_dp
        )
        b = settle_outputs(run_backward(f, inputs, cotangent, tabs, line(b_out), line(b_down), n_dp))
        flat_of = lambda v: v.reshape(-1)
        slope_sum = flat_of(b["o_s"])
        return (
            b["done"], b["final"], b["o_qkv"], b["o_out"], b["o_up"], b["o_down"],
            flat_of(b["o_bqkv"]), flat_of(b["o_bup"]), flat_of(b["o_g1"]), flat_of(b["o_b1"]),
            flat_of(b["o_g2"]), flat_of(b["o_b2"]), slope_sum, slope_sum,
        )

    return on_device


def solution(mesh):
    in_specs = (
        P(DP, TP, None),
        P(DP, TP, None),
        P(DP),
        P(DP, None),
        P(),
        P(),
        P(),
        P(),
        P(DP, TP),
        P(TP),
        P(DP, TP),
        P(),
        P(DP, TP),
        P(TP),
        P(DP, TP),
        P(),
    )
    out_specs = (
        P(DP, TP, None),
        P(DP, TP, None),
        P(DP, TP),
        P(DP, TP),
        P(DP, TP),
        P(DP, TP),
        P(TP),
        P(TP),
        P(),
        P(),
        P(),
        P(),
        P(),
        P(),
    )
    return jax.shard_map(
        make(mesh.shape[DP], mesh.shape[TP]),
        mesh=mesh,
        in_specs=in_specs,
        out_specs=out_specs,
        check_vma=False,
    )
```

```python
import jax
import jax.numpy as jnp
import numpy as np
from jax import lax
from jax.experimental import pallas as pl
from jax.experimental.pallas import tpu as pltpu
from jax.sharding import PartitionSpec as P

HEAD = 64
ROT = 16
BLOCK = 256
F32 = jnp.float32
BF16 = jnp.bfloat16
MIB = 1 << 20
CHUNK = 256


def mm(a, b, ca, cb):
    return lax.dot_general(a, b, (((ca,), (cb,)), ((), ())), preferred_element_type=F32)


def norm_parts(v):
    centre = jnp.mean(v, axis=-1, keepdims=True)
    shifted = v - centre
    spread = jnp.mean(shifted * shifted, axis=-1, keepdims=True)
    inv = lax.rsqrt(spread + 1e-05)
    return shifted * inv, inv


def turn_back_and_forth(rows, cos_t, sin_t):
    reps = rows.shape[1] // cos_t.shape[1]
    if reps > 1:
        cos_t = jnp.concatenate([cos_t] * reps, axis=1)
        sin_t = jnp.concatenate([sin_t] * reps, axis=1)
    ahead = pltpu.roll(rows, rows.shape[1] - ROT // 2, 1)
    behind = pltpu.roll(rows, ROT // 2, 1)
    lane = lax.broadcasted_iota(jnp.int32, rows.shape, 1)
    return rows * cos_t + jnp.where(lane % HEAD < ROT // 2, ahead, behind) * sin_t


def rope_lanes(length):
    halved = ROT // 2
    frequency = 1.0 / 10000.0 ** (np.arange(halved, dtype=np.float32) * np.float32(2.0 / ROT))
    angles = np.arange(length, dtype=np.float32)[:, None] * frequency[None, :].astype(np.float32)
    cos_t, sin_t = np.cos(angles), np.sin(angles)
    flat = np.zeros((length, HEAD - ROT), np.float32)
    one_head = np.concatenate([cos_t, cos_t, flat + 1.0], axis=1)
    turned = np.concatenate([-sin_t, sin_t, flat], axis=1)
    return np.stack([np.concatenate([t, t], axis=1) for t in (one_head, turned)]).astype(np.float32)


def tiles_of(length):
    out = []
    for first in range(0, length, CHUNK):
        out.append((first, min(length, first + CHUNK + BLOCK)))
    return out


def halves(pair_rows, which):
    blank = jnp.zeros_like(pair_rows)
    return jnp.concatenate([pair_rows, blank] if which == 0 else [blank, pair_rows], axis=0)


def lane_half(rows, which):
    lane = lax.broadcasted_iota(jnp.int32, rows.shape, 1)
    keep = lane < HEAD if which == 0 else lane >= HEAD
    return jnp.where(keep, rows, jnp.zeros_like(rows))


def sds(shape, dtype):
    return jax.ShapeDtypeStruct(shape, dtype)


VM = pltpu.VMEM
ANY = pl.ANY
MESH = pl.DeviceIdType.MESH
DMA = pltpu.SemaphoreType.DMA
TP, DP = "tensor", "dp"
LOAD, STORE = object(), object()
LINE = 4


class Refs:
    def __init__(self, refs, stores):
        self.refs, self.stores = refs, stores

    def __getattr__(self, name):
        refs = self.__dict__["refs"]
        return refs.get(name + "@", refs.get(name))

    def copy_of(self, name, cut, incoming, n):
        far, near = self.refs[name].at[cut], self.refs[name + "@"].at[cut]
        src, dst = (far, near) if incoming else (near, far)
        return pltpu.make_async_copy(src, dst, self.refs[name + "#"].at[n])

    def load(self, *names, cut=..., n=0):
        for name in names:
            self.copy_of(name, cut, True, n).start()

    def ready(self, *names, cut=..., n=0):
        for name in names:
            self.copy_of(name, cut, True, n).wait()

    def flush(self, *names, cut=...):
        for name in names:
            self.copy_of(name, cut, False, 0).start()

    def drain(self):
        for name in self.stores:
            self.copy_of(name, ..., False, 0).wait()


def call(name, body, ins, outs, scratch, cid, limit):
    arrays, in_specs, in_names, out_shapes, out_specs = [], [], [], [], []
    stores, extra = [], {}
    for key, (array, kind) in ins.items():
        arrays.append(array)
        in_names.append(key)
        if kind is LOAD:
            extra[key + "@"] = VM(array.shape, array.dtype)
            extra[key + "#"] = DMA((2,))
            kind = ANY
        in_specs.append(pl.BlockSpec(memory_space=kind))
    for key, (shape, kind) in outs.items():
        out_shapes.append(shape)
        if kind is STORE:
            stores.append(key)
            extra[key + "@"] = VM(shape.shape, shape.dtype)
            extra[key + "#"] = DMA((1,))
            kind = ANY
        out_specs.append(pl.BlockSpec(memory_space=kind))
    scratch = {**extra, **scratch}
    names = in_names + list(outs) + list(scratch)

    def kernel(*refs):
        body(Refs(dict(zip(names, refs, strict=True)), stores))

    res = pl.pallas_call(
        kernel,
        name=name,
        out_shape=out_shapes,
        in_specs=in_specs,
        out_specs=out_specs,
        scratch_shapes=list(scratch.values()),
        compiler_params=pltpu.CompilerParams(
            vmem_limit_bytes=limit * MIB, collective_id=cid, has_side_effects=cid is not None
        ),
    )(*arrays)
    return dict(zip(outs, res))


def remote(src, dst, send, recv, peer):
    return pltpu.make_async_remote_copy(
        src_ref=src, dst_ref=dst, send_sem=send, recv_sem=recv, device_id=peer, device_id_type=MESH
    )


def bits_of(n):
    return [1 << k for k in range(n.bit_length() - 1)]


def span(bits):
    masks = [0]
    for bit in bits:
        masks = masks + [m ^ bit for m in masks]
    return masks


def greet(n_dp):
    barrier = pltpu.get_barrier_semaphore()
    me, dp = lax.axis_index(TP), lax.axis_index(DP)
    others = [{DP: dp ^ 1}] + [{DP: dp ^ (2 * mask)} for mask in range(1, n_dp // 2)]
    others += [{TP: me ^ 2}, {DP: dp ^ 1, TP: me ^ 2}]

    def signal(peer):
        pl.semaphore_signal(barrier, inc=1, device_id=peer, device_id_type=MESH)

    for peer in others:
        signal(peer)
    for t in range(LINE):

        @pl.when(me == t)
        def _():
            near = [s for s in (t - 1, t + 1) if 0 <= s < LINE]
            for s in near:
                signal({TP: s})
            pl.semaphore_wait(barrier, len(others) + len(near))


def at_each(run):
    me = lax.axis_index(TP)
    for t in range(LINE):

        @pl.when(me == t)
        def _():
            run(t)


def way(src, dst):
    return 0 if dst > src else 1


class LineGather:
    MOVES = {
        1: ((0, 1, 0, 0), (1, 2, 1, 1), (2, 3, 1, 2), (1, 0, 0, 1), (2, 1, 0, 2), (3, 2, 1, 3)),
        2: ((0, 2, 1, 0), (2, 3, 1, 1), (3, 1, 0, 3), (1, 0, 0, 2)),
        3: ((2, 3, 1, 0), (1, 0, 0, 3)),
    }

    def __init__(self, own, full, sems, shares, local, parts):
        self.own, self.full = own, full
        self.sems, self.shares, self.local, self.parts = sems, shares, local, parts
        self.size = own.shape[1]

    @staticmethod
    def scratch(parts):
        return [DMA((4, 3, parts)), DMA((2, LINE)), DMA]

    def rows(self, part, base=0):
        size = self.size // self.parts
        return slice(base + part * size, base + (part + 1) * size)

    def place(self, which, block):
        return self.full.at[which, block * self.size : (block + 1) * self.size, :]

    def spot(self, block, part):
        return self.full.at[0, self.rows(part, block * self.size), :]

    def copy(self, step, move, part):
        src, dst, seq, block = move
        if block == src:
            a = self.own.at[seq, self.rows(part), :]
        else:
            a = self.spot(block, part)
        k = 2 * way(src, dst)
        return remote(
            a,
            self.spot(block, part),
            self.sems.at[k, step - 1, part],
            self.sems.at[k + 1, step - 1, part],
            {TP: dst},
        )

    def share(self, block, own=None):
        src = self.place(0, block) if own is None else self.own.at[own]
        dp = lax.axis_index(DP)
        return remote(
            src, self.place(1, block), self.shares.at[0, block], self.shares.at[1, block], {DP: dp ^ 1}
        )

    def keep(self, t):
        return pltpu.make_async_copy(self.own.at[t // 2], self.place(0, t), self.local)

    def sends(self, t, step, own):
        return [mv for mv in self.MOVES.get(step, ()) if mv[0] == t and (mv[3] == t) == own]

    def begin(self, steps, who=range(LINE)):
        def run(t):
            if t not in who:
                return
            for step in steps:
                for mv in self.sends(t, step, True):
                    for part in range(self.parts):
                        self.copy(step, mv, part).start()
            if 1 in steps:
                self.keep(t).start()
                self.share(t, t // 2).start()

        at_each(run)

    def advance(self, step, part):
        def run(t):
            got = [mv for mv in self.MOVES[step] if mv[1] == t]
            for mv in got:
                self.copy(step, mv, part).wait_recv()
                for go in self.sends(t, step + 1, False):
                    if go[2:] == mv[2:]:
                        self.copy(step + 1, go, part).start()
            if part == self.parts - 1:
                for mv in got:
                    if t // 2 == mv[2]:
                        self.share(mv[3]).start()

        at_each(run)

    def settle(self):
        at_each(lambda t: self.keep(t).wait())
        for block in range(LINE):
            self.share(block).wait_recv()

    def finish(self):
        def run(t):
            for step in self.MOVES:
                for mv in self.sends(t, step, True) + self.sends(t, step, False):
                    for part in range(self.parts):
                        self.copy(step, mv, part).wait_send()

        at_each(run)
        for block in range(LINE):
            self.share(block).wait_send()


RAW, SUM = 0, 1


class LineScatter:
    MOVES = {
        1: ((0, 1, 3, RAW), (2, 3, 3, RAW), (3, 2, 0, RAW), (1, 0, 0, RAW)),
        2: ((0, 1, 2, RAW), (1, 3, 3, SUM), (3, 2, 1, RAW), (2, 0, 0, SUM)),
        3: ((0, 1, 1, RAW), (1, 2, 2, SUM), (3, 2, 2, RAW), (2, 1, 1, SUM)),
    }
    LAST = (
        ((True, 1, 1), (False, 1, 2)),
        ((True, 0, 3), (False, 1, 3)),
        ((False, 0, 3), (True, 1, 3)),
        ((False, 0, 2), (True, 0, 1)),
    )

    def __init__(self, far, near, inbox, sems, parts):
        self.far, self.near, self.inbox, self.sems, self.parts = far, near, inbox, sems, parts
        self.size = inbox.shape[2]

    @staticmethod
    def scratch(rows, width, parts):
        return [VM((2, 3, rows, width), BF16), DMA((4, 3, parts))]

    def rows(self, part, base=0):
        size = self.size // self.parts
        return slice(base + part * size, base + (part + 1) * size)

    def copy(self, step, move, part):
        src, dst, block, kind = move
        d = way(src, dst)
        rows = self.rows(part)
        if kind == RAW:
            a = self.far.at[self.rows(part, block * self.size), :]
        else:
            a = self.inbox.at[d, step - 2, rows, :]
        b = self.inbox.at[d, step - 1, rows, :]
        return remote(a, b, self.sems.at[2 * d, step - 1, part], self.sems.at[2 * d + 1, step - 1, part], {TP: dst})

    def begin(self, steps):
        def run(t):
            for step in steps:
                for mv in self.MOVES[step]:
                    if mv[0] == t and mv[3] == RAW:
                        for part in range(self.parts):
                            self.copy(step, mv, part).start()

        at_each(run)

    def advance(self, step, part):
        def run(t):
            for mv in self.MOVES[step]:
                if mv[1] == t:
                    self.copy(step, mv, part).wait_recv()
            for mv in self.MOVES.get(step + 1, ()):
                if mv[0] != t or mv[3] == RAW:
                    continue
                if mv[3] == SUM:
                    d = way(mv[0], mv[1])
                    rows = self.rows(part)
                    term = self.near(self.rows(part, mv[2] * self.size))
                    self.inbox[d, step - 1, rows, :] = (
                        self.inbox[d, step - 1, rows, :].astype(F32) + term.astype(F32)
                    ).astype(BF16)
                self.copy(step + 1, mv, part).start()

        at_each(run)

    def totals(self, use):
        def run(t):
            for seq, (mine, d, step) in enumerate(self.LAST[t]):
                for part in range(self.parts):
                    rows = self.rows(part)
                    total = self.inbox[d, step - 1, rows, :].astype(F32)
                    if mine:
                        total = total + self.near(self.rows(part, t * self.size)).astype(F32)
                    use(seq, rows, total)

        at_each(run)

    def finish(self):
        def run(t):
            for step, moves in self.MOVES.items():
                for mv in moves:
                    if mv[0] == t:
                        for part in range(self.parts):
                            self.copy(step, mv, part).wait_send()

        at_each(run)


def halves_of(cols):
    middle = (cols.start + cols.stop) // 2
    return [slice(cols.start, middle), slice(middle, cols.stop)]


class WeightGather:
    def __init__(self, own, full, near_sems, z_sems, xy_sems, cuts, n_dp):
        self.own, self.full, self.cuts = own, full, cuts
        self.near_sems, self.z_sems, self.xy_sems = near_sems, z_sems, xy_sems
        self.dp, self.tp = lax.axis_index(DP), lax.axis_index(TP)
        self.q, self.core = self.dp // 2, self.dp % 2
        self.home = self.tp // 2
        self.fast = self.core == self.home
        self.pairs = n_dp // 2

    @staticmethod
    def scratch(cuts, n_dp):
        return [DMA((cuts, 3)), DMA((cuts, 3)), DMA((cuts, 2, max(n_dp // 2, 1)))]

    def kept(self, k):
        cols = self.cuts[k]
        return pltpu.make_async_copy(
            self.own.at[:, cols], self.full.at[self.dp, :, cols], self.near_sems.at[k, 2]
        )

    def beside(self, k):
        cols = self.cuts[k]
        return remote(
            self.own.at[:, cols],
            self.full.at[self.dp, :, cols],
            self.near_sems.at[k, 0],
            self.near_sems.at[k, 1],
            {DP: self.dp ^ 1},
        )

    def across(self, k, core):
        cols = self.cuts[k]
        return remote(
            self.own.at[:, cols],
            self.full.at[self.dp, :, cols],
            self.z_sems.at[k, 2],
            self.z_sems.at[k, core],
            {DP: 2 * self.q + self.home, TP: self.tp ^ 2},
        )

    def begin_plane(self, k):
        @pl.when(self.fast)
        def _():
            self.kept(k).start()

        @pl.when(jnp.logical_not(self.fast))
        def _():
            self.beside(k).start()

    def begin_z(self, k):
        self.across(k, self.core).start()

    def pair(self, k, mask):
        place = self.full.at[pl.ds(2 * self.q, 2), :, self.cuts[k]]
        return remote(
            place, place, self.xy_sems.at[k, 0, mask], self.xy_sems.at[k, 1, mask], {DP: self.dp ^ (2 * mask)}
        )

    def send(self, k):
        for mask in range(1, self.pairs):
            self.pair(k, mask).start()

    def from_plane(self, k):
        self.kept(k).wait()
        self.beside(k).wait_recv()
        self.send(k)

    def from_z(self, k):
        for core in range(2):
            self.across(k, core).wait_recv()
        self.send(k)

    def arrive(self, k):
        for mask in range(1, self.pairs):
            self.pair(k, mask).wait_recv()

    def finish(self):
        for k in range(len(self.cuts)):
            self.across(k, self.core).wait_send()

            @pl.when(jnp.logical_not(self.fast))
            def _():
                self.beside(k).wait_send()

            for mask in range(1, self.pairs):
                self.pair(k, mask).wait_send()


class GradScatter:
    def __init__(self, part, inbox, zbox, sbox, xy_sems, end_sems, cuts, n_dp):
        self.part, self.inbox, self.zbox, self.sbox = part, inbox, zbox, sbox
        self.xy_sems, self.end_sems, self.cuts = xy_sems, end_sems, cuts
        self.dp, self.tp = lax.axis_index(DP), lax.axis_index(TP)
        self.q, self.core = self.dp // 2, self.dp % 2
        self.home = self.tp // 2
        self.fast = self.core == self.home
        high = [b // 2 for b in bits_of(n_dp)[1:]]
        self.orders = [high, high[::-1]]
        self.stages = len(high)

    @staticmethod
    def scratch(cuts, n_dp, rows, cols):
        pairs = max(n_dp // 2, 2)
        return [
            VM((pairs - 1, 2, rows, cols), BF16),
            VM((rows, cols), BF16),
            VM((rows, cols), BF16),
            DMA((cuts, 2, 2, pairs)),
            DMA((cuts, 5)),
        ]

    def pair(self, k, half, stage, mask):
        bit = self.orders[half][stage]
        cols = halves_of(self.cuts[k])[half]
        return remote(
            self.part.at[pl.ds(2 * (self.q ^ mask), 2), :, cols],
            self.inbox.at[mask - 1, :, :, cols],
            self.xy_sems.at[k, half, 0, mask],
            self.xy_sems.at[k, half, 1, mask],
            {DP: self.dp ^ (2 * bit)},
        )

    def moved(self, half, stage):
        order = self.orders[half]
        return [m ^ order[stage] for m in span(order[stage + 1 :])]

    def to_owner(self, k, which):
        cols = self.cuts[k]
        return remote(
            self.part.at[2 * self.q + which, :, cols],
            self.zbox.at[:, cols],
            self.end_sems.at[k, which],
            self.end_sems.at[k, 2],
            {DP: 2 * self.q + which, TP: self.tp ^ 2},
        )

    def to_sibling(self, k):
        cols = self.cuts[k]
        return remote(
            self.part.at[self.dp ^ 1, :, cols],
            self.sbox.at[:, cols],
            self.end_sems.at[k, 3],
            self.end_sems.at[k, 4],
            {DP: self.dp ^ 1},
        )

    def send(self, k, stage):
        if stage < self.stages:
            for half in range(2):
                for mask in self.moved(half, stage):
                    self.pair(k, half, stage, mask).start()
            return

        @pl.when(self.fast)
        def _():
            self.to_sibling(k).start()

        @pl.when(jnp.logical_not(self.fast))
        def _():
            self.to_owner(k, 0).start()
            self.to_owner(k, 1).start()

    def advance(self, k, stage):
        for half in range(2):
            bit = self.orders[half][stage]
            cols = halves_of(self.cuts[k])[half]
            for mask in self.moved(half, stage):
                self.pair(k, half, stage, mask).wait_recv()
                rows = pl.ds(2 * (self.q ^ mask ^ bit), 2)
                self.part[rows, :, cols] = (
                    self.part[rows, :, cols].astype(F32) + self.inbox[mask - 1, :, :, cols].astype(F32)
                ).astype(BF16)
        self.send(k, stage + 1)

    def result(self, k, use):
        cols = self.cuts[k]
        self.to_owner(k, 0).wait_recv()

        @pl.when(self.fast)
        def _():
            use(self.part[self.dp, :, cols].astype(F32) + self.zbox[:, cols].astype(F32))

        @pl.when(jnp.logical_not(self.fast))
        def _():
            self.to_sibling(k).wait_recv()
            use(self.sbox[:, cols].astype(F32) + self.zbox[:, cols].astype(F32))

    def finish(self):
        for k in range(len(self.cuts)):
            for half in range(2):
                for stage in range(self.stages):
                    for mask in self.moved(half, stage):
                        self.pair(k, half, stage, mask).wait_send()

            @pl.when(self.fast)
            def _():
                self.to_sibling(k).wait_send()

            @pl.when(jnp.logical_not(self.fast))
            def _():
                self.to_owner(k, 0).wait_send()
                self.to_owner(k, 1).wait_send()


class AllSum:
    def __init__(self, value, inbox, sems, hops):
        self.value, self.inbox, self.sems, self.hops = value, inbox, sems, hops

    @staticmethod
    def scratch(hops, shape):
        return [VM((hops + 1,) + shape, F32), VM((hops,) + shape, F32), DMA((2, hops))]

    def copy(self, k):
        axis, bit = self.hops[k]
        peer = {axis: lax.axis_index(axis) ^ bit}
        return remote(self.value.at[k], self.inbox.at[k], self.sems.at[0, k], self.sems.at[1, k], peer)

    def start(self, k):
        if k < len(self.hops):
            self.copy(k).start()

    def step(self, k):
        if k < len(self.hops):
            self.copy(k).wait_recv()
            self.value[k + 1] = self.value[k] + self.inbox[k]
            self.start(k + 1)

    def finish(self):
        for k in range(len(self.hops)):
            self.copy(k).wait_send()


def spread_ids(m, s, length):
    for first in range(0, length, 128):
        lanes = jnp.broadcast_to(m.ids[s : s + 1, first : first + 128], (128, 128))
        m.key_ids[first : first + 128, :] = lanes.T


def seen_by(m, s, end, cols):
    keys = jnp.concatenate([m.key_ids[0:end, :]] * (CHUNK // 128), axis=1)
    return keys <= m.ids[2 + s : 3 + s, cols]


def chunk_rows(r):
    return pl.ds(pl.multiple_of(r * CHUNK, CHUNK), CHUNK)


def flat(w, cols):
    part = w[:, :, cols]
    return part.reshape(part.shape[0] * part.shape[1], part.shape[2])


def tables(m, rows, sign=1):
    return m.tabs[0, rows, :], m.tabs[1, rows, :] * sign


def regroup(out, row, heads):
    wide = heads * HEAD
    for h in range(heads):
        for j in range(3):
            out[:, (3 * h + j) * HEAD : (3 * h + j + 1) * HEAD] = row[
                :, j * wide + h * HEAD : j * wide + (h + 1) * HEAD
            ]


def degroup(out, row, heads):
    wide = heads * HEAD
    for h in range(heads):
        for j in range(3):
            out[:, j * wide + h * HEAD : j * wide + (h + 1) * HEAD] = row[
                :, (3 * h + j) * HEAD : (3 * h + j + 1) * HEAD
            ]


def project(m, s, qkv, wide):
    scaling = HEAD ** (-0.5)

    @pl.loop(0, m.x.shape[1] // CHUNK)
    def _(r):
        rows = chunk_rows(r)
        xhat, _ = norm_parts(m.x[s, rows, :].astype(F32))
        one = (xhat * m.vec[0:1, :] + m.vec[1:2, :]).astype(BF16)
        m.two[s, rows, :] = (xhat * m.vec[2:3, :] + m.vec[3:4, :]).astype(BF16)
        proj = mm(one, flat(m.w, slice(0, qkv)), 1, 0) + m.bias_now[0:1, 0:qkv]
        tabs = tables(m, rows)
        q = turn_back_and_forth(proj[:, 0:wide], *tabs).astype(BF16) * BF16(scaling)
        k = turn_back_and_forth(proj[:, wide : 2 * wide], *tabs).astype(BF16)
        v = proj[:, 2 * wide : qkv].astype(BF16)
        m.pk[s, rows, 0:wide] = q
        m.pk[s, rows, wide : 2 * wide] = k
        m.pk[s, rows, 2 * wide : qkv] = v
        m.qt[s, :, rows] = q.T
        m.kt[s, :, rows] = k.T
        m.vt[:, rows] = v.T


def attend(m, s, length, wide, midway):
    spread_ids(m, s, length)

    @pl.loop(0, wide // (2 * HEAD))
    def _(p):
        lanes = pl.ds(pl.multiple_of(p * 2 * HEAD, 2 * HEAD), 2 * HEAD)
        key_lanes = pl.ds(pl.multiple_of(wide + p * 2 * HEAD, 2 * HEAD), 2 * HEAD)
        for first, end in tiles_of(length):
            cols = slice(first, first + CHUNK)
            outs = []
            for h in range(2):
                head = pl.ds(pl.multiple_of(p * 2 * HEAD + h * HEAD, HEAD), HEAD)
                sc = mm(m.pk[s, 0:end, key_lanes], halves(m.qt[s, head, cols], h), 1, 0)
                sc = jnp.where(seen_by(m, s, end, cols), sc, -1e30)
                peak = jnp.max(sc, axis=0, keepdims=True)
                pw = jnp.exp(sc - peak)
                total = jnp.sum(pw, axis=0, keepdims=True)
                o = mm(m.vt[head, 0:end], pw.astype(BF16), 1, 0) / total
                outs.append(o)
                m.lse[s, pl.ds(p * 2 + h, 1), cols] = peak + jnp.log(total)
            m.att[s, cols, lanes] = jnp.concatenate(outs, axis=0).T.astype(BF16)

        @pl.when(p == 0)
        def _():
            midway()


def feed_up(m, s, wide, hidden):
    qkv = 3 * wide
    half = hidden // 2

    @pl.loop(0, m.x.shape[1] // CHUNK)
    def _(r):
        rows = chunk_rows(r)
        for c in range(2):
            cols = slice(c * half, (c + 1) * half)
            up = slice(qkv + c * half, qkv + (c + 1) * half)
            h = mm(m.two[s, rows, :], flat(m.w, up), 1, 0) + m.bias_now[0:1, up]
            cdf = 0.5 * (1.0 + lax.erf(h * (0.5**0.5)))
            pdf = jnp.exp(-0.5 * h * h) * 0.3989422804014327
            m.act[s, rows, cols] = (h * cdf).astype(BF16)
            m.dg[s, rows, cols] = (cdf + h * pdf).astype(BF16)
        m.flush("act", "dg", cut=(s, rows))


def feed_down(m, s, wide, hidden, use):
    at = 3 * wide + hidden

    @pl.loop(0, m.x.shape[1] // CHUNK)
    def _(r):
        rows = chunk_rows(r)
        acc = mm(m.att[s, rows, :], flat(m.w, slice(at, at + wide)), 1, 1)
        acc = acc + mm(m.act[s, rows, :], flat(m.w, slice(at + wide, at + wide + hidden)), 1, 1)
        use(r, rows, acc)


def run_forward(inputs, cotangent, shards, bias, vec, tabs, lengths, query_row, n_dp):
    _, own_rows, width = inputs.shape
    length = query_row.shape[1]
    shard_rows, qkv = shards["w_qkv"].shape
    wide = shards["w_out"].shape[1]
    hidden = shards["w_up"].shape[1]
    heads = wide // HEAD
    cols = qkv + wide + 2 * hidden
    cuts = [slice(0, qkv), slice(qkv, qkv + hidden), slice(qkv + hidden, cols)]
    ins = dict(
        inputs=(inputs, ANY), cotangent=(cotangent, ANY), tabs=(tabs, LOAD), b_qkv=(bias[0], VM), b_up=(bias[1], VM),
        g1=(vec[0], VM), b1=(vec[1], VM), g2=(vec[2], VM), b2=(vec[3], VM),
        lengths=(lengths, pltpu.SMEM), query_row=(query_row, VM),
        w_qkv=(shards["w_qkv"], VM), w_out=(shards["w_out"], ANY), w_up=(shards["w_up"], ANY),
        w_down=(shards["w_down"], ANY),
    )
    outs = dict(
        x=(sds((2, length, width), BF16), STORE),
        c=(sds((2, length, width), BF16), ANY),
        w=(sds((n_dp, shard_rows, cols), BF16), STORE),
        two=(sds((2, length, width), BF16), STORE),
        pk=(sds((2, length, qkv), BF16), STORE),
        qt=(sds((2, wide, length), BF16), STORE),
        kt=(sds((2, wide, length), BF16), STORE),
        att=(sds((2, length, wide), BF16), STORE),
        lse=(sds((2, heads, length), F32), STORE),
        act=(sds((2, length, hidden), BF16), STORE),
        dg=(sds((2, length, hidden), BF16), STORE),
        s_out=(sds((length, width), BF16), STORE),
        ids=(sds((4, length), jnp.int32), VM),
        vec=(sds((4, width), F32), VM),
    )
    small = (1, qkv + hidden)
    scratch = dict(
        vt=VM((wide, length), BF16),
        key_ids=VM((length, 128), jnp.int32),
        mine=VM((shard_rows, cols), BF16),
        term=VM((length, width), BF16),
        term_in=VM((length, width), BF16),
        bias=VM(small, F32),
        bias_in=VM(small, F32),
        bias_now=VM(small, F32),
        key_row=VM(query_row.shape, jnp.int32),
        key_in=VM(query_row.shape, jnp.int32),
        query_in=VM(query_row.shape, jnp.int32),
        piece_sems=DMA((3,)),
        small_sems=DMA((2, 3)),
        term_sems=DMA((2, length // CHUNK)),
    )
    for tag, group in (
        ("xg", LineGather.scratch(2)), ("cg", LineGather.scratch(2)), ("wg", WeightGather.scratch(3, n_dp)),
    ):
        for n, item in enumerate(group):
            scratch[tag + str(n)] = item

    def body(m):
        tp, dp = lax.axis_index(TP), lax.axis_index(DP)
        fast = dp % 2 == tp // 2
        slow = jnp.logical_not(fast)
        sibling = {DP: dp ^ 1}
        greet(n_dp)
        xg = LineGather(m.inputs, m.x, m.xg0, m.xg1, m.xg2, 2)
        cg = LineGather(m.cotangent, m.c, m.cg0, m.cg1, m.cg2, 2)
        wg = WeightGather(m.mine, m.w, m.wg0, m.wg1, m.wg2, cuts, n_dp)
        xg.begin((2,))
        xg.begin((1,), (1, 2))
        at, copies = qkv, []
        for n, src in enumerate((m.w_up, m.w_out, m.w_down)):
            copies.append(
                pltpu.make_async_copy(src, m.mine.at[:, at : at + src.shape[1]], m.piece_sems.at[n])
            )
            copies[-1].start()
            at += src.shape[1]
        degroup(m.mine, m.w_qkv, heads)
        wg.begin_z(0)
        xg.begin((1,), (0, 3))
        wg.begin_plane(0)
        for copy in copies:
            copy.wait()
        wg.begin_plane(1)
        wg.begin_plane(2)
        edge = (tp == 0) | (tp == LINE - 1)

        @pl.when(edge)
        def _():
            wg.begin_z(1)
            wg.begin_z(2)


        degroup(m.bias, m.b_qkv, heads)
        m.bias[:, qkv:] = m.b_up[...]
        place = lax.broadcasted_iota(jnp.int32, (1, length), 1)
        for s in range(2):
            m.key_row[s : s + 1, :] = jnp.where(place < m.lengths[s], m.query_row[s : s + 1, :], 1 << 30)
        swaps = [
            remote(a, b, m.small_sems.at[0, n], m.small_sems.at[1, n], peer)
            for n, (a, b, peer) in enumerate(
                (
                    (m.key_row, m.key_in, sibling),
                    (m.query_row, m.query_in, sibling),
                    (m.bias, m.bias_in, {TP: tp ^ 2}),
                )
            )
        ]
        for swap in swaps:
            swap.start()
        m.load("tabs")
        for n, ref in enumerate((m.g1, m.b1, m.g2, m.b2)):
            m.vec[n : n + 1, :] = ref[...]

        @pl.when(fast)
        def _():
            for k in range(3):
                wg.from_plane(k)

        def from_z(k):
            @pl.when(slow)
            def _():
                wg.from_z(k)

        xg.advance(1, 0)
        xg.advance(1, 1)
        xg.advance(2, 0)
        from_z(0)
        xg.advance(2, 1)

        @pl.when(jnp.logical_not(edge))
        def _():
            wg.begin_z(1)
            wg.begin_z(2)

        for swap in swaps:
            swap.wait()
        group = pl.ds(tp // 2, 1)
        m.ids[0:1, :] = m.key_row[group, :]
        m.ids[1:2, :] = m.key_in[group, :]
        m.ids[2:3, :] = m.query_row[group, :]
        m.ids[3:4, :] = m.query_in[group, :]
        m.bias_now[...] = jnp.where(fast, m.bias[...], m.bias_in[...])
        xg.advance(3, 0)
        xg.advance(3, 1)
        xg.settle()
        cg.begin((2, 1))
        m.flush("x")
        m.ready("tabs")
        wg.arrive(0)
        project(m, 0, qkv, wide)
        attend(m, 0, length, wide, lambda: from_z(1))
        from_z(2)
        project(m, 1, qkv, wide)
        m.flush("two", "pk", "qt", "kt")

        def midway():
            cg.advance(1, 0)
            cg.advance(1, 1)

        attend(m, 1, length, wide, midway)
        m.flush("att", "lse")
        cg.advance(2, 0)
        wg.arrive(1)

        def term(r, rows):
            return remote(
                m.term.at[rows, :], m.term_in.at[rows, :], m.term_sems.at[0, r], m.term_sems.at[1, r], sibling
            )

        def give(r, rows, acc):
            m.term[rows, :] = acc.astype(BF16)
            term(r, rows).start()

        def take(r, rows, acc):
            term(r, rows).wait_recv()
            m.s_out[rows, :] = (acc + m.term_in[rows, :].astype(F32)).astype(BF16)
            m.flush("s_out", cut=(rows,))

        feed_up(m, 1, wide, hidden)
        cg.advance(2, 1)
        feed_up(m, 0, wide, hidden)
        wg.arrive(2)
        m.flush("w")
        feed_down(m, 1, wide, hidden, give)
        feed_down(m, 0, wide, hidden, take)
        cg.advance(3, 0)
        cg.advance(3, 1)
        cg.settle()
        for r in range(length // CHUNK):
            term(r, slice(r * CHUNK, (r + 1) * CHUNK)).wait_send()
        xg.finish()
        cg.finish()
        wg.finish()
        m.drain()

    return call("forward_all", body, ins, outs, scratch, 1, 60)


def hidden_back(m, s, wide, hidden):
    qkv = 3 * wide
    half = hidden // 2

    @pl.loop(0, m.slope.shape[1] // CHUNK)
    def _(r):
        rows = chunk_rows(r)
        slope = m.slope[s, rows, :]
        at = qkv + hidden
        g = mm(slope, flat(m.w, slice(at, at + wide)), 1, 0).astype(BF16)
        m.gat[s, rows, :] = g
        for c in range(2):
            cols = slice(c * half, (c + 1) * half)
            down = slice(at + wide + c * half, at + wide + (c + 1) * half)
            t = (mm(slope, flat(m.w, down), 1, 0) * m.dg[s, rows, cols].astype(F32)).astype(BF16)
            m.dg[s, rows, cols] = t
            m.tok[0:1, qkv + c * half : qkv + (c + 1) * half] += jnp.sum(
                t.astype(F32), axis=0, keepdims=True
            )


def attend_back(m, s, length, wide, midway):
    scaling = HEAD ** (-0.5)
    spread_ids(m, s, length)
    m.gk[...] = jnp.zeros_like(m.gk)
    m.gv[...] = jnp.zeros_like(m.gv)
    for first in range(0, length, CHUNK):
        rows = slice(first, first + CHUNK)
        both = (m.gat[s, rows, :].astype(F32) * m.att[s, rows, :].astype(F32)).T
        for h in range(wide // HEAD):
            m.delta[h : h + 1, rows] = jnp.sum(both[h * HEAD : (h + 1) * HEAD, :], axis=0, keepdims=True)

    @pl.loop(0, wide // (2 * HEAD))
    def _(p):
        def lanes_at(start):
            return pl.ds(pl.multiple_of(start + p * 2 * HEAD, 2 * HEAD), 2 * HEAD)

        lanes, k_lanes, v_lanes = lanes_at(0), lanes_at(wide), lanes_at(2 * wide)
        for first, end in tiles_of(length):
            cols = slice(first, first + CHUNK)
            dqs, dss, pws = [], [], []
            turned = m.gat[s, cols, lanes].T
            for h in range(2):
                head = pl.ds(pl.multiple_of(p * 2 * HEAD + h * HEAD, HEAD), HEAD)
                row = pl.ds(p * 2 + h, 1)
                sc = mm(m.act[s, 0:end, k_lanes], halves(m.qt[s, head, cols], h), 1, 0)
                pw = jnp.where(seen_by(m, s, end, cols), jnp.exp(sc - m.lse[s, row, cols]), 0.0)
                dp = mm(m.act[s, 0:end, v_lanes], halves(turned[h * HEAD : (h + 1) * HEAD, :], h), 1, 0)
                ds = (pw * (dp - m.delta[row, cols])).astype(BF16)
                dss.append(ds)
                pws.append(pw.astype(BF16))
                dqs.append(mm(m.kt[s, head, 0:end], ds, 1, 0))
            qs = jnp.concatenate([lane_half(m.act[s, cols, lanes], h) for h in range(2)], axis=0)
            gs = jnp.concatenate([lane_half(m.gat[s, cols, lanes], h) for h in range(2)], axis=0)
            m.gk[0:end, lanes] += mm(jnp.concatenate(dss, axis=1), qs, 1, 0)
            m.gv[0:end, lanes] += mm(jnp.concatenate(pws, axis=1), gs, 1, 0)
            dq = jnp.concatenate(dqs, axis=0).T * scaling
            m.gp[cols, lanes] = turn_back_and_forth(dq, *tables(m, cols, -1)).astype(BF16)

        @pl.when(p == 0)
        def _():
            midway()


def input_back(m, s, wide, hidden, use):
    qkv = 3 * wide
    chunks = m.gp.shape[0] // CHUNK

    @pl.loop(0, chunks)
    def _(n):
        r = lax.rem(n + chunks - 1, chunks)
        rows = chunk_rows(r)
        m.gp[rows, wide : 2 * wide] = turn_back_and_forth(m.gk[rows, :], *tables(m, rows, -1)).astype(BF16)
        m.gp[rows, 2 * wide : qkv] = m.gv[rows, :].astype(BF16)
        g = m.gp[rows, :]
        m.tok[0:1, 0:qkv] += jnp.sum(g.astype(F32), axis=0, keepdims=True)
        xhat, _ = norm_parts(m.bx[s, rows, :].astype(F32))
        m.bx[s, rows, :] = (xhat * m.vec[0:1, :] + m.vec[1:2, :]).astype(BF16)
        d1 = mm(g, flat(m.w, slice(0, qkv)), 1, 1)
        d2 = mm(m.dg[s, rows, :], flat(m.w, slice(qkv, qkv + hidden)), 1, 1)
        m.sums[0:1, :] += jnp.sum(d1 * xhat, axis=0, keepdims=True)
        m.sums[1:2, :] += jnp.sum(d1, axis=0, keepdims=True)
        m.sums[2:3, :] += jnp.sum(d2 * xhat, axis=0, keepdims=True)
        m.sums[3:4, :] += jnp.sum(d2, axis=0, keepdims=True)
        use(n, r, rows, d1 * m.vec[0:1, :] + d2 * m.vec[2:3, :])


def weight_back(m, cols, pairs, again=False):
    n_dp, shard_rows, _ = m.grad.shape
    per = CHUNK // shard_rows

    @pl.loop(0, n_dp // per)
    def _(r):
        rows = chunk_rows(r)
        new = None
        for left, right in pairs:
            term = mm(left[:, rows], right[...], 0, 0)
            new = term if new is None else new + term
        new = new.reshape(per, shard_rows, new.shape[1])
        blocks = pl.ds(r * per, per)
        if again:
            new = new + m.grad[blocks, :, cols].astype(F32)
        m.grad[blocks, :, cols] = new.astype(BF16)


def run_backward(f, inputs, cotangent, tabs, b_out, b_down, n_dp):
    _, own_rows, width = inputs.shape
    _, length, _ = f["x"].shape
    _, shard_rows, cols = f["w"].shape
    wide = f["att"].shape[2]
    hidden = f["act"].shape[2]
    qkv = 3 * wide
    heads = wide // HEAD
    out_at, down_at = qkv + hidden, qkv + hidden + wide
    cuts = [slice(out_at, cols), slice(qkv, out_at), slice(0, qkv)]
    hops = [(DP, b) for b in bits_of(n_dp)] + [(TP, 1), (TP, 2)]
    tok_hops = [(DP, b) for b in bits_of(n_dp)[1:]] + [(TP, 2)]
    ins = dict(
        s_out=(f["s_out"], ANY), slope=(f["c"], LOAD), w=(f["w"], LOAD), dg=(f["dg"], LOAD),
        act=(f["act"], LOAD), att=(f["att"], LOAD), lse=(f["lse"], LOAD),
        qt=(f["qt"], LOAD), kt=(f["kt"], LOAD), tabs=(tabs, LOAD), ids=(f["ids"], VM),
        two=(f["two"], ANY), x=(f["x"], ANY), pk=(f["pk"], ANY),
        vec=(f["vec"], VM), b_out=(b_out, VM), b_down=(b_down, VM), inputs=(inputs, ANY), cotangent=(cotangent, ANY),
    )
    line = lambda n: sds((1, n), F32)
    outs = dict(
        done=(sds((2, own_rows, width), BF16), ANY),
        final=(sds((2, own_rows, width), F32), ANY),
        o_qkv=(sds((shard_rows, qkv), F32), VM),
        o_out=(sds((shard_rows, wide), F32), VM),
        o_up=(sds((shard_rows, hidden), F32), VM),
        o_down=(sds((shard_rows, hidden), F32), VM),
        o_bqkv=(line(qkv), VM),
        o_bup=(line(hidden), VM),
        o_g1=(line(width), VM),
        o_b1=(line(width), VM),
        o_g2=(line(width), VM),
        o_b2=(line(width), VM),
        o_s=(line(width), VM),
        o_t=(line(width), VM),
    )
    scratch = dict(
        key_ids=VM((length, 128), jnp.int32),
        bx=VM((2, length, width), BF16),
        gat=VM((2, length, wide), BF16),
        delta=VM((heads, length), F32),
        gk=VM((length, wide), F32),
        gv=VM((length, wide), F32),
        gp=VM((length, qkv), BF16),
        grad=VM((n_dp, shard_rows, cols), BF16),
        term_in=VM((length, width), BF16),
        sums=VM((8, width), F32),
        tok=VM((1, qkv + hidden), F32),
        tok_in=VM((1, qkv + hidden), F32),
        term_sems=DMA((2, length // CHUNK)),
        piece=VM((own_rows, width), BF16),
        more_sems=DMA((16,)),
        final_sems=DMA((2, width // wide)),
    )
    for tag, group in (
        ("zo", LineScatter.scratch(own_rows, width, 1)), ("ze", LineScatter.scratch(own_rows, width, 2)),
        ("gs", GradScatter.scratch(3, n_dp, shard_rows, cols)),
        ("sm", AllSum.scratch(len(hops), (8, width))), ("tk", AllSum.scratch(len(tok_hops), (1, qkv + hidden))),
    ):
        for n, item in enumerate(group):
            scratch[tag + str(n)] = item

    def body(m):
        tp, dp = lax.axis_index(TP), lax.axis_index(DP)
        fast = dp % 2 == tp // 2
        sibling = {DP: dp ^ 1}
        greet(n_dp)

        def fetched(rows):
            copy = pltpu.make_async_copy(m.s_out.at[rows, :], m.piece, m.more_sems.at[7])
            copy.start()
            copy.wait()
            return m.piece[...]

        zo = LineScatter(m.s_out, fetched, m.zo0, m.zo1, 1)
        ze = LineScatter(m.slope.at[0], lambda rows: m.slope[0, rows, :], m.ze0, m.ze1, 2)
        gs = GradScatter(m.grad, m.gs0, m.gs1, m.gs2, m.gs3, m.gs4, cuts, n_dp)
        small = AllSum(m.sm0, m.sm1, m.sm2, hops)
        toks = AllSum(m.tk0, m.tk1, m.tk2, tok_hops)
        zo.begin((1, 2, 3))
        tail = (slice(None), slice(None), slice(out_at, cols))
        front = (slice(None), slice(None), slice(0, out_at))
        m.load("slope", "dg", cut=(1,))
        m.load("w", cut=tail)
        m.load("slope", "dg", cut=(0,), n=1)

        def more(far, near, n):
            return pltpu.make_async_copy(far, near, m.more_sems.at[n])

        m.tok[...] = jnp.zeros_like(m.tok)
        m.sums[...] = jnp.zeros_like(m.sums)
        m.ready("slope", "dg", cut=(1,))
        m.ready("w", cut=tail)
        m.load("act", "att", "qt", "kt", "lse", "tabs")
        m.load("w", cut=front, n=1)
        xs = more(m.x, m.bx, 0)
        xs.start()
        hidden_back(m, 1, wide, hidden)
        m.ready("slope", "dg", cut=(0,), n=1)
        hidden_back(m, 0, wide, hidden)
        m.ready("w", cut=front, n=1)
        m.ready("act", "att", "qt", "kt", "lse", "tabs")
        zo.advance(1, 0)
        weight_back(m, slice(down_at, cols), [(m.slope.at[s], m.act.at[s]) for s in range(2)])
        pks = [more(m.pk.at[s], m.act.at[s, :, 0:qkv], 1 + s) for s in range(2)]
        for s in (1, 0):
            pks[s].start()
        weight_back(m, slice(out_at, down_at), [(m.slope.at[s], m.att.at[s]) for s in range(2)])
        gs.send(0, 0)
        pks[1].wait()

        attend_back(m, 1, length, wide, lambda: zo.advance(2, 0))
        spare = m.act.at[1]
        own_x = [pl.ds(s * own_rows, own_rows) for s in range(2)]
        own_c = [pl.ds((2 + s) * own_rows, own_rows) for s in range(2)]
        x_in = [more(m.inputs.at[s], spare.at[own_x[s], :], 8 + s) for s in range(2)]
        c_in = [more(m.cotangent.at[s], spare.at[own_c[s], :], 10 + s) for s in range(2)]
        out = [more(spare.at[own_c[s], :], m.done.at[s], 12 + s) for s in range(2)]
        for copy in x_in:
            copy.start()
        xs.wait()

        def term(r, rows):
            return remote(
                m.slope.at[1, rows, :], m.term_in.at[rows, :], m.term_sems.at[0, r], m.term_sems.at[1, r], sibling
            )

        def give(n, r, rows, e):
            m.slope[1, rows, :] = e.astype(BF16)
            term(r, rows).start()

        input_back(m, 1, wide, hidden, give)
        gs.advance(0, 0)
        weight_back(m, cuts[2], [(m.bx.at[1], m.gp)])
        twos = [more(m.two.at[0], m.act.at[0], 3), more(m.two.at[1], m.bx.at[1], 4)]
        twos[1].start()
        zo.advance(3, 0)
        for copy in x_in:
            copy.wait()
        bias = m.b_out[...] + m.b_down[...]

        def put_out(seq, rows, total):
            here = pl.ds(seq * own_rows + rows.start, rows.stop - rows.start)
            there = pl.ds((2 + seq) * own_rows + rows.start, rows.stop - rows.start)
            m.act[1, there, :] = (m.act[1, here, :].astype(F32) + total + bias).astype(BF16)

        zo.totals(put_out)
        for copy in out:
            copy.start()
        pks[0].wait()
        attend_back(m, 0, length, wide, lambda: gs.advance(0, 1))
        twos[0].start()
        for copy in out:
            copy.wait()
        for copy in c_in:
            copy.start()

        def take(n, r, rows, e):
            term(r, rows).wait_recv()
            m.slope[0, rows, :] = (e + m.term_in[rows, :].astype(F32)).astype(BF16)

            @pl.when(n == 1)
            def _():
                ze.begin((1,))

        input_back(m, 0, wide, hidden, take)
        ze.begin((2, 3))
        for s in range(2):
            c_in[s].wait()
            m.sums[4:5, :] += jnp.sum(m.act[1, own_c[s], :].astype(F32), axis=0, keepdims=True)
        m.sm0[0] = m.sums[...]
        m.tk0[0] = m.tok[...]
        small.start(0)
        toks.start(0)
        for copy in twos:
            copy.wait()
        weight_back(m, cuts[1], [(m.act.at[0], m.dg.at[0]), (m.bx.at[1], m.dg.at[1])])
        gs.send(1, 0)
        weight_back(m, cuts[2], [(m.bx.at[0], m.gp)], again=True)
        gs.send(2, 0)
        def save(k):
            def use(value):
                if k == 0:
                    m.o_out[...] = value[:, 0:wide]
                    m.o_down[...] = value[:, wide:]
                elif k == 1:
                    m.o_up[...] = value
                else:
                    regroup(m.o_qkv, value, heads)

            return use

        def sums(k):
            small.step(k)
            toks.step(k)

        ze.advance(1, 0)
        sums(0)
        ze.advance(1, 1)
        sums(1)
        for stage in range(2, gs.stages):
            gs.advance(0, stage)
        ze.advance(2, 0)
        gs.advance(1, 0)
        sums(2)
        ze.advance(2, 1)
        gs.result(0, save(0))
        gs.advance(2, 0)
        sums(3)
        ze.advance(3, 0)
        for stage in range(1, gs.stages):
            gs.advance(1, stage)
            gs.advance(2, stage)
        for k in range(4, len(hops)):
            sums(k)
        last_tok = remote(
            m.tk0.at[len(tok_hops)], m.tok_in, m.more_sems.at[5], m.more_sems.at[6], sibling
        )
        last_tok.start()
        ze.advance(3, 1)

        parts = width // wide
        boxes = (m.gk, m.gv)

        def put_total(seq, rows, total):
            for k in range(parts):
                here = pl.ds(k * own_rows + rows.start, rows.stop - rows.start)
                boxes[seq][here, :] = total[:, k * wide : (k + 1) * wide]

        def box(seq, k):
            return boxes[seq].at[k * own_rows : (k + 1) * own_rows, :]

        def finals(seq):
            return [
                pltpu.make_async_copy(
                    box(seq, k), m.final.at[seq, :, k * wide : (k + 1) * wide], m.final_sems.at[seq, k]
                )
                for k in range(parts)
            ]

        ze.totals(put_total)
        for seq in range(2):
            e = jnp.concatenate([box(seq, k)[...] for k in range(parts)], axis=1)
            xh, inv = norm_parts(m.act[1, own_x[seq], :].astype(F32))
            back = e - jnp.mean(e, axis=-1, keepdims=True) - xh * jnp.mean(e * xh, axis=-1, keepdims=True)
            back = m.act[1, own_c[seq], :].astype(F32) + back * inv
            for k in range(parts):
                box(seq, k)[...] = back[:, k * wide : (k + 1) * wide]
            for copy in finals(seq):
                copy.start()
        last_tok.wait_recv()
        tok = jnp.where(fast, m.tk0[len(tok_hops)], m.tok_in[...])
        regroup(m.o_bqkv, tok[:, 0:qkv], heads)
        m.o_bup[...] = tok[:, qkv:]
        for n, ref in enumerate((m.o_g1, m.o_b1, m.o_g2, m.o_b2, m.o_s)):
            ref[...] = m.sm0[len(hops), n : n + 1, :]
        m.o_t[...] = m.sm0[len(hops), 4:5, :]
        gs.result(1, save(1))
        gs.result(2, save(2))
        for r in range(length // CHUNK):
            term(r, slice(r * CHUNK, (r + 1) * CHUNK)).wait_send()
        last_tok.wait_send()
        for seq in range(2):
            for copy in finals(seq):
                copy.wait()
        zo.finish()
        ze.finish()
        gs.finish()
        small.finish()
        toks.finish()

    return call("backward_all", body, ins, outs, scratch, 2, 63)


def settle_outputs(arrays):
    keys = list(arrays)

    def body(m):
        m.load(*keys)
        for n, key in enumerate(keys):
            m.ready(key)
            pltpu.make_async_copy(m.refs[key + "@"], m.refs[key + key], m.sems.at[n]).start()
        for n, key in enumerate(keys):
            pltpu.make_async_copy(m.refs[key + "@"], m.refs[key + key], m.sems.at[n]).wait()

    ins = {key: (a, LOAD) for key, a in arrays.items()}
    outs = {key + key: (sds(a.shape, a.dtype), ANY) for key, a in arrays.items()}
    res = call("settle", body, ins, outs, dict(sems=DMA((len(keys),))), None, 62)
    return {key: res[key + key] for key in keys}


def make(n_dp, n_tp):
    assert n_tp == LINE

    def on_device(
        inputs, cotangent, lengths, block_ids, ln1_gain, ln1_bias, ln2_gain, ln2_bias,
        w_qkv, b_qkv, w_out, b_out, w_up, b_up, w_down, b_down,
    ):
        shards = dict(w_qkv=w_qkv, w_out=w_out, w_up=w_up, w_down=w_down)
        line = lambda v: v.reshape(1, -1)
        tabs = jnp.asarray(rope_lanes(block_ids.shape[1]))
        vec = [line(v) for v in (ln1_gain, ln1_bias, ln2_gain, ln2_bias)]
        f = run_forward(
            inputs, cotangent, shards, (line(b_qkv), line(b_up)), vec, tabs, lengths, block_ids, n_dp
        )
        b = settle_outputs(run_backward(f, inputs, cotangent, tabs, line(b_out), line(b_down), n_dp))
        flat_of = lambda v: v.reshape(-1)
        return (
            b["done"], b["final"], b["o_qkv"], b["o_out"], b["o_up"], b["o_down"],
            flat_of(b["o_bqkv"]), flat_of(b["o_bup"]), flat_of(b["o_g1"]), flat_of(b["o_b1"]),
            flat_of(b["o_g2"]), flat_of(b["o_b2"]), flat_of(b["o_s"]), flat_of(b["o_t"]),
        )

    return on_device


def solution(mesh):
    in_specs = (
        P(DP, TP, None),
        P(DP, TP, None),
        P(DP),
        P(DP, None),
        P(),
        P(),
        P(),
        P(),
        P(DP, TP),
        P(TP),
        P(DP, TP),
        P(),
        P(DP, TP),
        P(TP),
        P(DP, TP),
        P(),
    )
    out_specs = (
        P(DP, TP, None),
        P(DP, TP, None),
        P(DP, TP),
        P(DP, TP),
        P(DP, TP),
        P(DP, TP),
        P(TP),
        P(TP),
        P(),
        P(),
        P(),
        P(),
        P(),
        P(),
    )
    return jax.shard_map(
        make(mesh.shape[DP], mesh.shape[TP]),
        mesh=mesh,
        in_specs=in_specs,
        out_specs=out_specs,
        check_vma=False,
    )
```

```python
import jax
import jax.numpy as jnp
import numpy as np
from jax import lax
from jax.experimental import pallas as pl
from jax.experimental.pallas import tpu as pltpu
from jax.sharding import PartitionSpec as P

HEAD = 64
ROT = 16
BLOCK = 256
F32 = jnp.float32
BF16 = jnp.bfloat16
MIB = 1 << 20
CHUNK = 256


def mm(a, b, ca, cb):
    return lax.dot_general(a, b, (((ca,), (cb,)), ((), ())), preferred_element_type=F32)


def norm_parts(v):
    centre = jnp.mean(v, axis=-1, keepdims=True)
    shifted = v - centre
    spread = jnp.mean(shifted * shifted, axis=-1, keepdims=True)
    inv = lax.rsqrt(spread + 1e-05)
    return shifted * inv, inv


def turn_back_and_forth(rows, cos_t, sin_t):
    reps = rows.shape[1] // cos_t.shape[1]
    if reps > 1:
        cos_t = jnp.concatenate([cos_t] * reps, axis=1)
        sin_t = jnp.concatenate([sin_t] * reps, axis=1)
    ahead = pltpu.roll(rows, rows.shape[1] - ROT // 2, 1)
    behind = pltpu.roll(rows, ROT // 2, 1)
    lane = lax.broadcasted_iota(jnp.int32, rows.shape, 1)
    return rows * cos_t + jnp.where(lane % HEAD < ROT // 2, ahead, behind) * sin_t


def rope_lanes(length):
    halved = ROT // 2
    frequency = 1.0 / 10000.0 ** (np.arange(halved, dtype=np.float32) * np.float32(2.0 / ROT))
    angles = np.arange(length, dtype=np.float32)[:, None] * frequency[None, :].astype(np.float32)
    cos_t, sin_t = np.cos(angles), np.sin(angles)
    flat = np.zeros((length, HEAD - ROT), np.float32)
    one_head = np.concatenate([cos_t, cos_t, flat + 1.0], axis=1)
    turned = np.concatenate([-sin_t, sin_t, flat], axis=1)
    return np.stack([np.concatenate([t, t], axis=1) for t in (one_head, turned)]).astype(np.float32)


def tiles_of(length):
    out = []
    for first in range(0, length, CHUNK):
        out.append((first, min(length, first + CHUNK + BLOCK)))
    return out


def halves(pair_rows, which):
    blank = jnp.zeros_like(pair_rows)
    return jnp.concatenate([pair_rows, blank] if which == 0 else [blank, pair_rows], axis=0)


def lane_half(rows, which):
    lane = lax.broadcasted_iota(jnp.int32, rows.shape, 1)
    keep = lane < HEAD if which == 0 else lane >= HEAD
    return jnp.where(keep, rows, jnp.zeros_like(rows))


def sds(shape, dtype):
    return jax.ShapeDtypeStruct(shape, dtype)


VM = pltpu.VMEM
ANY = pl.ANY
MESH = pl.DeviceIdType.MESH
DMA = pltpu.SemaphoreType.DMA
TP, DP = "tensor", "dp"
LOAD, STORE = object(), object()
LINE = 4


class Refs:
    def __init__(self, refs, stores):
        self.refs, self.stores = refs, stores

    def __getattr__(self, name):
        refs = self.__dict__["refs"]
        return refs.get(name + "@", refs.get(name))

    def copy_of(self, name, cut, incoming, n):
        far, near = self.refs[name].at[cut], self.refs[name + "@"].at[cut]
        src, dst = (far, near) if incoming else (near, far)
        return pltpu.make_async_copy(src, dst, self.refs[name + "#"].at[n])

    def load(self, *names, cut=..., n=0):
        for name in names:
            self.copy_of(name, cut, True, n).start()

    def ready(self, *names, cut=..., n=0):
        for name in names:
            self.copy_of(name, cut, True, n).wait()

    def flush(self, *names, cut=...):
        for name in names:
            self.copy_of(name, cut, False, 0).start()

    def drain(self):
        for name in self.stores:
            self.copy_of(name, ..., False, 0).wait()


def call(name, body, ins, outs, scratch, cid, limit):
    arrays, in_specs, in_names, out_shapes, out_specs = [], [], [], [], []
    stores, extra = [], {}
    for key, (array, kind) in ins.items():
        arrays.append(array)
        in_names.append(key)
        if kind is LOAD:
            extra[key + "@"] = VM(array.shape, array.dtype)
            extra[key + "#"] = DMA((2,))
            kind = ANY
        in_specs.append(pl.BlockSpec(memory_space=kind))
    for key, (shape, kind) in outs.items():
        out_shapes.append(shape)
        if kind is STORE:
            stores.append(key)
            extra[key + "@"] = VM(shape.shape, shape.dtype)
            extra[key + "#"] = DMA((1,))
            kind = ANY
        out_specs.append(pl.BlockSpec(memory_space=kind))
    scratch = {**extra, **scratch}
    names = in_names + list(outs) + list(scratch)

    def kernel(*refs):
        body(Refs(dict(zip(names, refs, strict=True)), stores))

    res = pl.pallas_call(
        kernel,
        name=name,
        out_shape=out_shapes,
        in_specs=in_specs,
        out_specs=out_specs,
        scratch_shapes=list(scratch.values()),
        compiler_params=pltpu.CompilerParams(
            vmem_limit_bytes=limit * MIB, collective_id=cid, has_side_effects=cid is not None
        ),
    )(*arrays)
    return dict(zip(outs, res))


def remote(src, dst, send, recv, peer):
    return pltpu.make_async_remote_copy(
        src_ref=src, dst_ref=dst, send_sem=send, recv_sem=recv, device_id=peer, device_id_type=MESH
    )


def bits_of(n):
    return [1 << k for k in range(n.bit_length() - 1)]


def span(bits):
    masks = [0]
    for bit in bits:
        masks = masks + [m ^ bit for m in masks]
    return masks


def greet(n_dp):
    barrier = pltpu.get_barrier_semaphore()
    me, dp = lax.axis_index(TP), lax.axis_index(DP)
    others = [{DP: dp ^ 1}] + [{DP: dp ^ (2 * mask)} for mask in range(1, n_dp // 2)]
    others += [{TP: me ^ 2}, {DP: dp ^ 1, TP: me ^ 2}]

    def signal(peer):
        pl.semaphore_signal(barrier, inc=1, device_id=peer, device_id_type=MESH)

    for peer in others:
        signal(peer)
    for t in range(LINE):

        @pl.when(me == t)
        def _():
            near = [s for s in (t - 1, t + 1) if 0 <= s < LINE]
            for s in near:
                signal({TP: s})
            pl.semaphore_wait(barrier, len(others) + len(near))


def at_each(run):
    me = lax.axis_index(TP)
    for t in range(LINE):

        @pl.when(me == t)
        def _():
            run(t)


def way(src, dst):
    return 0 if dst > src else 1


class LineGather:
    MOVES = {
        1: ((0, 1, 0, 0), (1, 2, 1, 1), (2, 3, 1, 2), (1, 0, 0, 1), (2, 1, 0, 2), (3, 2, 1, 3)),
        2: ((0, 2, 1, 0), (2, 3, 1, 1), (3, 1, 0, 3), (1, 0, 0, 2)),
        3: ((2, 3, 1, 0), (1, 0, 0, 3)),
    }

    def __init__(self, own, full, sems, shares, local, parts):
        self.own, self.full = own, full
        self.sems, self.shares, self.local, self.parts = sems, shares, local, parts
        self.size = own.shape[1]

    @staticmethod
    def scratch(parts):
        return [DMA((4, 3, parts)), DMA((2, LINE)), DMA]

    def rows(self, part, base=0):
        size = self.size // self.parts
        return slice(base + part * size, base + (part + 1) * size)

    def place(self, which, block):
        return self.full.at[which, block * self.size : (block + 1) * self.size, :]

    def spot(self, block, part):
        return self.full.at[0, self.rows(part, block * self.size), :]

    def copy(self, step, move, part):
        src, dst, seq, block = move
        if block == src:
            a = self.own.at[seq, self.rows(part), :]
        else:
            a = self.spot(block, part)
        k = 2 * way(src, dst)
        return remote(
            a,
            self.spot(block, part),
            self.sems.at[k, step - 1, part],
            self.sems.at[k + 1, step - 1, part],
            {TP: dst},
        )

    def share(self, block, own=None):
        src = self.place(0, block) if own is None else self.own.at[own]
        dp = lax.axis_index(DP)
        return remote(
            src, self.place(1, block), self.shares.at[0, block], self.shares.at[1, block], {DP: dp ^ 1}
        )

    def keep(self, t):
        return pltpu.make_async_copy(self.own.at[t // 2], self.place(0, t), self.local)

    def sends(self, t, step, own):
        return [mv for mv in self.MOVES.get(step, ()) if mv[0] == t and (mv[3] == t) == own]

    def begin(self, steps, who=range(LINE)):
        def run(t):
            if t not in who:
                return
            for step in steps:
                for mv in self.sends(t, step, True):
                    for part in range(self.parts):
                        self.copy(step, mv, part).start()
            if 1 in steps:
                self.keep(t).start()
                self.share(t, t // 2).start()

        at_each(run)

    def advance(self, step, part):
        def run(t):
            got = [mv for mv in self.MOVES[step] if mv[1] == t]
            for mv in got:
                self.copy(step, mv, part).wait_recv()
                for go in self.sends(t, step + 1, False):
                    if go[2:] == mv[2:]:
                        self.copy(step + 1, go, part).start()
            if part == self.parts - 1:
                for mv in got:
                    if t // 2 == mv[2]:
                        self.share(mv[3]).start()

        at_each(run)

    def settle(self):
        at_each(lambda t: self.keep(t).wait())
        for block in range(LINE):
            self.share(block).wait_recv()

    def finish(self):
        def run(t):
            for step in self.MOVES:
                for mv in self.sends(t, step, True) + self.sends(t, step, False):
                    for part in range(self.parts):
                        self.copy(step, mv, part).wait_send()

        at_each(run)
        for block in range(LINE):
            self.share(block).wait_send()


RAW, SUM = 0, 1


class LineScatter:
    MOVES = {
        1: ((0, 1, 3, RAW), (2, 3, 3, RAW), (3, 2, 0, RAW), (1, 0, 0, RAW)),
        2: ((0, 1, 2, RAW), (1, 3, 3, SUM), (3, 2, 1, RAW), (2, 0, 0, SUM)),
        3: ((0, 1, 1, RAW), (1, 2, 2, SUM), (3, 2, 2, RAW), (2, 1, 1, SUM)),
    }
    LAST = (
        ((True, 1, 1), (False, 1, 2)),
        ((True, 0, 3), (False, 1, 3)),
        ((False, 0, 3), (True, 1, 3)),
        ((False, 0, 2), (True, 0, 1)),
    )

    def __init__(self, far, near, inbox, sems, parts):
        self.far, self.near, self.inbox, self.sems, self.parts = far, near, inbox, sems, parts
        self.size = inbox.shape[2]

    @staticmethod
    def scratch(rows, width, parts):
        return [VM((2, 3, rows, width), BF16), DMA((4, 3, parts))]

    def rows(self, part, base=0):
        size = self.size // self.parts
        return slice(base + part * size, base + (part + 1) * size)

    def copy(self, step, move, part):
        src, dst, block, kind = move
        d = way(src, dst)
        rows = self.rows(part)
        if kind == RAW:
            a = self.far.at[self.rows(part, block * self.size), :]
        else:
            a = self.inbox.at[d, step - 2, rows, :]
        b = self.inbox.at[d, step - 1, rows, :]
        return remote(a, b, self.sems.at[2 * d, step - 1, part], self.sems.at[2 * d + 1, step - 1, part], {TP: dst})

    def begin(self, steps):
        def run(t):
            for step in steps:
                for mv in self.MOVES[step]:
                    if mv[0] == t and mv[3] == RAW:
                        for part in range(self.parts):
                            self.copy(step, mv, part).start()

        at_each(run)

    def advance(self, step, part):
        def run(t):
            for mv in self.MOVES[step]:
                if mv[1] == t:
                    self.copy(step, mv, part).wait_recv()
            for mv in self.MOVES.get(step + 1, ()):
                if mv[0] != t or mv[3] == RAW:
                    continue
                if mv[3] == SUM:
                    d = way(mv[0], mv[1])
                    rows = self.rows(part)
                    term = self.near(self.rows(part, mv[2] * self.size))
                    self.inbox[d, step - 1, rows, :] = (
                        self.inbox[d, step - 1, rows, :].astype(F32) + term.astype(F32)
                    ).astype(BF16)
                self.copy(step + 1, mv, part).start()

        at_each(run)

    def totals(self, use):
        def run(t):
            for seq, (mine, d, step) in enumerate(self.LAST[t]):
                for part in range(self.parts):
                    rows = self.rows(part)
                    total = self.inbox[d, step - 1, rows, :].astype(F32)
                    if mine:
                        total = total + self.near(self.rows(part, t * self.size)).astype(F32)
                    use(seq, rows, total)

        at_each(run)

    def finish(self):
        def run(t):
            for step, moves in self.MOVES.items():
                for mv in moves:
                    if mv[0] == t:
                        for part in range(self.parts):
                            self.copy(step, mv, part).wait_send()

        at_each(run)


def halves_of(cols):
    middle = (cols.start + cols.stop) // 2
    return [slice(cols.start, middle), slice(middle, cols.stop)]


class WeightGather:
    def __init__(self, own, full, near_sems, z_sems, xy_sems, cuts, n_dp):
        self.own, self.full, self.cuts = own, full, cuts
        self.near_sems, self.z_sems, self.xy_sems = near_sems, z_sems, xy_sems
        self.dp, self.tp = lax.axis_index(DP), lax.axis_index(TP)
        self.q, self.core = self.dp // 2, self.dp % 2
        self.home = self.tp // 2
        self.fast = self.core == self.home
        self.pairs = n_dp // 2

    @staticmethod
    def scratch(cuts, n_dp):
        return [DMA((cuts, 3)), DMA((cuts, 3)), DMA((cuts, 2, max(n_dp // 2, 1)))]

    def kept(self, k):
        cols = self.cuts[k]
        return pltpu.make_async_copy(
            self.own.at[:, cols], self.full.at[self.dp, :, cols], self.near_sems.at[k, 2]
        )

    def beside(self, k):
        cols = self.cuts[k]
        return remote(
            self.own.at[:, cols],
            self.full.at[self.dp, :, cols],
            self.near_sems.at[k, 0],
            self.near_sems.at[k, 1],
            {DP: self.dp ^ 1},
        )

    def across(self, k, core):
        cols = self.cuts[k]
        return remote(
            self.own.at[:, cols],
            self.full.at[self.dp, :, cols],
            self.z_sems.at[k, 2],
            self.z_sems.at[k, core],
            {DP: 2 * self.q + self.home, TP: self.tp ^ 2},
        )

    def begin_plane(self, k):
        @pl.when(self.fast)
        def _():
            self.kept(k).start()

        @pl.when(jnp.logical_not(self.fast))
        def _():
            self.beside(k).start()

    def begin_z(self, k):
        self.across(k, self.core).start()

    def pair(self, k, mask):
        place = self.full.at[pl.ds(2 * self.q, 2), :, self.cuts[k]]
        return remote(
            place, place, self.xy_sems.at[k, 0, mask], self.xy_sems.at[k, 1, mask], {DP: self.dp ^ (2 * mask)}
        )

    def send(self, k):
        for mask in range(1, self.pairs):
            self.pair(k, mask).start()

    def from_plane(self, k):
        self.kept(k).wait()
        self.beside(k).wait_recv()
        self.send(k)

    def from_z(self, k):
        for core in range(2):
            self.across(k, core).wait_recv()
        self.send(k)

    def arrive(self, k):
        for mask in range(1, self.pairs):
            self.pair(k, mask).wait_recv()

    def finish(self):
        for k in range(len(self.cuts)):
            self.across(k, self.core).wait_send()

            @pl.when(jnp.logical_not(self.fast))
            def _():
                self.beside(k).wait_send()

            for mask in range(1, self.pairs):
                self.pair(k, mask).wait_send()


class GradScatter:
    def __init__(self, part, inbox, zbox, sbox, xy_sems, end_sems, cuts, n_dp):
        self.part, self.inbox, self.zbox, self.sbox = part, inbox, zbox, sbox
        self.xy_sems, self.end_sems, self.cuts = xy_sems, end_sems, cuts
        self.dp, self.tp = lax.axis_index(DP), lax.axis_index(TP)
        self.q, self.core = self.dp // 2, self.dp % 2
        self.home = self.tp // 2
        self.fast = self.core == self.home
        high = [b // 2 for b in bits_of(n_dp)[1:]]
        self.orders = [high, high[::-1]]
        self.stages = len(high)

    @staticmethod
    def scratch(cuts, n_dp, rows, cols):
        pairs = max(n_dp // 2, 2)
        return [
            VM((pairs - 1, 2, rows, cols), BF16),
            VM((rows, cols), BF16),
            VM((rows, cols), BF16),
            DMA((cuts, 2, 2, pairs)),
            DMA((cuts, 5)),
        ]

    def pair(self, k, half, stage, mask):
        bit = self.orders[half][stage]
        cols = halves_of(self.cuts[k])[half]
        return remote(
            self.part.at[pl.ds(2 * (self.q ^ mask), 2), :, cols],
            self.inbox.at[mask - 1, :, :, cols],
            self.xy_sems.at[k, half, 0, mask],
            self.xy_sems.at[k, half, 1, mask],
            {DP: self.dp ^ (2 * bit)},
        )

    def moved(self, half, stage):
        order = self.orders[half]
        return [m ^ order[stage] for m in span(order[stage + 1 :])]

    def to_owner(self, k, which):
        cols = self.cuts[k]
        return remote(
            self.part.at[2 * self.q + which, :, cols],
            self.zbox.at[:, cols],
            self.end_sems.at[k, which],
            self.end_sems.at[k, 2],
            {DP: 2 * self.q + which, TP: self.tp ^ 2},
        )

    def to_sibling(self, k):
        cols = self.cuts[k]
        return remote(
            self.part.at[self.dp ^ 1, :, cols],
            self.sbox.at[:, cols],
            self.end_sems.at[k, 3],
            self.end_sems.at[k, 4],
            {DP: self.dp ^ 1},
        )

    def send(self, k, stage):
        if stage < self.stages:
            for half in range(2):
                for mask in self.moved(half, stage):
                    self.pair(k, half, stage, mask).start()
            return

        @pl.when(self.fast)
        def _():
            self.to_sibling(k).start()

        @pl.when(jnp.logical_not(self.fast))
        def _():
            self.to_owner(k, 0).start()
            self.to_owner(k, 1).start()

    def advance(self, k, stage):
        for half in range(2):
            bit = self.orders[half][stage]
            cols = halves_of(self.cuts[k])[half]
            for mask in self.moved(half, stage):
                self.pair(k, half, stage, mask).wait_recv()
                rows = pl.ds(2 * (self.q ^ mask ^ bit), 2)
                self.part[rows, :, cols] = (
                    self.part[rows, :, cols].astype(F32) + self.inbox[mask - 1, :, :, cols].astype(F32)
                ).astype(BF16)
        self.send(k, stage + 1)

    def result(self, k, use):
        cols = self.cuts[k]
        self.to_owner(k, 0).wait_recv()

        @pl.when(self.fast)
        def _():
            use(self.part[self.dp, :, cols].astype(F32) + self.zbox[:, cols].astype(F32))

        @pl.when(jnp.logical_not(self.fast))
        def _():
            self.to_sibling(k).wait_recv()
            use(self.sbox[:, cols].astype(F32) + self.zbox[:, cols].astype(F32))

    def finish(self):
        for k in range(len(self.cuts)):
            for half in range(2):
                for stage in range(self.stages):
                    for mask in self.moved(half, stage):
                        self.pair(k, half, stage, mask).wait_send()

            @pl.when(self.fast)
            def _():
                self.to_sibling(k).wait_send()

            @pl.when(jnp.logical_not(self.fast))
            def _():
                self.to_owner(k, 0).wait_send()
                self.to_owner(k, 1).wait_send()


class AllSum:
    def __init__(self, value, inbox, sems, hops):
        self.value, self.inbox, self.sems, self.hops = value, inbox, sems, hops

    @staticmethod
    def scratch(hops, shape):
        return [VM((hops + 1,) + shape, F32), VM((hops,) + shape, F32), DMA((2, hops))]

    def copy(self, k):
        axis, bit = self.hops[k]
        peer = {axis: lax.axis_index(axis) ^ bit}
        return remote(self.value.at[k], self.inbox.at[k], self.sems.at[0, k], self.sems.at[1, k], peer)

    def start(self, k):
        if k < len(self.hops):
            self.copy(k).start()

    def step(self, k):
        if k < len(self.hops):
            self.copy(k).wait_recv()
            self.value[k + 1] = self.value[k] + self.inbox[k]
            self.start(k + 1)

    def finish(self):
        for k in range(len(self.hops)):
            self.copy(k).wait_send()


def spread_ids(m, s, length):
    for first in range(0, length, 128):
        lanes = jnp.broadcast_to(m.ids[s : s + 1, first : first + 128], (128, 128))
        m.key_ids[first : first + 128, :] = lanes.T


def seen_by(m, s, end, cols):
    keys = jnp.concatenate([m.key_ids[0:end, :]] * (CHUNK // 128), axis=1)
    return keys <= m.ids[2 + s : 3 + s, cols]


def chunk_rows(r):
    return pl.ds(pl.multiple_of(r * CHUNK, CHUNK), CHUNK)


def flat(w, cols):
    part = w[:, :, cols]
    return part.reshape(part.shape[0] * part.shape[1], part.shape[2])


def tables(m, rows, sign=1):
    return m.tabs[0, rows, :], m.tabs[1, rows, :] * sign


def regroup(out, row, heads):
    wide = heads * HEAD
    for h in range(heads):
        for j in range(3):
            out[:, (3 * h + j) * HEAD : (3 * h + j + 1) * HEAD] = row[
                :, j * wide + h * HEAD : j * wide + (h + 1) * HEAD
            ]


def degroup(out, row, heads):
    wide = heads * HEAD
    for h in range(heads):
        for j in range(3):
            out[:, j * wide + h * HEAD : j * wide + (h + 1) * HEAD] = row[
                :, (3 * h + j) * HEAD : (3 * h + j + 1) * HEAD
            ]


def project(m, s, qkv, wide):
    scaling = HEAD ** (-0.5)

    @pl.loop(0, m.x.shape[1] // CHUNK)
    def _(r):
        rows = chunk_rows(r)
        xhat, _ = norm_parts(m.x[s, rows, :].astype(F32))
        one = (xhat * m.vec[0:1, :] + m.vec[1:2, :]).astype(BF16)
        m.two[s, rows, :] = (xhat * m.vec[2:3, :] + m.vec[3:4, :]).astype(BF16)
        proj = mm(one, flat(m.w, slice(0, qkv)), 1, 0) + m.bias_now[0:1, 0:qkv]
        tabs = tables(m, rows)
        q = turn_back_and_forth(proj[:, 0:wide], *tabs).astype(BF16) * BF16(scaling)
        k = turn_back_and_forth(proj[:, wide : 2 * wide], *tabs).astype(BF16)
        v = proj[:, 2 * wide : qkv].astype(BF16)
        m.pk[s, rows, 0:wide] = q
        m.pk[s, rows, wide : 2 * wide] = k
        m.pk[s, rows, 2 * wide : qkv] = v
        m.qt[s, :, rows] = q.T
        m.kt[s, :, rows] = k.T
        m.vt[:, rows] = v.T


def attend(m, s, length, wide, midway):
    spread_ids(m, s, length)

    @pl.loop(0, wide // (2 * HEAD))
    def _(p):
        lanes = pl.ds(pl.multiple_of(p * 2 * HEAD, 2 * HEAD), 2 * HEAD)
        key_lanes = pl.ds(pl.multiple_of(wide + p * 2 * HEAD, 2 * HEAD), 2 * HEAD)
        for first, end in tiles_of(length):
            cols = slice(first, first + CHUNK)
            outs = []
            for h in range(2):
                head = pl.ds(pl.multiple_of(p * 2 * HEAD + h * HEAD, HEAD), HEAD)
                sc = mm(m.pk[s, 0:end, key_lanes], halves(m.qt[s, head, cols], h), 1, 0)
                sc = jnp.where(seen_by(m, s, end, cols), sc, -1e30)
                peak = jnp.max(sc, axis=0, keepdims=True)
                pw = jnp.exp(sc - peak)
                total = jnp.sum(pw, axis=0, keepdims=True)
                o = mm(m.vt[head, 0:end], pw.astype(BF16), 1, 0) / total
                outs.append(o)
                m.lse[s, pl.ds(p * 2 + h, 1), cols] = peak + jnp.log(total)
            m.att[s, cols, lanes] = jnp.concatenate(outs, axis=0).T.astype(BF16)

        @pl.when(p == 0)
        def _():
            midway()


def feed_up(m, s, wide, hidden):
    qkv = 3 * wide
    half = hidden // 2

    @pl.loop(0, m.x.shape[1] // CHUNK)
    def _(r):
        rows = chunk_rows(r)
        for c in range(2):
            cols = slice(c * half, (c + 1) * half)
            up = slice(qkv + c * half, qkv + (c + 1) * half)
            h = mm(m.two[s, rows, :], flat(m.w, up), 1, 0) + m.bias_now[0:1, up]
            cdf = 0.5 * (1.0 + lax.erf(h * (0.5**0.5)))
            pdf = jnp.exp(-0.5 * h * h) * 0.3989422804014327
            m.act[s, rows, cols] = (h * cdf).astype(BF16)
            m.dg[s, rows, cols] = (cdf + h * pdf).astype(BF16)
        m.flush("act", "dg", cut=(s, rows))


def feed_down(m, s, wide, hidden, use):
    at = 3 * wide + hidden

    @pl.loop(0, m.x.shape[1] // CHUNK)
    def _(r):
        rows = chunk_rows(r)
        acc = mm(m.att[s, rows, :], flat(m.w, slice(at, at + wide)), 1, 1)
        acc = acc + mm(m.act[s, rows, :], flat(m.w, slice(at + wide, at + wide + hidden)), 1, 1)
        use(r, rows, acc)


def run_forward(inputs, cotangent, shards, bias, vec, tabs, lengths, query_row, n_dp):
    _, own_rows, width = inputs.shape
    length = query_row.shape[1]
    shard_rows, qkv = shards["w_qkv"].shape
    wide = shards["w_out"].shape[1]
    hidden = shards["w_up"].shape[1]
    heads = wide // HEAD
    cols = qkv + wide + 2 * hidden
    cuts = [slice(0, qkv), slice(qkv, qkv + hidden), slice(qkv + hidden, cols)]
    ins = dict(
        inputs=(inputs, ANY), cotangent=(cotangent, ANY), tabs=(tabs, LOAD), b_qkv=(bias[0], VM), b_up=(bias[1], VM),
        g1=(vec[0], VM), b1=(vec[1], VM), g2=(vec[2], VM), b2=(vec[3], VM),
        lengths=(lengths, pltpu.SMEM), query_row=(query_row, VM),
        w_qkv=(shards["w_qkv"], VM), w_out=(shards["w_out"], ANY), w_up=(shards["w_up"], ANY),
        w_down=(shards["w_down"], ANY),
    )
    outs = dict(
        x=(sds((2, length, width), BF16), STORE),
        c=(sds((2, length, width), BF16), ANY),
        w=(sds((n_dp, shard_rows, cols), BF16), STORE),
        two=(sds((2, length, width), BF16), STORE),
        pk=(sds((2, length, qkv), BF16), STORE),
        qt=(sds((2, wide, length), BF16), STORE),
        kt=(sds((2, wide, length), BF16), STORE),
        att=(sds((2, length, wide), BF16), STORE),
        lse=(sds((2, heads, length), F32), STORE),
        act=(sds((2, length, hidden), BF16), STORE),
        dg=(sds((2, length, hidden), BF16), STORE),
        s_out=(sds((length, width), BF16), STORE),
        ids=(sds((4, length), jnp.int32), VM),
        vec=(sds((4, width), F32), VM),
    )
    small = (1, qkv + hidden)
    scratch = dict(
        vt=VM((wide, length), BF16),
        key_ids=VM((length, 128), jnp.int32),
        mine=VM((shard_rows, cols), BF16),
        term=VM((length, width), BF16),
        term_in=VM((length, width), BF16),
        bias=VM(small, F32),
        bias_in=VM(small, F32),
        bias_now=VM(small, F32),
        key_row=VM(query_row.shape, jnp.int32),
        key_in=VM(query_row.shape, jnp.int32),
        query_in=VM(query_row.shape, jnp.int32),
        piece_sems=DMA((3,)),
        small_sems=DMA((2, 3)),
        term_sems=DMA((2, length // CHUNK)),
    )
    for tag, group in (
        ("xg", LineGather.scratch(2)), ("cg", LineGather.scratch(2)), ("wg", WeightGather.scratch(3, n_dp)),
    ):
        for n, item in enumerate(group):
            scratch[tag + str(n)] = item

    def body(m):
        tp, dp = lax.axis_index(TP), lax.axis_index(DP)
        fast = dp % 2 == tp // 2
        slow = jnp.logical_not(fast)
        sibling = {DP: dp ^ 1}
        xg = LineGather(m.inputs, m.x, m.xg0, m.xg1, m.xg2, 2)
        cg = LineGather(m.cotangent, m.c, m.cg0, m.cg1, m.cg2, 2)
        wg = WeightGather(m.mine, m.w, m.wg0, m.wg1, m.wg2, cuts, n_dp)
        at, copies = qkv, []
        for n, src in enumerate((m.w_up, m.w_out, m.w_down)):
            copies.append(
                pltpu.make_async_copy(src, m.mine.at[:, at : at + src.shape[1]], m.piece_sems.at[n])
            )
            copies[-1].start()
            at += src.shape[1]
        degroup(m.mine, m.w_qkv, heads)
        greet(n_dp)
        xg.begin((2,))
        xg.begin((1,), (1, 2))
        wg.begin_z(0)
        xg.begin((1,), (0, 3))
        wg.begin_plane(0)
        for copy in copies:
            copy.wait()
        wg.begin_plane(1)
        wg.begin_plane(2)
        edge = (tp == 0) | (tp == LINE - 1)

        @pl.when(edge)
        def _():
            wg.begin_z(1)
            wg.begin_z(2)


        degroup(m.bias, m.b_qkv, heads)
        m.bias[:, qkv:] = m.b_up[...]
        place = lax.broadcasted_iota(jnp.int32, (1, length), 1)
        for s in range(2):
            m.key_row[s : s + 1, :] = jnp.where(place < m.lengths[s], m.query_row[s : s + 1, :], 1 << 30)
        swaps = [
            remote(a, b, m.small_sems.at[0, n], m.small_sems.at[1, n], peer)
            for n, (a, b, peer) in enumerate(
                (
                    (m.key_row, m.key_in, sibling),
                    (m.query_row, m.query_in, sibling),
                    (m.bias, m.bias_in, {TP: tp ^ 2}),
                )
            )
        ]
        for swap in swaps:
            swap.start()
        m.load("tabs")
        for n, ref in enumerate((m.g1, m.b1, m.g2, m.b2)):
            m.vec[n : n + 1, :] = ref[...]

        @pl.when(fast)
        def _():
            for k in range(3):
                wg.from_plane(k)

        def from_z(k):
            @pl.when(slow)
            def _():
                wg.from_z(k)

        xg.advance(1, 0)
        xg.advance(1, 1)
        xg.advance(2, 0)
        from_z(0)
        xg.advance(2, 1)

        @pl.when(jnp.logical_not(edge))
        def _():
            wg.begin_z(1)
            wg.begin_z(2)

        for swap in swaps:
            swap.wait()
        group = pl.ds(tp // 2, 1)
        m.ids[0:1, :] = m.key_row[group, :]
        m.ids[1:2, :] = m.key_in[group, :]
        m.ids[2:3, :] = m.query_row[group, :]
        m.ids[3:4, :] = m.query_in[group, :]
        m.bias_now[...] = jnp.where(fast, m.bias[...], m.bias_in[...])
        xg.advance(3, 0)
        xg.advance(3, 1)
        xg.settle()
        cg.begin((2, 1))
        m.flush("x")
        m.ready("tabs")
        wg.arrive(0)
        project(m, 0, qkv, wide)
        attend(m, 0, length, wide, lambda: from_z(1))
        from_z(2)
        project(m, 1, qkv, wide)
        m.flush("two", "pk", "qt", "kt")

        def midway():
            cg.advance(1, 0)
            cg.advance(1, 1)

        attend(m, 1, length, wide, midway)
        m.flush("att", "lse")
        cg.advance(2, 0)
        wg.arrive(1)

        def term(r, rows):
            return remote(
                m.term.at[rows, :], m.term_in.at[rows, :], m.term_sems.at[0, r], m.term_sems.at[1, r], sibling
            )

        def give(r, rows, acc):
            m.term[rows, :] = acc.astype(BF16)
            term(r, rows).start()

        def take(r, rows, acc):
            term(r, rows).wait_recv()
            m.s_out[rows, :] = (acc + m.term_in[rows, :].astype(F32)).astype(BF16)
            m.flush("s_out", cut=(rows,))

        feed_up(m, 1, wide, hidden)
        cg.advance(2, 1)
        feed_up(m, 0, wide, hidden)
        wg.arrive(2)
        m.flush("w")
        feed_down(m, 1, wide, hidden, give)
        feed_down(m, 0, wide, hidden, take)
        cg.advance(3, 0)
        cg.advance(3, 1)
        cg.settle()
        for r in range(length // CHUNK):
            term(r, slice(r * CHUNK, (r + 1) * CHUNK)).wait_send()
        xg.finish()
        cg.finish()
        wg.finish()
        m.drain()

    return call("forward_all", body, ins, outs, scratch, 1, 60)


def hidden_back(m, s, wide, hidden):
    qkv = 3 * wide
    half = hidden // 2

    @pl.loop(0, m.slope.shape[1] // CHUNK)
    def _(r):
        rows = chunk_rows(r)
        slope = m.slope[s, rows, :]
        at = qkv + hidden
        g = mm(slope, flat(m.w, slice(at, at + wide)), 1, 0).astype(BF16)
        m.gat[s, rows, :] = g
        for c in range(2):
            cols = slice(c * half, (c + 1) * half)
            down = slice(at + wide + c * half, at + wide + (c + 1) * half)
            t = (mm(slope, flat(m.w, down), 1, 0) * m.dg[s, rows, cols].astype(F32)).astype(BF16)
            m.dg[s, rows, cols] = t
            m.tok[0:1, qkv + c * half : qkv + (c + 1) * half] += jnp.sum(
                t.astype(F32), axis=0, keepdims=True
            )


def attend_back(m, s, length, wide, midway):
    scaling = HEAD ** (-0.5)
    spread_ids(m, s, length)
    m.gk[...] = jnp.zeros_like(m.gk)
    m.gv[...] = jnp.zeros_like(m.gv)
    for first in range(0, length, CHUNK):
        rows = slice(first, first + CHUNK)
        both = (m.gat[s, rows, :].astype(F32) * m.att[s, rows, :].astype(F32)).T
        for h in range(wide // HEAD):
            m.delta[h : h + 1, rows] = jnp.sum(both[h * HEAD : (h + 1) * HEAD, :], axis=0, keepdims=True)

    @pl.loop(0, wide // (2 * HEAD))
    def _(p):
        def lanes_at(start):
            return pl.ds(pl.multiple_of(start + p * 2 * HEAD, 2 * HEAD), 2 * HEAD)

        lanes, k_lanes, v_lanes = lanes_at(0), lanes_at(wide), lanes_at(2 * wide)
        for first, end in tiles_of(length):
            cols = slice(first, first + CHUNK)
            dqs, dss, pws = [], [], []
            turned = m.gat[s, cols, lanes].T
            for h in range(2):
                head = pl.ds(pl.multiple_of(p * 2 * HEAD + h * HEAD, HEAD), HEAD)
                row = pl.ds(p * 2 + h, 1)
                sc = mm(m.act[s, 0:end, k_lanes], halves(m.qt[s, head, cols], h), 1, 0)
                pw = jnp.where(seen_by(m, s, end, cols), jnp.exp(sc - m.lse[s, row, cols]), 0.0)
                dp = mm(m.act[s, 0:end, v_lanes], halves(turned[h * HEAD : (h + 1) * HEAD, :], h), 1, 0)
                ds = (pw * (dp - m.delta[row, cols])).astype(BF16)
                dss.append(ds)
                pws.append(pw.astype(BF16))
                dqs.append(mm(m.kt[s, head, 0:end], ds, 1, 0))
            qs = jnp.concatenate([lane_half(m.act[s, cols, lanes], h) for h in range(2)], axis=0)
            gs = jnp.concatenate([lane_half(m.gat[s, cols, lanes], h) for h in range(2)], axis=0)
            m.gk[0:end, lanes] += mm(jnp.concatenate(dss, axis=1), qs, 1, 0)
            m.gv[0:end, lanes] += mm(jnp.concatenate(pws, axis=1), gs, 1, 0)
            dq = jnp.concatenate(dqs, axis=0).T * scaling
            m.gp[cols, lanes] = turn_back_and_forth(dq, *tables(m, cols, -1)).astype(BF16)

        @pl.when(p == 0)
        def _():
            midway()


def input_back(m, s, wide, hidden, use):
    qkv = 3 * wide
    chunks = m.gp.shape[0] // CHUNK

    @pl.loop(0, chunks)
    def _(n):
        r = lax.rem(n + chunks - 1, chunks)
        rows = chunk_rows(r)
        m.gp[rows, wide : 2 * wide] = turn_back_and_forth(m.gk[rows, :], *tables(m, rows, -1)).astype(BF16)
        m.gp[rows, 2 * wide : qkv] = m.gv[rows, :].astype(BF16)
        g = m.gp[rows, :]
        m.tok[0:1, 0:qkv] += jnp.sum(g.astype(F32), axis=0, keepdims=True)
        xhat, _ = norm_parts(m.bx[s, rows, :].astype(F32))
        m.bx[s, rows, :] = (xhat * m.vec[0:1, :] + m.vec[1:2, :]).astype(BF16)
        d1 = mm(g, flat(m.w, slice(0, qkv)), 1, 1)
        d2 = mm(m.dg[s, rows, :], flat(m.w, slice(qkv, qkv + hidden)), 1, 1)
        m.sums[0:1, :] += jnp.sum(d1 * xhat, axis=0, keepdims=True)
        m.sums[1:2, :] += jnp.sum(d1, axis=0, keepdims=True)
        m.sums[2:3, :] += jnp.sum(d2 * xhat, axis=0, keepdims=True)
        m.sums[3:4, :] += jnp.sum(d2, axis=0, keepdims=True)
        use(n, r, rows, d1 * m.vec[0:1, :] + d2 * m.vec[2:3, :])


def weight_back(m, cols, pairs, again=False):
    n_dp, shard_rows, _ = m.grad.shape
    per = CHUNK // shard_rows

    @pl.loop(0, n_dp // per)
    def _(r):
        rows = chunk_rows(r)
        new = None
        for left, right in pairs:
            term = mm(left[:, rows], right[...], 0, 0)
            new = term if new is None else new + term
        new = new.reshape(per, shard_rows, new.shape[1])
        blocks = pl.ds(r * per, per)
        if again:
            new = new + m.grad[blocks, :, cols].astype(F32)
        m.grad[blocks, :, cols] = new.astype(BF16)


def run_backward(f, inputs, cotangent, tabs, b_out, b_down, n_dp):
    _, own_rows, width = inputs.shape
    _, length, _ = f["x"].shape
    _, shard_rows, cols = f["w"].shape
    wide = f["att"].shape[2]
    hidden = f["act"].shape[2]
    qkv = 3 * wide
    heads = wide // HEAD
    out_at, down_at = qkv + hidden, qkv + hidden + wide
    cuts = [slice(out_at, cols), slice(qkv, out_at), slice(0, qkv)]
    hops = [(DP, b) for b in bits_of(n_dp)] + [(TP, 1), (TP, 2)]
    tok_hops = [(DP, b) for b in bits_of(n_dp)[1:]] + [(TP, 2)]
    ins = dict(
        s_out=(f["s_out"], ANY), slope=(f["c"], LOAD), w=(f["w"], LOAD), dg=(f["dg"], LOAD),
        act=(f["act"], LOAD), att=(f["att"], LOAD), lse=(f["lse"], LOAD),
        qt=(f["qt"], LOAD), kt=(f["kt"], LOAD), tabs=(tabs, LOAD), ids=(f["ids"], VM),
        two=(f["two"], ANY), x=(f["x"], ANY), pk=(f["pk"], ANY),
        vec=(f["vec"], VM), b_out=(b_out, VM), b_down=(b_down, VM), inputs=(inputs, ANY), cotangent=(cotangent, ANY),
    )
    line = lambda n: sds((1, n), F32)
    outs = dict(
        done=(sds((2, own_rows, width), BF16), ANY),
        final=(sds((2, own_rows, width), F32), ANY),
        o_qkv=(sds((shard_rows, qkv), F32), VM),
        o_out=(sds((shard_rows, wide), F32), VM),
        o_up=(sds((shard_rows, hidden), F32), VM),
        o_down=(sds((shard_rows, hidden), F32), VM),
        o_bqkv=(line(qkv), VM),
        o_bup=(line(hidden), VM),
        o_g1=(line(width), VM),
        o_b1=(line(width), VM),
        o_g2=(line(width), VM),
        o_b2=(line(width), VM),
        o_s=(line(width), VM),
        o_t=(line(width), VM),
    )
    scratch = dict(
        key_ids=VM((length, 128), jnp.int32),
        bx=VM((2, length, width), BF16),
        gat=VM((2, length, wide), BF16),
        delta=VM((heads, length), F32),
        gk=VM((length, wide), F32),
        gv=VM((length, wide), F32),
        gp=VM((length, qkv), BF16),
        grad=VM((n_dp, shard_rows, cols), BF16),
        term_in=VM((length, width), BF16),
        sums=VM((8, width), F32),
        tok=VM((1, qkv + hidden), F32),
        tok_in=VM((1, qkv + hidden), F32),
        term_sems=DMA((2, length // CHUNK)),
        piece=VM((own_rows, width), BF16),
        more_sems=DMA((16,)),
        final_sems=DMA((2, width // wide)),
    )
    for tag, group in (
        ("zo", LineScatter.scratch(own_rows, width, 1)), ("ze", LineScatter.scratch(own_rows, width, 2)),
        ("gs", GradScatter.scratch(3, n_dp, shard_rows, cols)),
        ("sm", AllSum.scratch(len(hops), (8, width))), ("tk", AllSum.scratch(len(tok_hops), (1, qkv + hidden))),
    ):
        for n, item in enumerate(group):
            scratch[tag + str(n)] = item

    def body(m):
        tp, dp = lax.axis_index(TP), lax.axis_index(DP)
        fast = dp % 2 == tp // 2
        sibling = {DP: dp ^ 1}
        tail = (slice(None), slice(None), slice(out_at, cols))
        front = (slice(None), slice(None), slice(0, out_at))
        m.load("slope", "dg", cut=(1,))
        m.load("w", cut=tail)
        m.load("slope", "dg", cut=(0,), n=1)
        greet(n_dp)

        def fetched(rows):
            copy = pltpu.make_async_copy(m.s_out.at[rows, :], m.piece, m.more_sems.at[7])
            copy.start()
            copy.wait()
            return m.piece[...]

        zo = LineScatter(m.s_out, fetched, m.zo0, m.zo1, 1)
        ze = LineScatter(m.slope.at[0], lambda rows: m.slope[0, rows, :], m.ze0, m.ze1, 2)
        gs = GradScatter(m.grad, m.gs0, m.gs1, m.gs2, m.gs3, m.gs4, cuts, n_dp)
        small = AllSum(m.sm0, m.sm1, m.sm2, hops)
        toks = AllSum(m.tk0, m.tk1, m.tk2, tok_hops)
        zo.begin((1, 2, 3))

        def more(far, near, n):
            return pltpu.make_async_copy(far, near, m.more_sems.at[n])

        m.tok[...] = jnp.zeros_like(m.tok)
        m.sums[...] = jnp.zeros_like(m.sums)
        m.ready("slope", "dg", cut=(1,))
        m.ready("w", cut=tail)
        m.load("act", "att", "qt", "kt", "lse", "tabs")
        m.load("w", cut=front, n=1)
        xs = more(m.x, m.bx, 0)
        xs.start()
        hidden_back(m, 1, wide, hidden)
        m.ready("slope", "dg", cut=(0,), n=1)
        hidden_back(m, 0, wide, hidden)
        m.ready("w", cut=front, n=1)
        m.ready("act", "att", "qt", "kt", "lse", "tabs")
        zo.advance(1, 0)
        weight_back(m, slice(down_at, cols), [(m.slope.at[s], m.act.at[s]) for s in range(2)])
        pks = [more(m.pk.at[s], m.act.at[s, :, 0:qkv], 1 + s) for s in range(2)]
        for s in (1, 0):
            pks[s].start()
        weight_back(m, slice(out_at, down_at), [(m.slope.at[s], m.att.at[s]) for s in range(2)])
        gs.send(0, 0)
        pks[1].wait()

        attend_back(m, 1, length, wide, lambda: zo.advance(2, 0))
        spare = m.act.at[1]
        own_x = [pl.ds(s * own_rows, own_rows) for s in range(2)]
        own_c = [pl.ds((2 + s) * own_rows, own_rows) for s in range(2)]
        x_in = [more(m.inputs.at[s], spare.at[own_x[s], :], 8 + s) for s in range(2)]
        c_in = [more(m.cotangent.at[s], spare.at[own_c[s], :], 10 + s) for s in range(2)]
        out = [more(spare.at[own_c[s], :], m.done.at[s], 12 + s) for s in range(2)]
        for copy in x_in:
            copy.start()
        xs.wait()

        def term(r, rows):
            return remote(
                m.slope.at[1, rows, :], m.term_in.at[rows, :], m.term_sems.at[0, r], m.term_sems.at[1, r], sibling
            )

        def give(n, r, rows, e):
            m.slope[1, rows, :] = e.astype(BF16)
            term(r, rows).start()

        input_back(m, 1, wide, hidden, give)
        gs.advance(0, 0)
        weight_back(m, cuts[2], [(m.bx.at[1], m.gp)])
        twos = [more(m.two.at[0], m.act.at[0], 3), more(m.two.at[1], m.bx.at[1], 4)]
        twos[1].start()
        zo.advance(3, 0)
        for copy in x_in:
            copy.wait()
        bias = m.b_out[...] + m.b_down[...]

        def put_out(seq, rows, total):
            here = pl.ds(seq * own_rows + rows.start, rows.stop - rows.start)
            there = pl.ds((2 + seq) * own_rows + rows.start, rows.stop - rows.start)
            m.act[1, there, :] = (m.act[1, here, :].astype(F32) + total + bias).astype(BF16)

        zo.totals(put_out)
        for copy in out:
            copy.start()
        pks[0].wait()
        attend_back(m, 0, length, wide, lambda: gs.advance(0, 1))
        twos[0].start()
        for copy in out:
            copy.wait()
        for copy in c_in:
            copy.start()

        def take(n, r, rows, e):
            term(r, rows).wait_recv()
            m.slope[0, rows, :] = (e + m.term_in[rows, :].astype(F32)).astype(BF16)

            @pl.when(n == 1)
            def _():
                ze.begin((1,))

        input_back(m, 0, wide, hidden, take)
        ze.begin((2, 3))
        for s in range(2):
            c_in[s].wait()
            m.sums[4:5, :] += jnp.sum(m.act[1, own_c[s], :].astype(F32), axis=0, keepdims=True)
        m.sm0[0] = m.sums[...]
        m.tk0[0] = m.tok[...]
        small.start(0)
        toks.start(0)
        for copy in twos:
            copy.wait()
        weight_back(m, cuts[1], [(m.act.at[0], m.dg.at[0]), (m.bx.at[1], m.dg.at[1])])
        gs.send(1, 0)
        weight_back(m, cuts[2], [(m.bx.at[0], m.gp)], again=True)
        gs.send(2, 0)
        def save(k):
            def use(value):
                if k == 0:
                    m.o_out[...] = value[:, 0:wide]
                    m.o_down[...] = value[:, wide:]
                elif k == 1:
                    m.o_up[...] = value
                else:
                    regroup(m.o_qkv, value, heads)

            return use

        def sums(k):
            small.step(k)
            toks.step(k)

        ze.advance(1, 0)
        sums(0)
        ze.advance(1, 1)
        sums(1)
        for stage in range(2, gs.stages):
            gs.advance(0, stage)
        ze.advance(2, 0)
        gs.advance(1, 0)
        sums(2)
        ze.advance(2, 1)
        gs.advance(2, 0)
        for stage in range(1, gs.stages):
            gs.advance(1, stage)
        gs.result(0, save(0))
        sums(3)
        for stage in range(1, gs.stages):
            gs.advance(2, stage)
        ze.advance(3, 0)
        for k in range(4, len(hops)):
            sums(k)
        last_tok = remote(
            m.tk0.at[len(tok_hops)], m.tok_in, m.more_sems.at[5], m.more_sems.at[6], sibling
        )
        last_tok.start()
        ze.advance(3, 1)

        parts = width // wide
        boxes = (m.gk, m.gv)

        def put_total(seq, rows, total):
            for k in range(parts):
                here = pl.ds(k * own_rows + rows.start, rows.stop - rows.start)
                boxes[seq][here, :] = total[:, k * wide : (k + 1) * wide]

        def box(seq, k):
            return boxes[seq].at[k * own_rows : (k + 1) * own_rows, :]

        def finals(seq):
            return [
                pltpu.make_async_copy(
                    box(seq, k), m.final.at[seq, :, k * wide : (k + 1) * wide], m.final_sems.at[seq, k]
                )
                for k in range(parts)
            ]

        ze.totals(put_total)
        for seq in range(2):
            e = jnp.concatenate([box(seq, k)[...] for k in range(parts)], axis=1)
            xh, inv = norm_parts(m.act[1, own_x[seq], :].astype(F32))
            back = e - jnp.mean(e, axis=-1, keepdims=True) - xh * jnp.mean(e * xh, axis=-1, keepdims=True)
            back = m.act[1, own_c[seq], :].astype(F32) + back * inv
            for k in range(parts):
                box(seq, k)[...] = back[:, k * wide : (k + 1) * wide]
            for copy in finals(seq):
                copy.start()
        last_tok.wait_recv()
        tok = jnp.where(fast, m.tk0[len(tok_hops)], m.tok_in[...])
        regroup(m.o_bqkv, tok[:, 0:qkv], heads)
        m.o_bup[...] = tok[:, qkv:]
        for n, ref in enumerate((m.o_g1, m.o_b1, m.o_g2, m.o_b2, m.o_s)):
            ref[...] = m.sm0[len(hops), n : n + 1, :]
        m.o_t[...] = m.sm0[len(hops), 4:5, :]
        gs.result(1, save(1))
        gs.result(2, save(2))
        for r in range(length // CHUNK):
            term(r, slice(r * CHUNK, (r + 1) * CHUNK)).wait_send()
        last_tok.wait_send()
        for seq in range(2):
            for copy in finals(seq):
                copy.wait()
        zo.finish()
        ze.finish()
        gs.finish()
        small.finish()
        toks.finish()

    return call("backward_all", body, ins, outs, scratch, 2, 63)


def settle_outputs(arrays):
    keys = list(arrays)

    def body(m):
        m.load(*keys)
        for n, key in enumerate(keys):
            m.ready(key)
            pltpu.make_async_copy(m.refs[key + "@"], m.refs[key + key], m.sems.at[n]).start()
        for n, key in enumerate(keys):
            pltpu.make_async_copy(m.refs[key + "@"], m.refs[key + key], m.sems.at[n]).wait()

    ins = {key: (a, LOAD) for key, a in arrays.items()}
    outs = {key + key: (sds(a.shape, a.dtype), ANY) for key, a in arrays.items()}
    res = call("settle", body, ins, outs, dict(sems=DMA((len(keys),))), None, 62)
    return {key: res[key + key] for key in keys}


def make(n_dp, n_tp):
    assert n_tp == LINE

    def on_device(
        inputs, cotangent, lengths, block_ids, ln1_gain, ln1_bias, ln2_gain, ln2_bias,
        w_qkv, b_qkv, w_out, b_out, w_up, b_up, w_down, b_down,
    ):
        shards = dict(w_qkv=w_qkv, w_out=w_out, w_up=w_up, w_down=w_down)
        line = lambda v: v.reshape(1, -1)
        tabs = jnp.asarray(rope_lanes(block_ids.shape[1]))
        vec = [line(v) for v in (ln1_gain, ln1_bias, ln2_gain, ln2_bias)]
        f = run_forward(
            inputs, cotangent, shards, (line(b_qkv), line(b_up)), vec, tabs, lengths, block_ids, n_dp
        )
        b = settle_outputs(run_backward(f, inputs, cotangent, tabs, line(b_out), line(b_down), n_dp))
        flat_of = lambda v: v.reshape(-1)
        return (
            b["done"], b["final"], b["o_qkv"], b["o_out"], b["o_up"], b["o_down"],
            flat_of(b["o_bqkv"]), flat_of(b["o_bup"]), flat_of(b["o_g1"]), flat_of(b["o_b1"]),
            flat_of(b["o_g2"]), flat_of(b["o_b2"]), flat_of(b["o_s"]), flat_of(b["o_t"]),
        )

    return on_device


def solution(mesh):
    in_specs = (
        P(DP, TP, None),
        P(DP, TP, None),
        P(DP),
        P(DP, None),
        P(),
        P(),
        P(),
        P(),
        P(DP, TP),
        P(TP),
        P(DP, TP),
        P(),
        P(DP, TP),
        P(TP),
        P(DP, TP),
        P(),
    )
    out_specs = (
        P(DP, TP, None),
        P(DP, TP, None),
        P(DP, TP),
        P(DP, TP),
        P(DP, TP),
        P(DP, TP),
        P(TP),
        P(TP),
        P(),
        P(),
        P(),
        P(),
        P(),
        P(),
    )
    return jax.shard_map(
        make(mesh.shape[DP], mesh.shape[TP]),
        mesh=mesh,
        in_specs=in_specs,
        out_specs=out_specs,
        check_vma=False,
    )
```
